32 devices in a mesh: expert: 2 (over y), fsdp: 16 (over z, x, core).
Axes of the slice: x: 2, y: 2, z: 4, core: 2. Of those that a mesh axis runs over, the one named last changes fastest.
Arguments:
- states: bfloat16 [4608, 2048], P(('expert', 'fsdp')), may hold values from -6 to 6
- w_query: bfloat16 [2048, 2048], P(('expert', 'fsdp')), may hold values from -0.1875 to 0.1875
- w_key: bfloat16 [2048, 2048], P(('expert', 'fsdp')), may hold values from -0.1875 to 0.1875
- w_value: bfloat16 [2048, 2048], P(('expert', 'fsdp')), may hold values from -0.125 to 0.125
- w_out: bfloat16 [2048, 2048], P(('expert', 'fsdp')), may hold values from -1 to 1
- b_query: bfloat16 [2048], P(('expert', 'fsdp')), may hold values from -0.59765625 to 0.59765625
- b_key: bfloat16 [2048], P(('expert', 'fsdp')), may hold values from -0.59765625 to 0.59765625
- b_value: bfloat16 [2048], P(('expert', 'fsdp')), may hold values from -0.3984375 to 0.3984375
- attn_gain: bfloat16 [2048], P(('expert', 'fsdp')), may hold values from 0.5 to 1.5
- ffn_gain: bfloat16 [2048], P(('expert', 'fsdp')), may hold values from 0.5 to 1.5
- router: bfloat16 [2048, 16], P(('expert', 'fsdp')), may hold values from -0.0625 to 0.0625
- shared_gate: bfloat16 [2048, 5632], P('fsdp', 'expert'), may hold values from -0.125 to 0.125
- shared_up: bfloat16 [2048, 5632], P('fsdp', 'expert'), may hold values from -0.125 to 0.125
- shared_down: bfloat16 [5632, 2048], P('expert', 'fsdp'), may hold values from -0.078125 to 0.078125
- shared_scale: bfloat16 [2048], P(('expert', 'fsdp')), may hold values from -0.125 to 0.125
- expert_gate: bfloat16 [16, 2048, 1408], P('fsdp', None, 'expert'), may hold values from -0.125 to 0.125
- expert_up: bfloat16 [16, 2048, 1408], P('fsdp', None, 'expert'), may hold values from -0.125 to 0.125
- expert_down: bfloat16 [16, 1408, 2048], P('fsdp', 'expert'), may hold values from -0.15625 to 0.15625
- routes: int32 [4608, 4], P(('expert', 'fsdp')), may hold values from 0 to 15, all different within a row; in each aligned block of 144 rows (0 to 143, 144 to 287, ...) at most 48 rows name the same one
- prefix: int32 [32], P(('expert', 'fsdp')), may hold values from 14 to 72
- cotangent: bfloat16 [4608, 2048], P(('expert', 'fsdp')), may hold values from -6 to 6
Outputs:
- output: bfloat16 [4608, 2048], P(('expert', 'fsdp'))
- grad_states: float32 [4608, 2048], P(('expert', 'fsdp'))
- grad_w_query: float32 [2048, 2048], P(('expert', 'fsdp'))
- grad_w_key: float32 [2048, 2048], P(('expert', 'fsdp'))
- grad_w_value: float32 [2048, 2048], P(('expert', 'fsdp'))
- grad_w_out: float32 [2048, 2048], P(('expert', 'fsdp'))
- grad_b_query: float32 [2048], P(('expert', 'fsdp'))
- grad_b_key: float32 [2048], P(('expert', 'fsdp'))
- grad_b_value: float32 [2048], P(('expert', 'fsdp'))
- grad_attn_gain: float32 [2048], P(('expert', 'fsdp'))
- grad_ffn_gain: float32 [2048], P(('expert', 'fsdp'))
- grad_router: float32 [2048, 16], P(('expert', 'fsdp'))
- grad_shared_gate: float32 [2048, 5632], P('fsdp', 'expert')
- grad_shared_up: float32 [2048, 5632], P('fsdp', 'expert')
- grad_shared_down: float32 [5632, 2048], P('expert', 'fsdp')
- grad_shared_scale: float32 [2048], P(('expert', 'fsdp'))
- grad_expert_gate: float32 [16, 2048, 1408], P('fsdp', None, 'expert')
- grad_expert_up: float32 [16, 2048, 1408], P('fsdp', None, 'expert')
- grad_expert_down: float32 [16, 1408, 2048], P('fsdp', 'expert')
The draws below stay inside these ranges and needn't reach their ends.
Inputs may be any that keep to these rules, and one draw needn't show every extreme that they name: `routes`: each token names 4 different experts; among the tokens of one device no expert is named more than 48 times, and that count is reached. One prefix length per sequence of 144 tokens.
All inputs are finite; a program needn't handle non-finite values.
Results may differ from the reference program's by a relative error of at most 0.02.
Values may be sent and summed in bfloat16 or wider, within the bound.
A program may use at most 384 MiB of HBM per device.

```python
import math
import jax
import jax.numpy as jnp
import numpy as np
from jax import lax

D = 2048
H = 16
FE = 1408
SH = 5632
TOP = 4
TOK_DEV = 144
EXPERTS = 16
CAP = 48
TOKENS = 4608
N_EXPERT = 2
N_FSDP = 16
DEVICES = 32


def with_ends(drawn, rng, smallest, top_value):
    shape = drawn.shape
    index_at = [jax.random.randint(jax.random.fold_in(rng, axis), (), 0, shape[axis]) for axis in range(len(shape))]
    drawn = drawn.at[tuple(index_at)].set(smallest)
    longest = shape.index(max(shape))
    index_at[longest] = (index_at[longest] + 1) % shape[longest]
    return drawn.at[tuple(index_at)].set(top_value)


def steps_of(rng, dims, pieces, smallest, high):
    level = 1.0
    for dim, blocks in pieces:
        heights = jax.random.uniform(jax.random.fold_in(jax.random.fold_in(rng, 6), dim), (blocks,), jnp.float32, smallest / len(pieces), high / len(pieces))
        level = level * jnp.repeat(jnp.exp(heights), dims[dim] // blocks).reshape((-1,) + (1,) * (len(dims) - 1 - dim))
    return level


def assign_block(own_key, own, number, rows, count, top, bound, skew):
    order = jax.random.permutation(own_key, count)
    crowded, ordinary = shares(count, rows * top, bound, skew, True), shares(count, rows * top, bound, skew, False)
    places = jnp.arange(count)

    def named(sizes, offset_by):
        used = int((sizes > 0).sum())
        fixed = max(1, used // 4)
        passed = fixed + (places - fixed + offset_by * (used - fixed)) % max(1, count - fixed)
        return jnp.zeros((count,), jnp.int32).at[order[jnp.where(places < fixed, places, passed)]].set(jnp.asarray(sizes, jnp.int32))

    sizes = jnp.where(number % 4 == 0, named(crowded, number // 4), named(ordinary, number - number // 4 - 1))
    mixed = jax.random.permutation(jax.random.fold_in(own, 3), count)
    donor, taker = mixed[0:count // 2 * 2:2], mixed[1:count // 2 * 2:2]
    room = jnp.minimum(sizes[donor] - 1, bound - sizes[taker]) // 2
    room = jnp.where((donor == order[0]) | (taker == order[0]) | (sizes[taker] == 0), 0, jnp.maximum(room, 0))
    passed = jax.random.randint(jax.random.fold_in(own, 4), (count // 2,), 0, 1 << 20) % (room + 1)
    sizes = sizes.at[donor].add(-passed).at[taker].add(passed)
    labels = jnp.searchsorted(jnp.cumsum(sizes), jnp.arange(rows * top), side="right").astype(jnp.int32)
    grid = labels.reshape(top, rows).T
    grid = grid[jax.random.permutation(jax.random.fold_in(own, 1), rows)]
    offset_by = jax.random.randint(jax.random.fold_in(own, 2), (rows, 1), 0, top)
    return jnp.take_along_axis(grid, (jnp.arange(top)[None, :] + offset_by) % top, axis=1)


def shares(count, total, most, slope, full):
    loads = [(1 << 20) // math.isqrt(rank ** slope) + 1 for rank in range(1, count + 1)]
    largest = most if full else min(most, max(-(-total // count), total * loads[0] // sum(loads)))
    least = 1 if total - largest >= count - 1 else 0
    counts, rest = [largest] + [least] * (count - 1), total - largest - least * (count - 1)
    while rest > 0:
        movable = [i for i in range(1, count) if counts[i] < largest] or [i for i in range(1, count) if counts[i] < most]
        pool, left = sum([loads[i] for i in movable]), rest
        for i in movable:
            more = min(most - counts[i], max(1, left * loads[i] // pool), rest)
            counts[i] = counts[i] + more
            rest = rest - more
    return np.array(counts)


def centred(rng, shape, scale, most, cuts=(), kind=jnp.bfloat16):
    drawn = jax.random.normal(rng, shape, jnp.float32) * scale
    if len(cuts) > 0:
        drawn = steps_of(rng, shape, cuts, -0.22, 0.18) * drawn
    return jnp.clip(drawn, min=-most, max=most).astype(kind)


def setup_inputs(seed: int = 0) -> dict:
    seeds = jax.random.split(jax.random.key(seed), 22)
    states = centred(seeds[0], (TOKENS, D), 1.0, 6.0, ((0, 32),))
    w_query = centred(seeds[1], (D, D), (D // 2) ** -0.5, 0.1875, ((0, 32),))
    w_key = centred(seeds[2], (D, D), (D // 2) ** -0.5, 0.1875, ((0, 32),))
    w_value = centred(seeds[3], (D, D), D ** -0.5, 0.125, ((0, 32),))
    w_out = centred(seeds[4], (D, D), (D // 64) ** -0.5, 1.0, ((0, 32),))
    b_query = centred(seeds[5], (D,), 0.15, 0.59765625, ((0, 32),))
    b_key = centred(seeds[6], (D,), 0.15, 0.59765625, ((0, 32),))
    b_value = centred(seeds[7], (D,), 0.1, 0.3984375, ((0, 32),))
    attn_gain = jnp.clip(1.0 + 0.1 * jax.random.normal(seeds[8], (D,), jnp.float32), 0.5, 1.5).astype(jnp.bfloat16)
    ffn_gain = jnp.clip(1.0 + 0.1 * jax.random.normal(seeds[9], (D,), jnp.float32), 0.5, 1.5).astype(jnp.bfloat16)
    router = centred(seeds[10], (D, EXPERTS), (4 * D) ** -0.5, 0.0625, ((0, 32),))
    shared_gate = centred(seeds[11], (D, SH), D ** -0.5, 0.125, ((0, 16), (1, 2)))
    shared_up = centred(seeds[12], (D, SH), D ** -0.5, 0.125, ((0, 16), (1, 2)))
    shared_down = centred(seeds[13], (SH, D), SH ** -0.5, 0.078125, ((0, 2), (1, 16)))
    shared_scale = centred(seeds[14], (D,), D ** -0.5, 0.125, ((0, 32),))
    expert_gate = centred(seeds[15], (EXPERTS, D, FE), D ** -0.5, 0.125, ((0, 16), (2, 2)))
    expert_up = centred(seeds[16], (EXPERTS, D, FE), D ** -0.5, 0.125, ((0, 16), (2, 2)))
    expert_down = centred(seeds[17], (EXPERTS, FE, D), FE ** -0.5, 0.15625, ((0, 16), (1, 2)))
    routes_keys = jax.random.split(jax.random.fold_in(seeds[18], 1), TOKENS // TOK_DEV)
    routes_turns = jax.random.permutation(jax.random.fold_in(seeds[18], 3), TOKENS // TOK_DEV)
    routes = jax.vmap(lambda own, number: assign_block(jax.random.fold_in(seeds[18], 2), own, number, TOK_DEV, EXPERTS, TOP, CAP, 1))(routes_keys, routes_turns).reshape((TOKENS, TOP))
    prefix = with_ends(jax.random.randint(seeds[19], (DEVICES,), TOK_DEV // 10, TOK_DEV // 2 + 1), jax.random.fold_in(seeds[19], 1), TOK_DEV // 10, (TOK_DEV // 2 + 1) - 1).astype(jnp.int32)
    cotangent = centred(seeds[20], (TOKENS, D), 1.0, 6.0, ((0, 32),))
    return {"states": states, "w_query": w_query, "w_key": w_key, "w_value": w_value, "w_out": w_out, "b_query": b_query, "b_key": b_key, "b_value": b_value, "attn_gain": attn_gain, "ffn_gain": ffn_gain, "router": router, "shared_gate": shared_gate, "shared_up": shared_up, "shared_down": shared_down, "shared_scale": shared_scale, "expert_gate": expert_gate, "expert_up": expert_up, "expert_down": expert_down, "routes": routes, "prefix": prefix, "cotangent": cotangent}


highest = lax.Precision.HIGHEST
norm_eps = 1e-06
rope_base = 1000000.0

@jax.custom_vjp
def low(v):
    return lax.optimization_barrier(v.astype(jnp.bfloat16)).astype(jnp.float32)

@jax.custom_vjp
def low_back(v):
    return v

def low_keep(v):
    return (low(v), None)

def low_pass(kept, grad):
    return (grad,)

def back_keep(v):
    return (v, None)

def back_low(kept, grad):
    return (low(grad),)
low.defvjp(low_keep, low_pass)
low_back.defvjp(back_keep, back_low)

def matmul(left, right):
    return jnp.dot(left, right, precision=highest)

def rms_scale(values, gain):
    inverse = lax.rsqrt(lax.optimization_barrier(jnp.mean(values * values, axis=-1, keepdims=True)) + norm_eps)
    return values * inverse * gain

def rope_tables(length, head_size):
    position = jnp.arange(length, dtype=jnp.float32)
    freqs = rope_base ** (-jnp.arange(0, head_size, 2, dtype=jnp.float32) / head_size)
    angles = position[:, None] * freqs[None, :]
    angles = jnp.concatenate([angles, angles], axis=-1)
    return (jnp.cos(angles)[:, None, :], jnp.sin(angles)[:, None, :])

def rotate(values, cos_table, sine_table):
    half_size = values.shape[-1] // 2
    turned = jnp.concatenate([-values[..., half_size:], values[..., :half_size]], axis=-1)
    return values * cos_table + turned * sine_table

def slot_tables(route_rows, expert_count, capacity):
    flat_ids = route_rows.reshape(-1)
    hit_table = (flat_ids[:, None] == jnp.arange(expert_count, dtype=jnp.int32)[None, :]).astype(jnp.int32)
    before = jnp.cumsum(hit_table, axis=0) - hit_table
    place_ids = lax.optimization_barrier(jnp.sum(before * hit_table, axis=1))
    slot_ids = flat_ids * capacity + place_ids
    match_table = (slot_ids[None, :] == jnp.arange(expert_count * capacity, dtype=jnp.int32)[:, None]).astype(jnp.int32)
    slot_owner = lax.optimization_barrier(jnp.sum(match_table * jnp.arange(flat_ids.shape[0], dtype=jnp.int32)[None, :], axis=1))
    filled = lax.optimization_barrier(jnp.sum(match_table, axis=1))
    return (slot_ids, slot_owner, filled)

def reference(states, w_query, w_key, w_value, w_out, b_query, b_key, b_value, attn_gain, ffn_gain, router, shared_gate, shared_up, shared_down, shared_scale, expert_gate, expert_up, expert_down, routes, prefix, cotangent):
    devices = N_EXPERT * N_FSDP
    head_size = D // H
    score_scale = head_size ** (-0.5)
    slot_ids, slot_owner, filled = jax.vmap(lambda route_rows: slot_tables(route_rows, EXPERTS, CAP))(routes.reshape(devices, TOK_DEV, TOP))
    token_of = slot_owner // TOP
    cos_table, sine_table = rope_tables(TOK_DEV, head_size)
    position = jnp.arange(TOK_DEV, dtype=jnp.int32)
    causal = position[None, :] <= position[:, None]
    route_hit = (routes[:, :, None] == jnp.arange(EXPERTS, dtype=jnp.int32)[None, None, :]).astype(jnp.float32)

    def attend(block_args):
        queries, keys_rot, values_all, length = block_args
        visible = causal | (position[None, :] < length)
        scores = low_back(jnp.einsum('thd,shd->hts', queries, keys_rot, precision=highest) * score_scale)
        scores = jnp.where(visible[None], scores, -1e+30)
        weights = low(jax.nn.softmax(scores, axis=-1))
        attn_mixed = jnp.einsum('hts,shd->thd', weights, values_all, precision=highest)
        return attn_mixed.reshape(TOK_DEV, D)

    def expert_apply(block_args):
        row_block, gate_weight_matrix, up_weight_matrix, down_w = block_args
        gate_pre = low_back(matmul(row_block, gate_weight_matrix))
        up_pre = low_back(matmul(row_block, up_weight_matrix))
        expert_act = low(jax.nn.silu(gate_pre) * up_pre)
        return low_back(low(matmul(expert_act, down_w)))

    def forward(states, w_query, w_key, w_value, w_out, b_query, b_key, b_value, attn_gain, ffn_gain, router, shared_gate, shared_up, shared_down, shared_scale, expert_gate, expert_up, expert_down):
        normed = low(rms_scale(states, attn_gain))
        query_pre = low_back(matmul(normed, w_query) + b_query)
        key_pre = low_back(matmul(normed, w_key) + b_key)
        value_pre = low_back(matmul(normed, w_value) + b_value)
        queries = low(rotate(query_pre.reshape(devices, TOK_DEV, H, head_size), cos_table, sine_table))
        keys_rot = low(rotate(key_pre.reshape(devices, TOK_DEV, H, head_size), cos_table, sine_table))
        values_all = low(value_pre).reshape(devices, TOK_DEV, H, head_size)
        attn_mixed = lax.map(jax.checkpoint(attend), (queries, keys_rot, values_all, prefix))
        attn_mixed = low_back(low(attn_mixed.reshape(devices * TOK_DEV, D)))
        middle = states + low_back(matmul(attn_mixed, w_out))
        normed_ffn = low(rms_scale(middle, ffn_gain))
        logits = low_back(matmul(normed_ffn, router))
        chosen = lax.optimization_barrier(jnp.sum(route_hit * logits[:, None, :], axis=-1))
        gate_probs = jax.nn.softmax(chosen, axis=-1)
        gathered = jnp.take_along_axis(normed_ffn.reshape(devices, TOK_DEV, D), token_of[..., None], axis=1)
        gathered = gathered * filled[..., None].astype(jnp.float32)
        buckets = gathered.reshape(devices, EXPERTS, CAP, D).transpose(1, 0, 2, 3).reshape(EXPERTS, devices * CAP, D)
        buckets = low_back(buckets)
        results = lax.map(jax.checkpoint(expert_apply), (buckets, expert_gate, expert_up, expert_down))
        results = results.reshape(EXPERTS, devices, CAP, D).transpose(1, 0, 2, 3).reshape(devices, EXPERTS * CAP, D)
        picked = jnp.take_along_axis(results, slot_ids[..., None], axis=1).reshape(devices * TOK_DEV, TOP, D)
        routed = lax.optimization_barrier(jnp.sum(gate_probs[..., None] * picked, axis=1))
        sgate_pre = low_back(matmul(normed_ffn, shared_gate))
        sup_pre = low_back(matmul(normed_ffn, shared_up))
        shared_act = low(jax.nn.silu(sgate_pre) * sup_pre)
        shared_out = low_back(matmul(shared_act, shared_down))
        shared_mix = jax.nn.sigmoid(low_back(matmul(normed_ffn, shared_scale)))
        return middle + routed + shared_mix[:, None] * shared_out
    floats = [operand.astype(jnp.float32) for operand in (states, w_query, w_key, w_value, w_out, b_query, b_key, b_value, attn_gain, ffn_gain, router, shared_gate, shared_up, shared_down, shared_scale, expert_gate, expert_up, expert_down)]
    result, pullback = jax.vjp(forward, *floats)
    gradients = pullback(cotangent.astype(jnp.float32))
    return (result.astype(jnp.bfloat16), gradients[0], gradients[1], gradients[2], gradients[3], gradients[4], gradients[5], gradients[6], gradients[7], gradients[8], gradients[9], gradients[10], gradients[11], gradients[12], gradients[13], gradients[14], gradients[15], gradients[16], gradients[17])
```

```python
import functools

import jax
import jax.numpy as jnp
from jax import lax
from jax.experimental import pallas as pl
from jax.experimental.pallas import tpu as pltpu
from jax.sharding import PartitionSpec as P

H = 16


norm_eps = 1e-06
rope_base = 1000000.0


def rope_tables(length, head_size):
    position = jnp.arange(length, dtype=jnp.float32)
    freqs = rope_base ** (-jnp.arange(0, head_size, 2, dtype=jnp.float32) / head_size)
    angles = position[:, None] * freqs[None, :]
    angles = jnp.concatenate([angles, angles], axis=-1)
    return (jnp.cos(angles)[:, None, :], jnp.sin(angles)[:, None, :])


def rotate(values, cos_table, sine_table):
    half_size = values.shape[-1] // 2
    turned = jnp.concatenate([-values[..., half_size:], values[..., :half_size]], axis=-1)
    return values * cos_table + turned * sine_table


def unrotate(values, cos_table, sine_table):
    half_size = values.shape[-1] // 2
    moved = values * sine_table
    turned = jnp.concatenate([moved[..., half_size:], -moved[..., :half_size]], axis=-1)
    return values * cos_table + turned


def slot_tables(route_rows, expert_count, capacity):
    flat_ids = route_rows.reshape(-1)
    hit_table = (flat_ids[:, None] == jnp.arange(expert_count, dtype=jnp.int32)[None, :]).astype(
        jnp.int32
    )
    before = jnp.cumsum(hit_table, axis=0) - hit_table
    place_ids = jnp.sum(before * hit_table, axis=1)
    slot_ids = flat_ids * capacity + place_ids
    match_table = (
        slot_ids[None, :] == jnp.arange(expert_count * capacity, dtype=jnp.int32)[:, None]
    ).astype(jnp.int32)
    slot_owner = jnp.sum(
        match_table * jnp.arange(flat_ids.shape[0], dtype=jnp.int32)[None, :], axis=1
    )
    filled = jnp.sum(match_table, axis=1)
    return (slot_ids, slot_owner, filled)


def crossing_token_rows(left, right):
    return lax.dot_general(
        left, right, (((0,), (0,)), ((), ())), preferred_element_type=jnp.float32
    )


def multiply_by_transpose(left, right):
    return lax.dot_general(
        left, right, (((1,), (1,)), ((), ())), preferred_element_type=jnp.float32
    )


def rms_parts(values):
    inverse = lax.rsqrt(jnp.mean(values * values, axis=-1, keepdims=True) + norm_eps)
    return (inverse, values * inverse)


def norm_back(grad_in, unit_rows, inverse, gain_full):
    scaled = grad_in * gain_full
    grad_rows = inverse * (
        scaled - unit_rows * jnp.mean(scaled * unit_rows, axis=-1, keepdims=True)
    )
    return (grad_rows, jnp.sum(grad_in * unit_rows, axis=0))


def silu_slope(values):
    sigma = jax.nn.sigmoid(values)
    return sigma * (1.0 + values * (1.0 - sigma))


def shards(
    states,
    w_query,
    w_key,
    w_value,
    w_out,
    b_query,
    b_key,
    b_value,
    attn_gain,
    ffn_gain,
    router,
    shared_gate,
    shared_up,
    shared_down,
    shared_scale,
    expert_gate,
    expert_up,
    expert_down,
    routes,
    prefix,
    cotangent,
):
    length = states.shape[0]
    model_width = states.shape[1]
    head_count = H
    head_size = model_width // head_count
    expert_count = router.shape[1]
    top_count = routes.shape[1]
    capacity = 4 * length * top_count // (3 * expert_count)
    score_scale = head_size ** (-0.5)
    (
        query_full,
        key_full,
        value_full,
        out_full,
        query_bias,
        key_bias,
        value_bias,
        gain_attn,
        router_full,
        sscale_full,
        gain_ffn,
    ) = (
        lax.all_gather(w_query, ("expert", "fsdp"), axis=0, tiled=True),
        lax.all_gather(w_key, ("expert", "fsdp"), axis=0, tiled=True),
        lax.all_gather(w_value, ("expert", "fsdp"), axis=0, tiled=True),
        lax.all_gather(w_out, ("expert", "fsdp"), axis=0, tiled=True),
        lax.all_gather(b_query, ("expert", "fsdp"), axis=0, tiled=True),
        lax.all_gather(b_key, ("expert", "fsdp"), axis=0, tiled=True),
        lax.all_gather(b_value, ("expert", "fsdp"), axis=0, tiled=True),
        lax.all_gather(attn_gain, ("expert", "fsdp"), axis=0, tiled=True),
        lax.all_gather(router, ("expert", "fsdp"), axis=0, tiled=True),
        lax.all_gather(shared_scale, ("expert", "fsdp"), axis=0, tiled=True),
        lax.all_gather(ffn_gain, ("expert", "fsdp"), axis=0, tiled=True),
    )
    residual = states.astype(jnp.float32)
    inverse_a, unit_a = rms_parts(residual)
    gain_a = gain_attn.astype(jnp.float32)
    normed_a = (unit_a * gain_a).astype(jnp.bfloat16)
    query_pre = jnp.dot(
        normed_a, query_full, preferred_element_type=jnp.float32
    ) + query_bias.astype(jnp.float32)
    key_pre = jnp.dot(normed_a, key_full, preferred_element_type=jnp.float32) + key_bias.astype(
        jnp.float32
    )
    value_pre = jnp.dot(
        normed_a, value_full, preferred_element_type=jnp.float32
    ) + value_bias.astype(jnp.float32)
    cos_table, sine_table = rope_tables(length, head_size)
    queries = rotate(
        query_pre.reshape(length, head_count, head_size), cos_table, sine_table
    ).astype(jnp.bfloat16)
    keys_rot = rotate(key_pre.reshape(length, head_count, head_size), cos_table, sine_table).astype(
        jnp.bfloat16
    )
    values_all = value_pre.astype(jnp.bfloat16).reshape(length, head_count, head_size)
    position = jnp.arange(length, dtype=jnp.int32)
    visible = (position[None, :] <= position[:, None]) | (position[None, :] < prefix[0])

    def masked_scores():
        scores = (
            jnp.einsum("thd,shd->hts", queries, keys_rot, preferred_element_type=jnp.float32)
            * score_scale
        )
        return jnp.where(visible[None], scores, -1e30)

    scores = masked_scores()
    top_score = jnp.max(scores, axis=-1, keepdims=True)
    log_total = top_score + jnp.log(jnp.sum(jnp.exp(scores - top_score), axis=-1, keepdims=True))
    attn_probs = jnp.exp(scores - log_total)
    probs_low = attn_probs.astype(jnp.bfloat16)
    attn_mixed = (
        jnp.einsum("hts,shd->thd", probs_low, values_all, preferred_element_type=jnp.float32)
        .reshape(length, model_width)
        .astype(jnp.bfloat16)
    )
    middle = residual + jnp.dot(attn_mixed, out_full, preferred_element_type=jnp.float32)
    sgate_rows, sup_rows, sdown_rows = (
        lax.all_gather(shared_gate, "fsdp", axis=0, tiled=True),
        lax.all_gather(shared_up, "fsdp", axis=0, tiled=True),
        lax.all_gather(shared_down, "fsdp", axis=1, tiled=True),
    )
    inverse_f, unit_f = rms_parts(middle)
    gain_f = gain_ffn.astype(jnp.float32)
    normed_f = (unit_f * gain_f).astype(jnp.bfloat16)
    logits = jnp.dot(normed_f, router_full, preferred_element_type=jnp.float32)
    route_hit = (
        routes[:, :, None] == jnp.arange(expert_count, dtype=jnp.int32)[None, None, :]
    ).astype(jnp.float32)
    chosen = jnp.sum(route_hit * logits[:, None, :], axis=-1)
    gate_probs = jax.nn.softmax(chosen, axis=-1)
    slot_ids, slot_owner, filled = slot_tables(routes, expert_count, capacity)
    token_of = slot_owner // top_count
    slot_live = filled > 0
    outgoing = jnp.where(slot_live[:, None], normed_f[token_of], jnp.zeros((), jnp.bfloat16))
    arrived = lax.all_to_all(
        outgoing.reshape(expert_count, capacity, model_width),
        "fsdp",
        split_axis=0,
        concat_axis=0,
        tiled=True,
    )
    expert_token_rows = lax.all_gather(arrived, "expert", axis=0, tiled=True).reshape(
        -1, model_width
    )
    gate_weight_matrix = expert_gate[0]
    up_weight_matrix = expert_up[0]
    down_w = expert_down[0]
    gate_pre = jnp.dot(expert_token_rows, gate_weight_matrix, preferred_element_type=jnp.float32)
    up_pre = jnp.dot(expert_token_rows, up_weight_matrix, preferred_element_type=jnp.float32)
    expert_act = (jax.nn.silu(gate_pre) * up_pre).astype(jnp.bfloat16)
    expert_sum = lax.psum_scatter(
        jnp.dot(expert_act, down_w, preferred_element_type=jnp.float32).astype(jnp.bfloat16),
        "expert",
        scatter_dimension=0,
        tiled=True,
    )
    returned = lax.all_to_all(
        expert_sum.reshape(arrived.shape), "fsdp", split_axis=0, concat_axis=0, tiled=True
    )
    returned = returned.reshape(expert_count * capacity, model_width)
    picked = returned[slot_ids].reshape(length, top_count, model_width).astype(jnp.float32)
    routed = jnp.sum(gate_probs[..., None] * picked, axis=1)
    sgate_use, sup_use, sdown_use = (sgate_rows, sup_rows, sdown_rows)
    pair_rows_in = lax.all_gather(normed_f, "expert", axis=0, tiled=True)
    sgate_pre = jnp.dot(pair_rows_in, sgate_use, preferred_element_type=jnp.float32)
    sup_pre = jnp.dot(pair_rows_in, sup_use, preferred_element_type=jnp.float32)
    shared_act = (jax.nn.silu(sgate_pre) * sup_pre).astype(jnp.bfloat16)
    shared_out = lax.psum_scatter(
        jnp.dot(shared_act, sdown_use, preferred_element_type=jnp.float32).astype(jnp.bfloat16),
        "expert",
        scatter_dimension=0,
        tiled=True,
    ).astype(jnp.float32)
    mix_pre = jnp.dot(normed_f, sscale_full, preferred_element_type=jnp.float32)
    shared_mix = jax.nn.sigmoid(mix_pre)
    output = (middle + routed + shared_mix[:, None] * shared_out).astype(jnp.bfloat16)
    grad_out = cotangent.astype(jnp.float32)
    scaled_cot = (shared_mix[:, None] * grad_out).astype(jnp.bfloat16)
    grad_mix = (shared_mix * (1.0 - shared_mix) * jnp.sum(grad_out * shared_out, axis=-1)).astype(
        jnp.bfloat16
    )
    cot_rows = lax.all_gather(scaled_cot, "expert", axis=0, tiled=True)
    grad_sdown = crossing_token_rows(shared_act, cot_rows)
    grad_sscale = crossing_token_rows(normed_f, grad_mix)
    grad_sact = multiply_by_transpose(cot_rows, sdown_use)
    grad_sgate = (grad_sact * sup_pre * silu_slope(sgate_pre)).astype(jnp.bfloat16)
    grad_sup = (grad_sact * jax.nn.silu(sgate_pre)).astype(jnp.bfloat16)
    grad_sgate_w = crossing_token_rows(pair_rows_in, grad_sgate)
    grad_sup_w = crossing_token_rows(pair_rows_in, grad_sup)
    gate_rows = grad_sgate
    up_rows = grad_sup
    shared_in = lax.psum_scatter(
        (
            multiply_by_transpose(gate_rows, sgate_use) + multiply_by_transpose(up_rows, sup_use)
        ).astype(jnp.bfloat16),
        "expert",
        scatter_dimension=0,
        tiled=True,
    ).astype(jnp.float32)
    grad_sgate_own, grad_sup_own, grad_sdown_own = (
        lax.psum_scatter(grad_sgate_w, "fsdp", scatter_dimension=0, tiled=True),
        lax.psum_scatter(grad_sup_w, "fsdp", scatter_dimension=0, tiled=True),
        lax.psum_scatter(grad_sdown, "fsdp", scatter_dimension=1, tiled=True),
    )
    grad_gate = jnp.sum(grad_out[:, None, :] * picked, axis=-1)
    grad_chosen = gate_probs * (grad_gate - jnp.sum(gate_probs * grad_gate, axis=-1, keepdims=True))
    grad_logits = jnp.sum(route_hit * grad_chosen[..., None], axis=1).astype(jnp.bfloat16)
    grad_router_all = crossing_token_rows(normed_f, grad_logits)
    grad_norm_f = shared_in + multiply_by_transpose(grad_logits, router_full)
    grad_norm_f = (
        grad_norm_f
        + grad_mix.astype(jnp.float32)[:, None] * sscale_full.astype(jnp.float32)[None, :]
    )
    gate_slot = gate_probs.reshape(-1)[slot_owner] * filled.astype(jnp.float32)
    grad_slots = (gate_slot[:, None] * grad_out[token_of]).astype(jnp.bfloat16)
    grad_arrived = lax.all_to_all(
        grad_slots.reshape(expert_count, capacity, model_width),
        "fsdp",
        split_axis=0,
        concat_axis=0,
        tiled=True,
    )
    grad_y = lax.all_gather(grad_arrived, "expert", axis=0, tiled=True).reshape(-1, model_width)
    gate_pullback_value, up_back = (gate_pre, up_pre)
    act_back = (jax.nn.silu(gate_pullback_value) * up_back).astype(jnp.bfloat16)
    grad_edown = crossing_token_rows(act_back, grad_y)
    activation_gradient = multiply_by_transpose(grad_y, down_w)
    expert_gate_gradient = (activation_gradient * up_back * silu_slope(gate_pullback_value)).astype(
        jnp.bfloat16
    )
    expert_up_gradient = (activation_gradient * jax.nn.silu(gate_pullback_value)).astype(
        jnp.bfloat16
    )
    grad_egate_w = crossing_token_rows(expert_token_rows, expert_gate_gradient)
    expert_up_weight_gradient = crossing_token_rows(expert_token_rows, expert_up_gradient)
    gate_rows = expert_gate_gradient
    up_rows = expert_up_gradient
    grad_rowin = lax.psum_scatter(
        multiply_by_transpose(gate_rows, gate_weight_matrix)
        + multiply_by_transpose(up_rows, up_weight_matrix),
        "expert",
        scatter_dimension=0,
        tiled=True,
    )
    grad_back = lax.all_to_all(
        grad_rowin.astype(jnp.bfloat16).reshape(arrived.shape),
        "fsdp",
        split_axis=0,
        concat_axis=0,
        tiled=True,
    )
    grad_back = grad_back.reshape(expert_count * capacity, model_width)
    grad_norm_f = grad_norm_f + jnp.sum(
        grad_back[slot_ids].reshape(length, top_count, model_width).astype(jnp.float32), axis=1
    )
    grad_from_f, grad_gain_f = norm_back(grad_norm_f, unit_f, inverse_f, gain_f)
    grad_mid = grad_out + grad_from_f
    grad_attn = grad_mid.astype(jnp.bfloat16)
    grad_wout = crossing_token_rows(attn_mixed, grad_attn)
    grad_mixed = (
        multiply_by_transpose(grad_attn, out_full)
        .astype(jnp.bfloat16)
        .reshape(length, head_count, head_size)
    )
    probs_again = jnp.exp(masked_scores() - log_total)
    probs_low_again = probs_again.astype(jnp.bfloat16)
    grad_probs = jnp.einsum(
        "thd,shd->hts", grad_mixed, values_all, preferred_element_type=jnp.float32
    )
    row_inner = jnp.sum(probs_again * grad_probs, axis=-1, keepdims=True)
    grad_scores = (probs_again * (grad_probs - row_inner)).astype(jnp.bfloat16)
    grad_q = (
        jnp.einsum("hts,shd->thd", grad_scores, keys_rot, preferred_element_type=jnp.float32)
        * score_scale
    )
    grad_k = (
        jnp.einsum("hts,thd->shd", grad_scores, queries, preferred_element_type=jnp.float32)
        * score_scale
    )
    grad_v = jnp.einsum(
        "hts,thd->shd", probs_low_again, grad_mixed, preferred_element_type=jnp.float32
    )
    grad_qpre = (
        unrotate(grad_q, cos_table, sine_table).reshape(length, model_width).astype(jnp.bfloat16)
    )
    grad_kpre = (
        unrotate(grad_k, cos_table, sine_table).reshape(length, model_width).astype(jnp.bfloat16)
    )
    grad_vpre = grad_v.reshape(length, model_width).astype(jnp.bfloat16)
    grad_norm_a = (
        multiply_by_transpose(grad_qpre, query_full)
        + multiply_by_transpose(grad_kpre, key_full)
        + multiply_by_transpose(grad_vpre, value_full)
    )
    grad_from_a, grad_gain_a = norm_back(grad_norm_a, unit_a, inverse_a, gain_a)
    grad_states = grad_mid + grad_from_a
    (
        grad_wq_own,
        grad_wk_own,
        grad_wv_own,
        grad_wo_own,
        grad_bq_own,
        grad_bk_own,
        grad_bv_own,
        grad_ga_own,
        grad_gf_own,
        grad_router_own,
        grad_sscale_own,
    ) = (
        lax.psum_scatter(
            crossing_token_rows(normed_a, grad_qpre),
            ("expert", "fsdp"),
            scatter_dimension=0,
            tiled=True,
        ),
        lax.psum_scatter(
            crossing_token_rows(normed_a, grad_kpre),
            ("expert", "fsdp"),
            scatter_dimension=0,
            tiled=True,
        ),
        lax.psum_scatter(
            crossing_token_rows(normed_a, grad_vpre),
            ("expert", "fsdp"),
            scatter_dimension=0,
            tiled=True,
        ),
        lax.psum_scatter(grad_wout, ("expert", "fsdp"), scatter_dimension=0, tiled=True),
        lax.psum_scatter(
            jnp.sum(grad_qpre.astype(jnp.float32), axis=0),
            ("expert", "fsdp"),
            scatter_dimension=0,
            tiled=True,
        ),
        lax.psum_scatter(
            jnp.sum(grad_kpre.astype(jnp.float32), axis=0),
            ("expert", "fsdp"),
            scatter_dimension=0,
            tiled=True,
        ),
        lax.psum_scatter(
            jnp.sum(grad_vpre.astype(jnp.float32), axis=0),
            ("expert", "fsdp"),
            scatter_dimension=0,
            tiled=True,
        ),
        lax.psum_scatter(grad_gain_a, ("expert", "fsdp"), scatter_dimension=0, tiled=True),
        lax.psum_scatter(grad_gain_f, ("expert", "fsdp"), scatter_dimension=0, tiled=True),
        lax.psum_scatter(grad_router_all, ("expert", "fsdp"), scatter_dimension=0, tiled=True),
        lax.psum_scatter(grad_sscale, ("expert", "fsdp"), scatter_dimension=0, tiled=True),
    )
    return (
        output,
        grad_states,
        grad_wq_own,
        grad_wk_own,
        grad_wv_own,
        grad_wo_own,
        grad_bq_own,
        grad_bk_own,
        grad_bv_own,
        grad_ga_own,
        grad_gf_own,
        grad_router_own,
        grad_sgate_own,
        grad_sup_own,
        grad_sdown_own,
        grad_sscale_own,
        grad_egate_w[None],
        expert_up_weight_gradient[None],
        grad_edown[None],
    )


def place():
    f = lax.axis_index("fsdp")
    return (f, f // 4, (f // 2) % 2, f % 2, f + 2 - 4 * ((f // 2) % 2), f + 1 - 2 * (f % 2))


def at_unit(target):
    return {"fsdp": target}


def greet(f, z, fx, fc, steps):
    barrier = pltpu.get_barrier_semaphore()

    def hello(target):
        pl.semaphore_signal(barrier, inc=1, device_id=at_unit(target))

    hello(fx)
    hello(fc)
    pl.when(z > 0)(lambda: hello(f - 4))
    pl.when(z < steps - 1)(lambda: hello(f + 4))
    count = 2 + jnp.where(z > 0, 1, 0) + jnp.where(z < steps - 1, 1, 0)
    pl.semaphore_wait(barrier, count)


def greet_all(units):
    barrier = pltpu.get_barrier_semaphore()
    e, f = lax.axis_index("expert"), lax.axis_index("fsdp")
    me = e * units + f

    def hello(step, carry):
        to = lax.rem(me + step, 2 * units)
        pl.semaphore_signal(
            barrier, inc=1, device_id={"expert": to // units, "fsdp": lax.rem(to, units)}
        )
        return carry

    lax.fori_loop(1, 2 * units, hello, 0)
    pl.semaphore_wait(barrier, 2 * units - 1)


def gather_body(steps, x_ref, out_ref, up_sem, down_sem, x_sem, c_sem, z_in, x_in, c_in):
    f, z, x, c, fx, fc = place()

    def copy(src, slot, target, done, arrived):
        return pltpu.make_async_remote_copy(
            src_ref=src,
            dst_ref=out_ref.at[slot],
            send_sem=done,
            recv_sem=arrived,
            device_id=at_unit(target),
        )

    def own_slot(at):
        return f + 4 * (at - z)

    def source(k, at):
        return x_ref if k == 0 else out_ref.at[own_slot(at)]

    def up(k, at):
        return copy(source(k, at), own_slot(at), f + 4, up_sem.at[at], z_in.at[at])

    def down(k, at):
        return copy(source(k, at), own_slot(at), f - 4, down_sem.at[at], z_in.at[at])

    def side(k, at):
        return copy(source(k, at), own_slot(at), fx, x_sem.at[at], x_in.at[at])

    def pair(k, at):
        index = x * steps + at
        return copy(source(k, at), own_slot(at), fc, c_sem.at[index], c_in.at[index])

    def step(k, below):
        at = z - k if below else z + k
        if k > 0:
            up(k, at).wait_recv()
        if k == 0 or below:
            pl.when(z < steps - 1)(lambda: up(k, at).start())
        if k == 0 or not below:
            pl.when(z > 0)(lambda: down(k, at).start())
        side(k, at).start()
        pair(k, at).start()

    def relay(k, below):
        at = z - k if below else z + k
        slot = fx + 4 * (at - z)
        index = (1 - x) * steps + at
        copy(out_ref.at[slot], slot, fx, x_sem.at[at], x_in.at[at]).wait_recv()
        copy(out_ref.at[slot], slot, fc, c_sem.at[index], c_in.at[index]).start()

    def begin():
        step(0, True)
        out_ref[f] = x_ref[...]

    def finish():
        for k in range(1, steps):
            pl.when(z - k >= 0)(functools.partial(step, k, True))
            pl.when(z + k < steps)(functools.partial(step, k, False))
            if k == 1:
                relay(0, True)
            else:
                pl.when(z - k + 1 >= 0)(functools.partial(relay, k - 1, True))
                pl.when(z + k - 1 < steps)(functools.partial(relay, k - 1, False))
        pl.when(z - steps + 1 >= 0)(functools.partial(relay, steps - 1, True))
        pl.when(z + steps - 1 < steps)(functools.partial(relay, steps - 1, False))
        for at in range(steps):
            pl.when((at <= z) & (z < steps - 1))(lambda at=at: up(1, at).wait_send())
            pl.when((at >= z) & (z > 0))(lambda at=at: down(1, at).wait_send())
            side(1, at).wait_send()
            for col in range(2):
                slot = 4 * at + 2 * col + 1 - c
                index = col * steps + at
                copy(out_ref.at[slot], slot, fc, c_sem.at[index], c_in.at[index]).wait()

    return begin, finish


def gather_sems(steps):
    dma = pltpu.SemaphoreType.DMA
    return [dma((n * steps,)) for n in (1, 1, 1, 2, 1, 1, 2)]


def gather_kernel(steps, x_ref, out_ref, *sems):
    f, z, x, c, fx, fc = place()
    greet(f, z, fx, fc, steps)
    begin, finish = gather_body(steps, x_ref, out_ref, *sems)
    begin()
    finish()


vmem = pl.BlockSpec(memory_space=pltpu.VMEM)
wire = pl.CostEstimate(flops=50_000_000_000, bytes_accessed=20_000_000, transcendentals=0)


def wire_params(which):
    return pltpu.CompilerParams(
        collective_id=which, has_side_effects=True, vmem_limit_bytes=60 << 20
    )


def gather_rows(value, units, which):
    rows, width = value.shape
    steps = units // 4
    return pl.pallas_call(
        functools.partial(gather_kernel, steps),
        out_shape=jax.ShapeDtypeStruct((units, rows, width), value.dtype),
        in_specs=[vmem],
        out_specs=vmem,
        scratch_shapes=gather_sems(steps),
        compiler_params=wire_params(which),
        cost_estimate=wire,
    )(value)


def start_kernel(
    units,
    x_ref,
    meta_ref,
    wq_ref,
    wk_ref,
    wv_ref,
    wo_ref,
    out_ref,
    meta_out,
    qkv_out,
    wo_out,
    meta_sent,
    meta_in,
    piece_sent,
    piece_in,
    other_sent,
    other_in,
    wo_sent,
    wo_in,
    *sems,
):
    steps = units // 4
    e, f = lax.axis_index("expert"), lax.axis_index("fsdp")
    me = e * units + f
    part, width = wq_ref.shape
    head = width // units
    greet_all(units)
    begin, finish = gather_body(steps, x_ref, out_ref, *sems)

    def rows_of(owner):
        return pl.ds(pl.multiple_of(owner * part, part), part)

    def columns_of(unit):
        return pl.ds(pl.multiple_of(unit * head, head), head)

    def meta_copy(step):
        to = lax.rem(me + step, 2 * units)
        return pltpu.make_async_remote_copy(
            src_ref=meta_ref,
            dst_ref=meta_out.at[me],
            send_sem=meta_sent.at[to],
            recv_sem=meta_in.at[me],
            device_id={"expert": to // units, "fsdp": lax.rem(to, units)},
        )

    def meta_got(owner):
        return pltpu.make_async_remote_copy(
            src_ref=meta_ref,
            dst_ref=meta_out.at[owner],
            send_sem=meta_sent.at[owner],
            recv_sem=meta_in.at[owner],
            device_id={"expert": e, "fsdp": f},
        )

    def piece(index, w_ref, owner, unit):
        return pltpu.make_async_remote_copy(
            src_ref=w_ref.at[:, columns_of(unit)],
            dst_ref=qkv_out.at[rows_of(owner), pl.ds(index * head, head)],
            send_sem=piece_sent.at[unit, index],
            recv_sem=piece_in.at[lax.rem(owner, units), index],
            device_id={"fsdp": unit},
        )

    def wo_copy(side):
        return pltpu.make_async_remote_copy(
            src_ref=wo_ref,
            dst_ref=wo_out.at[rows_of(lax.rem(me, 2))],
            send_sem=wo_sent.at[side],
            recv_sem=wo_in.at[lax.rem(me, 2)],
            device_id={"expert": side, "fsdp": me // 2},
        )

    def other_own(index, w_ref):
        return pltpu.make_async_remote_copy(
            src_ref=w_ref.at[:, columns_of(f)],
            dst_ref=qkv_out.at[rows_of(me), pl.ds(index * head, head)],
            send_sem=other_sent.at[f, index],
            recv_sem=other_in.at[f, index],
            device_id={"expert": 1 - e},
        )

    def other_piece(unit, half):
        owner = half * units + unit
        return pltpu.make_async_remote_copy(
            src_ref=qkv_out.at[rows_of(owner)],
            dst_ref=qkv_out.at[rows_of(owner)],
            send_sem=other_sent.at[unit, 0],
            recv_sem=other_in.at[unit, 0],
            device_id={"expert": 1 - e},
        )

    weights = ((0, wq_ref), (1, wk_ref), (2, wv_ref))

    def send_meta(step, carry):
        meta_copy(step).start()
        return carry

    lax.fori_loop(1, 2 * units, send_meta, 0)

    def send_pieces(step, carry):
        unit = lax.rem(f + step, units)
        for index, w_ref in weights:
            piece(index, w_ref, me, unit).start()
        return carry

    lax.fori_loop(1, units, send_pieces, 0)
    for index, w_ref in weights:
        other_own(index, w_ref).start()
    for side in range(2):
        away = jnp.logical_or(e != side, me // 2 != f)
        pl.when(away)(lambda side=side: wo_copy(side).start())
    begin()
    meta_out[me] = meta_ref[...]
    for index, w_ref in weights:
        qkv_out[rows_of(me), pl.ds(index * head, head)] = w_ref[:, columns_of(f)]

    def home(side):
        wo_out[rows_of(lax.rem(me, 2))] = wo_ref[...]

    for side in range(2):
        stays = jnp.logical_and(e == side, me // 2 == f)
        pl.when(stays)(functools.partial(home, side))

    def wait_pieces(step, carry):
        unit = lax.rem(f + step, units)
        for index, w_ref in weights:
            piece(index, w_ref, e * units + unit, unit).wait_recv()
        return carry

    lax.fori_loop(1, units, wait_pieces, 0)

    def pass_on(step, carry):
        other_piece(lax.rem(f + step, units), e).start()
        return carry

    lax.fori_loop(1, units, pass_on, 0)
    finish()

    def wait_meta(step, carry):
        meta_copy(step).wait_send()
        meta_got(lax.rem(me + step, 2 * units)).wait_recv()
        return carry

    lax.fori_loop(1, 2 * units, wait_meta, 0)

    def wait_sent(step, carry):
        unit = lax.rem(f + step, units)
        for index, w_ref in weights:
            piece(index, w_ref, me, unit).wait_send()
        other_piece(unit, e).wait_send()
        other_piece(unit, 1 - e).wait_recv()
        return carry

    lax.fori_loop(1, units, wait_sent, 0)
    for index, w_ref in weights:
        other_own(index, w_ref).wait_send()
        pltpu.make_async_remote_copy(
            src_ref=w_ref.at[:, columns_of(f)],
            dst_ref=qkv_out.at[
                rows_of((1 - e) * units + f), pl.ds(index * head, head)
            ],
            send_sem=other_sent.at[f, index],
            recv_sem=other_in.at[f, index],
            device_id={"expert": 1 - e},
        ).wait_recv()

    def wo_in_wait(half):
        pltpu.make_async_remote_copy(
            src_ref=wo_ref,
            dst_ref=wo_out.at[rows_of(half)],
            send_sem=wo_sent.at[0],
            recv_sem=wo_in.at[half],
            device_id={"expert": e, "fsdp": f},
        ).wait_recv()

    for side in range(2):
        away = jnp.logical_or(e != side, me // 2 != f)
        pl.when(away)(lambda side=side: wo_copy(side).wait_send())
    for half in range(2):
        pl.when(2 * f + half != me)(functools.partial(wo_in_wait, half))


def start(states, meta, w_query, w_key, w_value, w_out, units):
    rows, width = states.shape
    steps = units // 4
    head = width // units
    dma = pltpu.SemaphoreType.DMA
    return pl.pallas_call(
        functools.partial(start_kernel, units),
        out_shape=(
            jax.ShapeDtypeStruct((units, rows, width), states.dtype),
            jax.ShapeDtypeStruct((2 * units,) + meta.shape, meta.dtype),
            jax.ShapeDtypeStruct((width, 3 * head), states.dtype),
            jax.ShapeDtypeStruct((head, width), states.dtype),
        ),
        in_specs=[vmem] * 6,
        out_specs=(vmem,) * 4,
        scratch_shapes=[dma((2 * units,))] * 2
        + [dma((units, 3))] * 4
        + [dma((2,))] * 2
        + gather_sems(steps),
        compiler_params=wire_params(0),
        cost_estimate=wire,
    )(states, meta, w_query, w_key, w_value, w_out)


def scatter_kernel(steps, extra, wide_extra, *refs):
    if extra:
        p_ref, ex_ref, out_ref, ex_out, ex_sent, ex_in = refs[:6]
        refs = refs[6:]
    else:
        p_ref, out_ref = refs[:2]
        refs = refs[2:]
    c_buf, x_out, x_buf, z_out, z_buf, c_sem, x_sem, z_sem, c_in, x_in, z_in = refs
    f, z, x, c, fx, fc = place()
    units = 4 * steps
    if extra:
        greet_all(units)
        e = lax.axis_index("expert")
        me = e * units + f if wide_extra else f
        count = 2 * units if wide_extra else units

        def ex_copy(step):
            to = lax.rem(me + step, count)
            target = {"expert": to // units, "fsdp": lax.rem(to, units)}
            return pltpu.make_async_remote_copy(
                src_ref=ex_ref.at[to],
                dst_ref=ex_out.at[me],
                send_sem=ex_sent.at[to],
                recv_sem=ex_in.at[me],
                device_id=target if wide_extra else at_unit(to),
            )

        def ex_got(owner):
            return pltpu.make_async_remote_copy(
                src_ref=ex_ref.at[owner],
                dst_ref=ex_out.at[owner],
                send_sem=ex_sent.at[owner],
                recv_sem=ex_in.at[owner],
                device_id=at_unit(f),
            )

        def ex_send(step, carry):
            ex_copy(step).start()
            return carry

        def ex_wait(step, carry):
            ex_copy(step).wait_send()
            ex_got(lax.rem(me + step, count)).wait_recv()
            return carry
    else:
        greet(f, z, fx, fc, steps)

    def pair(col, at):
        return pltpu.make_async_remote_copy(
            src_ref=p_ref.at[4 * at + 2 * col + 1 - c],
            dst_ref=c_buf.at[col * steps + at],
            send_sem=c_sem.at[col * steps + at],
            recv_sem=c_in.at[col * steps + at],
            device_id=at_unit(fc),
        )

    def side(at):
        return pltpu.make_async_remote_copy(
            src_ref=x_out.at[at],
            dst_ref=x_buf.at[at],
            send_sem=x_sem.at[at],
            recv_sem=x_in.at[at],
            device_id=at_unit(fx),
        )

    def hop(at, up):
        slot = at if up else at + steps
        return pltpu.make_async_remote_copy(
            src_ref=z_out.at[at],
            dst_ref=z_buf.at[slot],
            send_sem=z_sem.at[at],
            recv_sem=z_in.at[slot],
            device_id=at_unit(f + 4 if up else f - 4),
        )

    def far(k, below):
        return z - k if below else z + k

    def each(first, last, body):
        for k in range(first, last - 1, -1):
            if k == 0:
                body(0, True)
            else:
                pl.when(z - k >= 0)(functools.partial(body, k, True))
                pl.when(z + k < steps)(functools.partial(body, k, False))

    each(steps - 1, 0, lambda k, below: pair(1 - x, far(k, below)).start())
    each(steps - 1, 0, lambda k, below: pair(x, far(k, below)).start())
    if extra:
        lax.fori_loop(1, count, ex_send, 0)
        ex_out[me] = ex_ref[me]

    def wide(value):
        return value.astype(jnp.float32)

    def send_side(k, below):
        at = far(k, below)
        pair(1 - x, at).wait_recv()
        total = wide(p_ref[4 * at + 2 * (1 - x) + c]) + wide(c_buf[(1 - x) * steps + at])
        x_out[at] = total.astype(x_out.dtype)
        side(at).start()

    each(steps - 1, 0, send_side)

    def send_hop(k, below):
        at = far(k, below)
        pair(x, at).wait_recv()
        side(at).wait_recv()
        up = not below

        def total():
            return (
                wide(p_ref[4 * at + 2 * x + c])
                + wide(c_buf[x * steps + at])
                + wide(x_buf[at])
            )

        def add():
            hop(at, up).wait_recv()
            z_out[at] = (total() + wide(z_buf[at if up else at + steps])).astype(z_out.dtype)

        def plain():
            z_out[at] = total().astype(z_out.dtype)

        more = z > 0 if up else z < steps - 1
        pl.when(more)(add)
        pl.when(jnp.logical_not(more))(plain)
        hop(at, up).start()

    each(steps - 1, 1, send_hop)
    pair(x, z).wait_recv()
    side(z).wait_recv()
    out_ref[...] = wide(p_ref[f]) + wide(c_buf[x * steps + z]) + wide(x_buf[z])

    def from_below():
        hop(z, True).wait_recv()
        out_ref[...] += wide(z_buf[z])

    def from_above():
        hop(z, False).wait_recv()
        out_ref[...] += wide(z_buf[z + steps])

    pl.when(z > 0)(from_below)
    pl.when(z < steps - 1)(from_above)
    for at in range(steps):
        pair(0, at).wait_send()
        pair(1, at).wait_send()
        side(at).wait_send()
        pl.when(z != at)(lambda at=at: hop(at, True).wait_send())
    if extra:
        lax.fori_loop(1, count, ex_wait, 0)


def scatter_rows(value, which, extra=None, wide_extra=False):
    units, rows, width = value.shape
    steps = units // 4
    dma = pltpu.SemaphoreType.DMA

    def buffers(count):
        return pltpu.VMEM((count, rows, width), value.dtype)

    out = jax.ShapeDtypeStruct((rows, width), jnp.float32)
    operands, scratch = [value], []
    if extra is not None:
        out = (out, jax.ShapeDtypeStruct(extra.shape, extra.dtype))
        operands, scratch = [value, extra], [dma((extra.shape[0],))] * 2
    return pl.pallas_call(
        functools.partial(scatter_kernel, steps, extra is not None, wide_extra),
        out_shape=out,
        in_specs=[vmem] * len(operands),
        out_specs=vmem if extra is None else (vmem, vmem),
        scratch_shapes=scratch
        + [buffers(n * steps) for n in (2, 1, 1, 1, 2)]
        + [dma((n * steps,)) for n in (2, 1, 1, 2, 1, 2)],
        compiler_params=wire_params(which),
        cost_estimate=wire,
    )(*operands)


def swap(value):
    return lax.ppermute(value, "expert", ((0, 1), (1, 0)))


def spread(value):
    return lax.all_to_all(value, "fsdp", split_axis=0, concat_axis=0, tiled=True)


def low(value):
    return value.astype(jnp.bfloat16)


def full(value):
    return value.astype(jnp.float32)


def mul(left, right):
    return jnp.dot(left, right, preferred_element_type=jnp.float32)


def plane_shards(
    states,
    w_query,
    w_key,
    w_value,
    w_out,
    b_query,
    b_key,
    b_value,
    attn_gain,
    ffn_gain,
    router,
    shared_gate,
    shared_up,
    shared_down,
    shared_scale,
    expert_gate,
    expert_up,
    expert_down,
    routes,
    prefix,
    cotangent,
):
    length, width = states.shape
    units = router.shape[1]
    head_size = width // units
    part = w_query.shape[0]
    top_count = routes.shape[1]
    capacity = 4 * length * top_count // (3 * units)
    plane = units * length
    slots = units * capacity
    score_scale = head_size ** (-0.5)
    side = lax.axis_index("expert")
    unit = lax.axis_index("fsdp")
    own_half = side == 0
    devices = tuple(range(2 * units))
    from_unit_a = tuple(((d % 2) * units + d // 2, d) for d in devices)
    from_unit_b = tuple(((1 - d % 2) * units + d // 2, d) for d in devices)

    vectors = jnp.concatenate(
        [
            jnp.stack([b_query, b_key, b_value, attn_gain, ffn_gain, shared_scale]),
            router.T,
        ]
    ).reshape(-1)
    count = vectors.shape[0]
    meta = jnp.concatenate([vectors, low(routes.reshape(-1)), low(prefix)])
    lines = -(-meta.shape[0] // 2048) * 16
    meta = jnp.pad(meta, (0, lines * 128 - meta.shape[0])).reshape(lines, 128)
    state_rows, meta, w_qkv, w_o = start(
        states, meta, w_query, w_key, w_value, w_out, units
    )
    meta = meta.reshape(2 * units, -1)
    vectors = meta[:, :count].reshape(2 * units, 6 + units, part)
    vectors = vectors.transpose(1, 0, 2).reshape(6 + units, width)
    gain_a = full(vectors[3])
    gain_f = full(vectors[4])
    small_w = jnp.concatenate([vectors[6:], vectors[5:6]])
    meta = lax.dynamic_index_in_dim(meta.reshape(2, units, -1), side, 0, keepdims=False)
    route_end = count + length * top_count
    plane_routes = meta[:, count:route_end].astype(jnp.int32).reshape(plane, top_count)
    prefixes = meta[:, route_end].astype(jnp.int32)

    hidden = shared_gate.shape[1] // units
    band = -(-2 * hidden // 128) * 128

    shared_own = jnp.stack([shared_gate.T, shared_up.T, shared_down])
    shared_own = shared_own.reshape(3, units, hidden, part * 2).transpose(1, 0, 2, 3)
    shared_own = spread(shared_own.reshape(units, 3 * hidden, part * 2))
    eg_other = swap(expert_gate[0])
    eu_other = swap(expert_up[0])
    ed = (expert_down[0], swap(expert_down[0]))

    state_rows = state_rows.reshape(plane, width)
    wide = full(state_rows)
    _, unit_rows = rms_parts(wide)
    normed_a = low(unit_rows * gain_a)
    bias = lax.dynamic_index_in_dim(
        full(vectors[:3]).reshape(3, units, head_size), unit, 1, keepdims=False
    )
    pre = mul(normed_a, w_qkv) + bias.reshape(1, -1)
    cos_table, sine_table = rope_tables(length, head_size)
    cos_table, sine_table = cos_table[:, 0], sine_table[:, 0]
    pre = pre.reshape(units, length, 3 * head_size)
    queries = low(rotate(pre[..., :head_size], cos_table, sine_table))
    keys_rot = low(rotate(pre[..., head_size : 2 * head_size], cos_table, sine_table))
    values_all = low(pre[..., 2 * head_size :])
    position = jnp.arange(length, dtype=jnp.int32)
    visible = (position[None, None, :] <= position[None, :, None]) | (
        position[None, None, :] < prefixes[:, None, None]
    )
    scores = (
        jnp.einsum("btd,bsd->bts", queries, keys_rot, preferred_element_type=jnp.float32)
        * score_scale
    )
    attn_probs = jax.nn.softmax(jnp.where(visible, scores, -1e30), axis=-1)
    probs_low = low(attn_probs)
    mixed = low(
        jnp.einsum("bts,bsd->btd", probs_low, values_all, preferred_element_type=jnp.float32)
    )
    mixed = mixed.reshape(plane, head_size)
    attn_part = low(mul(mixed, w_o)).reshape(units, length, width)
    attn_part, shared_own, eg_other = lax.optimization_barrier(
        (attn_part, shared_own, eg_other)
    )
    eg = (expert_gate[0], eg_other)
    shared_own = shared_own.transpose(1, 0, 2).reshape(3, hidden, width)
    shared_other = swap(shared_own)
    attn_out = scatter_rows(attn_part, 1)
    middle = full(states) + attn_out

    inverse_f, unit_f = rms_parts(middle)
    normed_f = low(unit_f * gain_f)
    normed_f, shared_other, eu_other = lax.optimization_barrier(
        (normed_f, shared_other, eu_other)
    )
    eu = (expert_up[0], eu_other)
    shared_all = jnp.concatenate(
        [
            shared_own,
            shared_other,
            jnp.zeros((3, band - 2 * hidden, width), jnp.bfloat16),
        ],
        axis=1,
    )
    s_gate, s_up, s_down = shared_all[0], shared_all[1], shared_all[2]
    rows = gather_rows(normed_f, units, 2)
    rows, cot_own = lax.optimization_barrier((rows, cotangent))
    cot_rows = lax.all_gather(cot_own, "fsdp", axis=0, tiled=True)
    rows = rows.reshape(plane, width)
    small = multiply_by_transpose(rows, small_w)
    logits, mix_pre = small[:, :units], small[:, units]
    unit_ids = jnp.arange(units, dtype=jnp.int32)
    route_hit = jnp.any(plane_routes[:, :, None] == unit_ids[None, None, :], axis=1)
    gates = jax.nn.softmax(jnp.where(route_hit, logits, -1e30), axis=-1)
    here = unit_ids == unit
    gate_here = jnp.sum(jnp.where(route_hit & here, gates, 0.0), axis=-1)
    gate_here = gate_here.reshape(units, length)
    hit = jnp.any(plane_routes == unit, axis=-1).reshape(units, length)
    hits = hit.astype(jnp.int32)
    place_ids = jnp.cumsum(hits, axis=1) - hits
    pick = hit[:, None, :] & (
        place_ids[:, None, :] == jnp.arange(capacity, dtype=jnp.int32)[None, :, None]
    )
    slot_gate = jnp.sum(jnp.where(pick, gate_here[:, None, :], 0.0), axis=-1).reshape(-1, 1)
    slot_of = jnp.where(hit, place_ids + capacity * unit_ids[:, None], -1).reshape(plane, 1)
    pick_back = low(slot_of == jnp.arange(slots, dtype=jnp.int32)[None, :])
    pick_low = low(pick)

    def take(value):
        return low(
            jnp.einsum(
                "spt,std->spd",
                pick_low,
                value.reshape(units, length, width),
                preferred_element_type=jnp.float32,
            )
        ).reshape(slots, width)

    shared_mix = jax.nn.sigmoid(mix_pre)[:, None]
    sgate_pre = multiply_by_transpose(rows, s_gate)
    sup_pre = multiply_by_transpose(rows, s_up)
    act_wide = jax.nn.silu(sgate_pre) * sup_pre
    act_mixed = low(shared_mix * act_wide)
    expert_rows = take(rows)
    gate_pre = [mul(expert_rows, w) for w in eg]
    up_pre = [mul(expert_rows, w) for w in eu]
    expert_act = [low(jax.nn.silu(g) * u) for g, u in zip(gate_pre, up_pre)]
    expert_y = mul(expert_act[0], ed[0]) + mul(expert_act[1], ed[1])
    ffn_part = low(
        mul(
            jnp.concatenate([act_mixed, pick_back], axis=1),
            jnp.concatenate([s_down, low(slot_gate * expert_y)]),
        )
    )
    ffn_part, cot_rows = lax.optimization_barrier((ffn_part, cot_rows))
    ffn_out = lax.psum_scatter(ffn_part, "fsdp", scatter_dimension=0, tiled=True)

    pull = multiply_by_transpose(cot_rows, s_down)
    mix_sum = jnp.sum(act_wide * pull, axis=-1)
    pull = shared_mix * pull
    grad_sgate = low(pull * sup_pre * silu_slope(sgate_pre))
    grad_sup = low(pull * jax.nn.silu(sgate_pre))
    cot_slots = take(cot_rows)
    pulls = [multiply_by_transpose(cot_slots, w) for w in ed]
    gate_sum = sum(jnp.sum(full(a) * p, axis=-1) for a, p in zip(expert_act, pulls))
    gate_sum = gate_sum.reshape(units, capacity)
    gate_sum = jnp.sum(jnp.where(pick, gate_sum[:, :, None], 0.0), axis=1)
    pulls = [slot_gate * p for p in pulls]
    grad_eg = [low(p * u * silu_slope(g)) for p, u, g in zip(pulls, up_pre, gate_pre)]
    grad_eu = [low(p * jax.nn.silu(g)) for p, g in zip(pulls, gate_pre)]
    rowin = sum(multiply_by_transpose(g, w) for g, w in zip(grad_eg + grad_eu, eg + eu))
    rows_part = low(
        mul(
            jnp.concatenate([grad_sgate, grad_sup, pick_back], axis=1),
            jnp.concatenate([s_gate, s_up, low(rowin)]),
        )
    )
    grad_ed = [crossing_token_rows(low(slot_gate * full(a)), cot_slots) for a in expert_act]
    grad_egw = [crossing_token_rows(expert_rows, g) for g in grad_eg]
    grad_euw = [crossing_token_rows(expert_rows, g) for g in grad_eu]
    grad_shared = jnp.stack(
        [
            crossing_token_rows(grad_sgate, rows),
            crossing_token_rows(grad_sup, rows),
            crossing_token_rows(act_mixed, cot_rows),
        ]
    )
    shared_pair = (grad_shared[:, :hidden], low(grad_shared[:, hidden : 2 * hidden]))
    egw_pair = (grad_egw[0], low(grad_egw[1]))
    euw_pair = (grad_euw[0], low(grad_euw[1]))
    ed_pair = (grad_ed[0], low(grad_ed[1]))
    rows_part, ffn_out, shared_pair, egw_pair, euw_pair, ed_pair = (
        lax.optimization_barrier(
            (rows_part, ffn_out, shared_pair, egw_pair, euw_pair, ed_pair)
        )
    )
    output = low(middle + full(ffn_out))
    shared_back = swap(shared_pair[1])
    egw_back = swap(egw_pair[1])
    euw_back = swap(euw_pair[1])
    ed_back = swap(ed_pair[1])
    scalars = jnp.stack([mix_sum.reshape(units, length), gate_sum], axis=1)
    lanes = -(-length // 128) * 128
    scalars = jnp.pad(scalars, ((0, 0), (0, 6), (0, lanes - length)))
    back, scalars = scatter_rows(
        rows_part.reshape(units, length, width), 3, scalars
    )

    grad_out = full(cotangent)
    own_small = multiply_by_transpose(normed_f, small_w)
    own_mix = jax.nn.sigmoid(own_small[:, units])
    own_hit = jnp.any(routes[:, :, None] == unit_ids[None, None, :], axis=1)
    own_gates = jax.nn.softmax(jnp.where(own_hit, own_small[:, :units], -1e30), axis=-1)
    own_gates = jnp.where(own_hit, own_gates, 0.0)
    mix_total = jnp.sum(scalars[:, 0, :length], axis=0)
    grad_mix = low(own_mix * (1.0 - own_mix) * mix_total)
    grad_gate = scalars[:, 1, :length].T
    grad_logits = low(
        own_gates * (grad_gate - jnp.sum(own_gates * grad_gate, axis=-1, keepdims=True))
    )
    grad_small = jnp.concatenate([grad_logits, grad_mix[:, None]], axis=1)
    grad_small_w = crossing_token_rows(grad_small, normed_f)
    grad_norm_f = back + mul(grad_small, small_w)
    grad_from_f, grad_gain_f = norm_back(grad_norm_f, unit_f, inverse_f, gain_f)
    grad_mid = grad_out + grad_from_f

    grad_low, shared_back, egw_back = lax.optimization_barrier(
        (low(grad_mid), shared_back, egw_back)
    )
    shared_sum = low(shared_pair[0] + full(shared_back))
    shared_sum = shared_sum.reshape(3 * hidden, units, part * 2).transpose(1, 0, 2)
    shared_sum = spread(shared_sum)
    grad_attn = gather_rows(grad_low, units, 4)
    grad_attn, euw_back = lax.optimization_barrier((grad_attn, euw_back))
    grad_attn = grad_attn.reshape(plane, width)
    grad_wo = crossing_token_rows(mixed, grad_attn)
    grad_mixed = low(multiply_by_transpose(grad_attn, w_o)).reshape(units, length, head_size)
    grad_probs = jnp.einsum(
        "btd,bsd->bts", grad_mixed, values_all, preferred_element_type=jnp.float32
    )
    row_inner = jnp.sum(attn_probs * grad_probs, axis=-1, keepdims=True)
    grad_scores = low(attn_probs * (grad_probs - row_inner))
    grad_q = (
        jnp.einsum("bts,bsd->btd", grad_scores, keys_rot, preferred_element_type=jnp.float32)
        * score_scale
    )
    grad_k = (
        jnp.einsum("bts,btd->bsd", grad_scores, queries, preferred_element_type=jnp.float32)
        * score_scale
    )
    grad_v = jnp.einsum(
        "bts,btd->bsd", probs_low, grad_mixed, preferred_element_type=jnp.float32
    )
    grad_pre = jnp.concatenate(
        [
            low(unrotate(grad_q, cos_table, sine_table)),
            low(unrotate(grad_k, cos_table, sine_table)),
            low(grad_v),
        ],
        axis=-1,
    ).reshape(plane, 3 * head_size)
    grad_qkv = crossing_token_rows(normed_a, grad_pre)
    grad_gain_a = jnp.sum(grad_qkv * full(w_qkv), axis=1) / gain_a
    grad_bias = jnp.sum(full(grad_pre), axis=0).reshape(3, head_size // part, part)
    norm_part = low(multiply_by_transpose(grad_pre, w_qkv)).reshape(units, length, width)

    norm_part, shared_sum = lax.optimization_barrier((norm_part, shared_sum))

    owners = jnp.arange(2 * units, dtype=jnp.int32)
    bias_rows = jnp.where(
        (owners // 2 == unit)[None, :, None], jnp.tile(grad_bias, (1, units, 1)), 0.0
    )
    tiny = jnp.concatenate([grad_small_w, grad_gain_a[None], grad_gain_f[None]])
    tiny = jnp.concatenate([tiny.reshape(units + 3, 2 * units, part), bias_rows])
    pad_rows = -(-tiny.shape[0] // 8) * 8 - tiny.shape[0]
    tiny = jnp.pad(tiny.transpose(1, 0, 2), ((0, 0), (0, pad_rows), (0, 128 - part)))
    grad_norm_a, tiny = scatter_rows(norm_part, 5, tiny, True)
    tiny = jnp.sum(tiny, axis=0)[:, :part]

    inverse_a, unit_a = rms_parts(full(states))
    grad_from_a, _ = norm_back(grad_norm_a, unit_a, inverse_a, gain_a)
    grad_states = grad_mid + grad_from_a

    def other_half(value):
        return lax.dynamic_index_in_dim(value, 1 - side, 0, keepdims=False)

    def this_half(value):
        return lax.dynamic_index_in_dim(value, side, 0, keepdims=False)

    grad_qkv = grad_qkv.reshape(2, units * part, 3 * head_size)
    grad_qkv = this_half(grad_qkv) + full(swap(low(other_half(grad_qkv))))
    grad_qkv = full(spread(low(grad_qkv).reshape(units, part, 3 * head_size)))
    grad_qkv = grad_qkv.reshape(units, part, 3, head_size).transpose(2, 1, 0, 3)
    grad_qkv = grad_qkv.reshape(3, part, width)

    blocks = grad_wo.reshape(2, part, width)
    grad_wo_own = lax.ppermute(
        jnp.where(own_half, blocks[0], blocks[1]), ("expert", "fsdp"), from_unit_a
    ) + lax.ppermute(
        jnp.where(own_half, blocks[1], blocks[0]), ("expert", "fsdp"), from_unit_b
    )

    def join(pair, received):
        return (pair[0] + full(received))[None]

    shared_sum = full(shared_sum).reshape(units, 3, hidden, part * 2)
    shared_sum = shared_sum.transpose(1, 0, 2, 3).reshape(3, units * hidden, part * 2)

    return (
        output,
        grad_states,
        grad_qkv[0],
        grad_qkv[1],
        grad_qkv[2],
        grad_wo_own,
        tiny[units + 3],
        tiny[units + 4],
        tiny[units + 5],
        tiny[units + 1],
        tiny[units + 2],
        tiny[:units].T,
        shared_sum[0].T,
        shared_sum[1].T,
        shared_sum[2],
        tiny[units],
        join(egw_pair, egw_back),
        join(euw_pair, euw_back),
        join(ed_pair, ed_back),
    )


def solution(mesh):
    placed = (
        P(("expert", "fsdp"), None),
        P(("expert", "fsdp"), None),
        P(("expert", "fsdp"), None),
        P(("expert", "fsdp"), None),
        P(("expert", "fsdp"), None),
        P(("expert", "fsdp")),
        P(("expert", "fsdp")),
        P(("expert", "fsdp")),
        P(("expert", "fsdp")),
        P(("expert", "fsdp")),
        P(("expert", "fsdp"), None),
        P("fsdp", "expert"),
        P("fsdp", "expert"),
        P("expert", "fsdp"),
        P(("expert", "fsdp")),
        P("fsdp", None, "expert"),
        P("fsdp", None, "expert"),
        P("fsdp", "expert", None),
        P(("expert", "fsdp"), None),
        P(("expert", "fsdp")),
        P(("expert", "fsdp"), None),
    )
    fits = mesh.shape["fsdp"] == H == 16 and mesh.shape["expert"] == 2
    return jax.shard_map(
        plane_shards if fits else shards,
        mesh=mesh,
        in_specs=placed,
        out_specs=(
            P(("expert", "fsdp"), None),
            P(("expert", "fsdp"), None),
            P(("expert", "fsdp"), None),
            P(("expert", "fsdp"), None),
            P(("expert", "fsdp"), None),
            P(("expert", "fsdp"), None),
            P(("expert", "fsdp")),
            P(("expert", "fsdp")),
            P(("expert", "fsdp")),
            P(("expert", "fsdp")),
            P(("expert", "fsdp")),
            P(("expert", "fsdp"), None),
            P("fsdp", "expert"),
            P("fsdp", "expert"),
            P("expert", "fsdp"),
            P(("expert", "fsdp")),
            P("fsdp", None, "expert"),
            P("fsdp", None, "expert"),
            P("fsdp", "expert", None),
        ),
        check_vma=False,
    )
```

```python
import functools

import jax
import jax.numpy as jnp
from jax import lax
from jax.experimental import pallas as pl
from jax.experimental.pallas import tpu as pltpu
from jax.sharding import PartitionSpec as P

H = 16
EXPERT, FSDP = "expert", "fsdp"


norm_eps = 1e-06
rope_base = 1000000.0


def rope_tables(length, head_size):
    position = jnp.arange(length, dtype=jnp.float32)
    freqs = rope_base ** (-jnp.arange(0, head_size, 2, dtype=jnp.float32) / head_size)
    angles = position[:, None] * freqs[None, :]
    angles = jnp.concatenate([angles, angles], axis=-1)
    return (jnp.cos(angles)[:, None, :], jnp.sin(angles)[:, None, :])


def rotate(values, cos_table, sine_table):
    half_size = values.shape[-1] // 2
    turned = jnp.concatenate([-values[..., half_size:], values[..., :half_size]], axis=-1)
    return values * cos_table + turned * sine_table


def unrotate(values, cos_table, sine_table):
    half_size = values.shape[-1] // 2
    moved = values * sine_table
    turned = jnp.concatenate([moved[..., half_size:], -moved[..., :half_size]], axis=-1)
    return values * cos_table + turned


def slot_tables(route_rows, expert_count, capacity):
    flat_ids = route_rows.reshape(-1)
    hit_table = (flat_ids[:, None] == jnp.arange(expert_count, dtype=jnp.int32)[None, :]).astype(
        jnp.int32
    )
    before = jnp.cumsum(hit_table, axis=0) - hit_table
    place_ids = jnp.sum(before * hit_table, axis=1)
    slot_ids = flat_ids * capacity + place_ids
    match_table = (
        slot_ids[None, :] == jnp.arange(expert_count * capacity, dtype=jnp.int32)[:, None]
    ).astype(jnp.int32)
    slot_owner = jnp.sum(
        match_table * jnp.arange(flat_ids.shape[0], dtype=jnp.int32)[None, :], axis=1
    )
    filled = jnp.sum(match_table, axis=1)
    return (slot_ids, slot_owner, filled)


def crossing_token_rows(left, right):
    return lax.dot_general(
        left, right, (((0,), (0,)), ((), ())), preferred_element_type=jnp.float32
    )


def multiply_by_transpose(left, right):
    return lax.dot_general(
        left, right, (((1,), (1,)), ((), ())), preferred_element_type=jnp.float32
    )


def rms_parts(values):
    inverse = lax.rsqrt(jnp.mean(values * values, axis=-1, keepdims=True) + norm_eps)
    return (inverse, values * inverse)


def norm_back(grad_in, unit_rows, inverse, gain_full):
    scaled = grad_in * gain_full
    grad_rows = inverse * (
        scaled - unit_rows * jnp.mean(scaled * unit_rows, axis=-1, keepdims=True)
    )
    return (grad_rows, jnp.sum(grad_in * unit_rows, axis=0))


def silu_slope(values):
    sigma = jax.nn.sigmoid(values)
    return sigma * (1.0 + values * (1.0 - sigma))


def shards(
    states,
    w_query,
    w_key,
    w_value,
    w_out,
    b_query,
    b_key,
    b_value,
    attn_gain,
    ffn_gain,
    router,
    shared_gate,
    shared_up,
    shared_down,
    shared_scale,
    expert_gate,
    expert_up,
    expert_down,
    routes,
    prefix,
    cotangent,
):
    length = states.shape[0]
    model_width = states.shape[1]
    head_count = H
    head_size = model_width // head_count
    expert_count = router.shape[1]
    top_count = routes.shape[1]
    capacity = 4 * length * top_count // (3 * expert_count)
    score_scale = head_size ** (-0.5)
    (
        query_full,
        key_full,
        value_full,
        out_full,
        query_bias,
        key_bias,
        value_bias,
        gain_attn,
        router_full,
        sscale_full,
        gain_ffn,
    ) = (
        lax.all_gather(w_query, (EXPERT, FSDP), axis=0, tiled=True),
        lax.all_gather(w_key, (EXPERT, FSDP), axis=0, tiled=True),
        lax.all_gather(w_value, (EXPERT, FSDP), axis=0, tiled=True),
        lax.all_gather(w_out, (EXPERT, FSDP), axis=0, tiled=True),
        lax.all_gather(b_query, (EXPERT, FSDP), axis=0, tiled=True),
        lax.all_gather(b_key, (EXPERT, FSDP), axis=0, tiled=True),
        lax.all_gather(b_value, (EXPERT, FSDP), axis=0, tiled=True),
        lax.all_gather(attn_gain, (EXPERT, FSDP), axis=0, tiled=True),
        lax.all_gather(router, (EXPERT, FSDP), axis=0, tiled=True),
        lax.all_gather(shared_scale, (EXPERT, FSDP), axis=0, tiled=True),
        lax.all_gather(ffn_gain, (EXPERT, FSDP), axis=0, tiled=True),
    )
    residual = states.astype(jnp.float32)
    inverse_a, unit_a = rms_parts(residual)
    gain_a = gain_attn.astype(jnp.float32)
    normed_a = (unit_a * gain_a).astype(jnp.bfloat16)
    query_pre = jnp.dot(
        normed_a, query_full, preferred_element_type=jnp.float32
    ) + query_bias.astype(jnp.float32)
    key_pre = jnp.dot(normed_a, key_full, preferred_element_type=jnp.float32) + key_bias.astype(
        jnp.float32
    )
    value_pre = jnp.dot(
        normed_a, value_full, preferred_element_type=jnp.float32
    ) + value_bias.astype(jnp.float32)
    cos_table, sine_table = rope_tables(length, head_size)
    queries = rotate(
        query_pre.reshape(length, head_count, head_size), cos_table, sine_table
    ).astype(jnp.bfloat16)
    keys_rot = rotate(key_pre.reshape(length, head_count, head_size), cos_table, sine_table).astype(
        jnp.bfloat16
    )
    values_all = value_pre.astype(jnp.bfloat16).reshape(length, head_count, head_size)
    position = jnp.arange(length, dtype=jnp.int32)
    visible = (position[None, :] <= position[:, None]) | (position[None, :] < prefix[0])

    def masked_scores():
        scores = (
            jnp.einsum("thd,shd->hts", queries, keys_rot, preferred_element_type=jnp.float32)
            * score_scale
        )
        return jnp.where(visible[None], scores, -1e30)

    scores = masked_scores()
    top_score = jnp.max(scores, axis=-1, keepdims=True)
    log_total = top_score + jnp.log(jnp.sum(jnp.exp(scores - top_score), axis=-1, keepdims=True))
    attn_probs = jnp.exp(scores - log_total)
    probs_low = attn_probs.astype(jnp.bfloat16)
    attn_mixed = (
        jnp.einsum("hts,shd->thd", probs_low, values_all, preferred_element_type=jnp.float32)
        .reshape(length, model_width)
        .astype(jnp.bfloat16)
    )
    middle = residual + jnp.dot(attn_mixed, out_full, preferred_element_type=jnp.float32)
    sgate_rows, sup_rows, sdown_rows = (
        lax.all_gather(shared_gate, FSDP, axis=0, tiled=True),
        lax.all_gather(shared_up, FSDP, axis=0, tiled=True),
        lax.all_gather(shared_down, FSDP, axis=1, tiled=True),
    )
    inverse_f, unit_f = rms_parts(middle)
    gain_f = gain_ffn.astype(jnp.float32)
    normed_f = (unit_f * gain_f).astype(jnp.bfloat16)
    logits = jnp.dot(normed_f, router_full, preferred_element_type=jnp.float32)
    route_hit = (
        routes[:, :, None] == jnp.arange(expert_count, dtype=jnp.int32)[None, None, :]
    ).astype(jnp.float32)
    chosen = jnp.sum(route_hit * logits[:, None, :], axis=-1)
    gate_probs = jax.nn.softmax(chosen, axis=-1)
    slot_ids, slot_owner, filled = slot_tables(routes, expert_count, capacity)
    token_of = slot_owner // top_count
    slot_live = filled > 0
    outgoing = jnp.where(slot_live[:, None], normed_f[token_of], jnp.zeros((), jnp.bfloat16))
    arrived = lax.all_to_all(
        outgoing.reshape(expert_count, capacity, model_width),
        FSDP,
        split_axis=0,
        concat_axis=0,
        tiled=True,
    )
    expert_token_rows = lax.all_gather(arrived, EXPERT, axis=0, tiled=True).reshape(
        -1, model_width
    )
    gate_weight_matrix = expert_gate[0]
    up_weight_matrix = expert_up[0]
    down_w = expert_down[0]
    gate_pre = jnp.dot(expert_token_rows, gate_weight_matrix, preferred_element_type=jnp.float32)
    up_pre = jnp.dot(expert_token_rows, up_weight_matrix, preferred_element_type=jnp.float32)
    expert_act = (jax.nn.silu(gate_pre) * up_pre).astype(jnp.bfloat16)
    expert_sum = lax.psum_scatter(
        jnp.dot(expert_act, down_w, preferred_element_type=jnp.float32).astype(jnp.bfloat16),
        EXPERT,
        scatter_dimension=0,
        tiled=True,
    )
    returned = lax.all_to_all(
        expert_sum.reshape(arrived.shape), FSDP, split_axis=0, concat_axis=0, tiled=True
    )
    returned = returned.reshape(expert_count * capacity, model_width)
    picked = returned[slot_ids].reshape(length, top_count, model_width).astype(jnp.float32)
    routed = jnp.sum(gate_probs[..., None] * picked, axis=1)
    sgate_use, sup_use, sdown_use = (sgate_rows, sup_rows, sdown_rows)
    pair_rows_in = lax.all_gather(normed_f, EXPERT, axis=0, tiled=True)
    sgate_pre = jnp.dot(pair_rows_in, sgate_use, preferred_element_type=jnp.float32)
    sup_pre = jnp.dot(pair_rows_in, sup_use, preferred_element_type=jnp.float32)
    shared_act = (jax.nn.silu(sgate_pre) * sup_pre).astype(jnp.bfloat16)
    shared_out = lax.psum_scatter(
        jnp.dot(shared_act, sdown_use, preferred_element_type=jnp.float32).astype(jnp.bfloat16),
        EXPERT,
        scatter_dimension=0,
        tiled=True,
    ).astype(jnp.float32)
    mix_pre = jnp.dot(normed_f, sscale_full, preferred_element_type=jnp.float32)
    shared_mix = jax.nn.sigmoid(mix_pre)
    output = (middle + routed + shared_mix[:, None] * shared_out).astype(jnp.bfloat16)
    grad_out = cotangent.astype(jnp.float32)
    scaled_cot = (shared_mix[:, None] * grad_out).astype(jnp.bfloat16)
    grad_mix = (shared_mix * (1.0 - shared_mix) * jnp.sum(grad_out * shared_out, axis=-1)).astype(
        jnp.bfloat16
    )
    cot_rows = lax.all_gather(scaled_cot, EXPERT, axis=0, tiled=True)
    grad_sdown = crossing_token_rows(shared_act, cot_rows)
    grad_sscale = crossing_token_rows(normed_f, grad_mix)
    grad_sact = multiply_by_transpose(cot_rows, sdown_use)
    grad_sgate = (grad_sact * sup_pre * silu_slope(sgate_pre)).astype(jnp.bfloat16)
    grad_sup = (grad_sact * jax.nn.silu(sgate_pre)).astype(jnp.bfloat16)
    grad_sgate_w = crossing_token_rows(pair_rows_in, grad_sgate)
    grad_sup_w = crossing_token_rows(pair_rows_in, grad_sup)
    gate_rows = grad_sgate
    up_rows = grad_sup
    shared_in = lax.psum_scatter(
        (
            multiply_by_transpose(gate_rows, sgate_use) + multiply_by_transpose(up_rows, sup_use)
        ).astype(jnp.bfloat16),
        EXPERT,
        scatter_dimension=0,
        tiled=True,
    ).astype(jnp.float32)
    grad_sgate_own, grad_sup_own, grad_sdown_own = (
        lax.psum_scatter(grad_sgate_w, FSDP, scatter_dimension=0, tiled=True),
        lax.psum_scatter(grad_sup_w, FSDP, scatter_dimension=0, tiled=True),
        lax.psum_scatter(grad_sdown, FSDP, scatter_dimension=1, tiled=True),
    )
    grad_gate = jnp.sum(grad_out[:, None, :] * picked, axis=-1)
    grad_chosen = gate_probs * (grad_gate - jnp.sum(gate_probs * grad_gate, axis=-1, keepdims=True))
    grad_logits = jnp.sum(route_hit * grad_chosen[..., None], axis=1).astype(jnp.bfloat16)
    grad_router_all = crossing_token_rows(normed_f, grad_logits)
    grad_norm_f = shared_in + multiply_by_transpose(grad_logits, router_full)
    grad_norm_f = (
        grad_norm_f
        + grad_mix.astype(jnp.float32)[:, None] * sscale_full.astype(jnp.float32)[None, :]
    )
    gate_slot = gate_probs.reshape(-1)[slot_owner] * filled.astype(jnp.float32)
    grad_slots = (gate_slot[:, None] * grad_out[token_of]).astype(jnp.bfloat16)
    grad_arrived = lax.all_to_all(
        grad_slots.reshape(expert_count, capacity, model_width),
        FSDP,
        split_axis=0,
        concat_axis=0,
        tiled=True,
    )
    grad_y = lax.all_gather(grad_arrived, EXPERT, axis=0, tiled=True).reshape(-1, model_width)
    gate_pullback_value, up_back = (gate_pre, up_pre)
    act_back = (jax.nn.silu(gate_pullback_value) * up_back).astype(jnp.bfloat16)
    grad_edown = crossing_token_rows(act_back, grad_y)
    activation_gradient = multiply_by_transpose(grad_y, down_w)
    expert_gate_gradient = (activation_gradient * up_back * silu_slope(gate_pullback_value)).astype(
        jnp.bfloat16
    )
    expert_up_gradient = (activation_gradient * jax.nn.silu(gate_pullback_value)).astype(
        jnp.bfloat16
    )
    grad_egate_w = crossing_token_rows(expert_token_rows, expert_gate_gradient)
    expert_up_weight_gradient = crossing_token_rows(expert_token_rows, expert_up_gradient)
    gate_rows = expert_gate_gradient
    up_rows = expert_up_gradient
    grad_rowin = lax.psum_scatter(
        multiply_by_transpose(gate_rows, gate_weight_matrix)
        + multiply_by_transpose(up_rows, up_weight_matrix),
        EXPERT,
        scatter_dimension=0,
        tiled=True,
    )
    grad_back = lax.all_to_all(
        grad_rowin.astype(jnp.bfloat16).reshape(arrived.shape),
        FSDP,
        split_axis=0,
        concat_axis=0,
        tiled=True,
    )
    grad_back = grad_back.reshape(expert_count * capacity, model_width)
    grad_norm_f = grad_norm_f + jnp.sum(
        grad_back[slot_ids].reshape(length, top_count, model_width).astype(jnp.float32), axis=1
    )
    grad_from_f, grad_gain_f = norm_back(grad_norm_f, unit_f, inverse_f, gain_f)
    grad_mid = grad_out + grad_from_f
    grad_attn = grad_mid.astype(jnp.bfloat16)
    grad_wout = crossing_token_rows(attn_mixed, grad_attn)
    grad_mixed = (
        multiply_by_transpose(grad_attn, out_full)
        .astype(jnp.bfloat16)
        .reshape(length, head_count, head_size)
    )
    probs_again = jnp.exp(masked_scores() - log_total)
    probs_low_again = probs_again.astype(jnp.bfloat16)
    grad_probs = jnp.einsum(
        "thd,shd->hts", grad_mixed, values_all, preferred_element_type=jnp.float32
    )
    row_inner = jnp.sum(probs_again * grad_probs, axis=-1, keepdims=True)
    grad_scores = (probs_again * (grad_probs - row_inner)).astype(jnp.bfloat16)
    grad_q = (
        jnp.einsum("hts,shd->thd", grad_scores, keys_rot, preferred_element_type=jnp.float32)
        * score_scale
    )
    grad_k = (
        jnp.einsum("hts,thd->shd", grad_scores, queries, preferred_element_type=jnp.float32)
        * score_scale
    )
    grad_v = jnp.einsum(
        "hts,thd->shd", probs_low_again, grad_mixed, preferred_element_type=jnp.float32
    )
    grad_qpre = (
        unrotate(grad_q, cos_table, sine_table).reshape(length, model_width).astype(jnp.bfloat16)
    )
    grad_kpre = (
        unrotate(grad_k, cos_table, sine_table).reshape(length, model_width).astype(jnp.bfloat16)
    )
    grad_vpre = grad_v.reshape(length, model_width).astype(jnp.bfloat16)
    grad_norm_a = (
        multiply_by_transpose(grad_qpre, query_full)
        + multiply_by_transpose(grad_kpre, key_full)
        + multiply_by_transpose(grad_vpre, value_full)
    )
    grad_from_a, grad_gain_a = norm_back(grad_norm_a, unit_a, inverse_a, gain_a)
    grad_states = grad_mid + grad_from_a
    (
        grad_wq_own,
        grad_wk_own,
        grad_wv_own,
        grad_wo_own,
        grad_bq_own,
        grad_bk_own,
        grad_bv_own,
        grad_ga_own,
        grad_gf_own,
        grad_router_own,
        grad_sscale_own,
    ) = (
        lax.psum_scatter(
            crossing_token_rows(normed_a, grad_qpre),
            (EXPERT, FSDP),
            scatter_dimension=0,
            tiled=True,
        ),
        lax.psum_scatter(
            crossing_token_rows(normed_a, grad_kpre),
            (EXPERT, FSDP),
            scatter_dimension=0,
            tiled=True,
        ),
        lax.psum_scatter(
            crossing_token_rows(normed_a, grad_vpre),
            (EXPERT, FSDP),
            scatter_dimension=0,
            tiled=True,
        ),
        lax.psum_scatter(grad_wout, (EXPERT, FSDP), scatter_dimension=0, tiled=True),
        lax.psum_scatter(
            jnp.sum(grad_qpre.astype(jnp.float32), axis=0),
            (EXPERT, FSDP),
            scatter_dimension=0,
            tiled=True,
        ),
        lax.psum_scatter(
            jnp.sum(grad_kpre.astype(jnp.float32), axis=0),
            (EXPERT, FSDP),
            scatter_dimension=0,
            tiled=True,
        ),
        lax.psum_scatter(
            jnp.sum(grad_vpre.astype(jnp.float32), axis=0),
            (EXPERT, FSDP),
            scatter_dimension=0,
            tiled=True,
        ),
        lax.psum_scatter(grad_gain_a, (EXPERT, FSDP), scatter_dimension=0, tiled=True),
        lax.psum_scatter(grad_gain_f, (EXPERT, FSDP), scatter_dimension=0, tiled=True),
        lax.psum_scatter(grad_router_all, (EXPERT, FSDP), scatter_dimension=0, tiled=True),
        lax.psum_scatter(grad_sscale, (EXPERT, FSDP), scatter_dimension=0, tiled=True),
    )
    return (
        output,
        grad_states,
        grad_wq_own,
        grad_wk_own,
        grad_wv_own,
        grad_wo_own,
        grad_bq_own,
        grad_bk_own,
        grad_bv_own,
        grad_ga_own,
        grad_gf_own,
        grad_router_own,
        grad_sgate_own,
        grad_sup_own,
        grad_sdown_own,
        grad_sscale_own,
        grad_egate_w[None],
        expert_up_weight_gradient[None],
        grad_edown[None],
    )


def place():
    f = lax.axis_index(FSDP)
    return (f, f // 4, (f // 2) % 2, f % 2, f + 2 - 4 * ((f // 2) % 2), f + 1 - 2 * (f % 2))


def at_unit(target):
    return {FSDP: target}


def greet(f, z, fx, fc, steps, across):
    barrier = pltpu.get_barrier_semaphore()

    def hello(target):
        pl.semaphore_signal(barrier, inc=1, device_id=at_unit(target))

    hello(fx)
    hello(fc)
    pl.when(z > 0)(lambda: hello(f - 4))
    pl.when(z < steps - 1)(lambda: hello(f + 4))
    count = 2 + jnp.where(z > 0, 1, 0) + jnp.where(z < steps - 1, 1, 0)
    if across:
        other = 1 - lax.axis_index(EXPERT)
        pl.semaphore_signal(barrier, inc=1, device_id={EXPERT: other})
        count += 1
    pl.semaphore_wait(barrier, count)


def swap_copy(src, dst, sent, arrived):
    return pltpu.make_async_remote_copy(
        src_ref=src,
        dst_ref=dst,
        send_sem=sent,
        recv_sem=arrived,
        device_id={EXPERT: 1 - lax.axis_index(EXPERT)},
    )


def greet_all(units):
    barrier = pltpu.get_barrier_semaphore()
    e, f = lax.axis_index(EXPERT), lax.axis_index(FSDP)
    me = e * units + f

    def hello(step, carry):
        to = lax.rem(me + step, 2 * units)
        pl.semaphore_signal(
            barrier, inc=1, device_id={EXPERT: to // units, FSDP: lax.rem(to, units)}
        )
        return carry

    lax.fori_loop(1, 2 * units, hello, 0)
    pl.semaphore_wait(barrier, 2 * units - 1)


def gather_body(steps, x_ref, out_ref, up_sem, down_sem, x_sem, c_sem, z_in, x_in, c_in):
    f, z, x, c, fx, fc = place()

    def copy(src, slot, target, done, arrived):
        return pltpu.make_async_remote_copy(
            src_ref=src,
            dst_ref=out_ref.at[slot],
            send_sem=done,
            recv_sem=arrived,
            device_id=at_unit(target),
        )

    def own_slot(at):
        return f + 4 * (at - z)

    def source(k, at):
        return x_ref if k == 0 else out_ref.at[own_slot(at)]

    def up(k, at):
        return copy(source(k, at), own_slot(at), f + 4, up_sem.at[at], z_in.at[at])

    def down(k, at):
        return copy(source(k, at), own_slot(at), f - 4, down_sem.at[at], z_in.at[at])

    def side(k, at):
        return copy(source(k, at), own_slot(at), fx, x_sem.at[at], x_in.at[at])

    def pair(k, at):
        index = x * steps + at
        return copy(source(k, at), own_slot(at), fc, c_sem.at[index], c_in.at[index])

    def step(k, below):
        at = z - k if below else z + k
        if k > 0:
            up(k, at).wait_recv()
        if k == 0 or below:
            pl.when(z < steps - 1)(lambda: up(k, at).start())
        if k == 0 or not below:
            pl.when(z > 0)(lambda: down(k, at).start())
        side(k, at).start()
        pair(k, at).start()

    def relay(k, below):
        at = z - k if below else z + k
        slot = fx + 4 * (at - z)
        index = (1 - x) * steps + at
        copy(out_ref.at[slot], slot, fx, x_sem.at[at], x_in.at[at]).wait_recv()
        copy(out_ref.at[slot], slot, fc, c_sem.at[index], c_in.at[index]).start()

    def begin():
        step(0, True)
        out_ref[f] = x_ref[...]

    def finish(between=None):
        for k in range(1, steps):
            pl.when(z - k >= 0)(functools.partial(step, k, True))
            pl.when(z + k < steps)(functools.partial(step, k, False))
            if k == 1:
                relay(0, True)
                if between is not None:
                    between()
            else:
                pl.when(z - k + 1 >= 0)(functools.partial(relay, k - 1, True))
                pl.when(z + k - 1 < steps)(functools.partial(relay, k - 1, False))
        pl.when(z - steps + 1 >= 0)(functools.partial(relay, steps - 1, True))
        pl.when(z + steps - 1 < steps)(functools.partial(relay, steps - 1, False))
        for at in range(steps):
            pl.when((at <= z) & (z < steps - 1))(lambda at=at: up(1, at).wait_send())
            pl.when((at >= z) & (z > 0))(lambda at=at: down(1, at).wait_send())
            side(1, at).wait_send()
            for col in range(2):
                slot = 4 * at + 2 * col + 1 - c
                index = col * steps + at
                copy(out_ref.at[slot], slot, fc, c_sem.at[index], c_in.at[index]).wait()

    return begin, finish


def gather_sems(steps):
    dma = pltpu.SemaphoreType.DMA
    return [dma((n * steps,)) for n in (1, 1, 1, 2, 1, 1, 2)]


def gather_kernel(steps, across, *refs):
    if across:
        x_ref, y_ref, out_ref, y_out, y_sent, y_in = refs[:6]
        sems = refs[6:]
    else:
        x_ref, out_ref = refs[:2]
        sems = refs[2:]
    f, z, x, c, fx, fc = place()
    greet(f, z, fx, fc, steps, across)
    if across:
        swap_copy(y_ref, y_out, y_sent, y_in).start()
    begin, finish = gather_body(steps, x_ref, out_ref, *sems)
    begin()
    finish()
    if across:
        swap_copy(y_ref, y_out, y_sent, y_in).wait()


vmem = pl.BlockSpec(memory_space=pltpu.VMEM)
anywhere = pl.BlockSpec(memory_space=pl.ANY)
wire = pl.CostEstimate(flops=50_000_000_000, bytes_accessed=20_000_000, transcendentals=0)


def wire_params(which):
    return pltpu.CompilerParams(
        collective_id=which, has_side_effects=True, vmem_limit_bytes=60 << 20
    )


def gather_rows(value, units, which, other=None):
    rows, width = value.shape
    steps = units // 4
    out = jax.ShapeDtypeStruct((units, rows, width), value.dtype)
    across = other is not None
    return pl.pallas_call(
        functools.partial(gather_kernel, steps, across),
        out_shape=(out, jax.ShapeDtypeStruct(other.shape, other.dtype)) if across else out,
        in_specs=[vmem, anywhere] if across else [vmem],
        out_specs=(vmem, anywhere) if across else vmem,
        scratch_shapes=[pltpu.SemaphoreType.DMA] * (2 * across) + gather_sems(steps),
        compiler_params=wire_params(which),
        cost_estimate=wire,
    )(*((value, other) if across else (value,)))


swap_parts = 4


def start_kernel(
    units,
    x_ref,
    parcel_ref,
    y_ref,
    out_ref,
    got_ref,
    y_out,
    y_sent,
    y_in,
    sent,
    arrived,
    other_sent,
    other_in,
    *sems,
):
    steps = units // 4
    e, f = lax.axis_index(EXPERT), lax.axis_index(FSDP)
    me = e * units + f
    greet_all(units)
    begin, finish = gather_body(steps, x_ref, out_ref, *sems)

    swap_rows = y_ref.shape[0] // swap_parts

    def swap_part(index):
        at = pl.ds(index * swap_rows, swap_rows)
        return swap_copy(y_ref.at[at], y_out.at[at], y_sent.at[index], y_in.at[index])

    def parcel(owner, unit):
        return pltpu.make_async_remote_copy(
            src_ref=parcel_ref.at[unit],
            dst_ref=got_ref.at[owner],
            send_sem=sent.at[unit],
            recv_sem=arrived.at[lax.rem(owner, units)],
            device_id={FSDP: unit},
        )

    def across(unit, half):
        owner = half * units + unit
        return swap_copy(
            got_ref.at[owner], got_ref.at[owner], other_sent.at[unit], other_in.at[unit]
        )

    def across_own(half):
        return swap_copy(
            parcel_ref.at[f], got_ref.at[half * units + f], other_sent.at[f], other_in.at[f]
        )

    def send(step, carry):
        parcel(me, lax.rem(f + step, units)).start()
        return carry

    def wait_parcel(step, carry):
        unit = lax.rem(f + step, units)
        parcel(e * units + unit, unit).wait_recv()
        return carry

    def pass_on(step, carry):
        across(lax.rem(f + step, units), e).start()
        return carry

    def wait_sent(step, carry):
        unit = lax.rem(f + step, units)
        parcel(me, unit).wait_send()
        across(unit, e).wait_send()
        across(unit, 1 - e).wait_recv()
        return carry

    begin()
    lax.fori_loop(1, units, send, 0)
    across_own(e).start()
    for index in range(swap_parts // 2):
        swap_part(index).start()
    got_ref[me] = parcel_ref[f]

    def hand_over():
        lax.fori_loop(1, units, wait_parcel, 0)
        lax.fori_loop(1, units, pass_on, 0)
        for index in range(swap_parts // 2, swap_parts):
            swap_part(index).start()

    finish(hand_over)
    lax.fori_loop(1, units, wait_sent, 0)
    across_own(e).wait_send()
    across_own(1 - e).wait_recv()
    for index in range(swap_parts):
        swap_part(index).wait()


def start(states, parcels, other):
    rows, width = states.shape
    units = parcels.shape[0]
    dma = pltpu.SemaphoreType.DMA
    return pl.pallas_call(
        functools.partial(start_kernel, units),
        out_shape=(
            jax.ShapeDtypeStruct((units, rows, width), states.dtype),
            jax.ShapeDtypeStruct((2 * units,) + parcels.shape[1:], states.dtype),
            jax.ShapeDtypeStruct(other.shape, other.dtype),
        ),
        in_specs=[vmem, vmem, anywhere],
        out_specs=(vmem, vmem, anywhere),
        scratch_shapes=[dma((swap_parts,))] * 2 + [dma((units,))] * 4 + gather_sems(units // 4),
        compiler_params=wire_params(0),
        cost_estimate=wire,
    )(states, parcels, other)


def scatter_kernel(steps, wide_extras, across, *refs):
    refs = list(refs)
    extra = len(wide_extras)

    def take(count):
        taken = refs[:count]
        del refs[:count]
        return taken

    (p_ref,) = take(1)
    ex_refs, y_ref = take(extra), take(across)
    (out_ref,) = take(1)
    ex_outs, y_out = take(extra), take(across)
    ex_sems = [take(2) for _ in range(extra)]
    y_sems = take(2 * across)
    c_buf, x_out, x_buf, z_out, z_buf, c_sem, x_sem, z_sem, c_in, x_in, z_in = refs
    f, z, x, c, fx, fc = place()
    units = 4 * steps
    e = lax.axis_index(EXPERT)
    extras = []

    def add_extra(wide, ex_ref, ex_out, sems):
        me = e * units + f if wide else f
        count = 2 * units if wide else units

        def copy(to):
            target = {EXPERT: to // units, FSDP: lax.rem(to, units)} if wide else at_unit(to)
            return pltpu.make_async_remote_copy(
                src_ref=ex_ref.at[to],
                dst_ref=ex_out.at[me],
                send_sem=sems[0].at[to],
                recv_sem=sems[1].at[me],
                device_id=target,
            )

        def got(owner):
            return pltpu.make_async_remote_copy(
                src_ref=ex_ref.at[owner],
                dst_ref=ex_out.at[owner],
                send_sem=sems[0].at[owner],
                recv_sem=sems[1].at[owner],
                device_id=at_unit(f),
            )

        def send(step, carry):
            copy(lax.rem(me + step, count)).start()
            return carry

        def wait(step, carry):
            owner = lax.rem(me + step, count)
            copy(owner).wait_send()
            got(owner).wait_recv()
            return carry

        def begin():
            lax.fori_loop(1, count, send, 0)
            ex_out[me] = ex_ref[me]

        extras.append((begin, lambda: lax.fori_loop(1, count, wait, 0)))

    for extra in zip(wide_extras, ex_refs, ex_outs, ex_sems):
        add_extra(*extra)
    if extras:
        greet_all(units)
    else:
        greet(f, z, fx, fc, steps, across)
    if across:
        swap_copy(y_ref[0], y_out[0], *y_sems).start()

    def pair(col, at):
        return pltpu.make_async_remote_copy(
            src_ref=p_ref.at[4 * at + 2 * col + 1 - c],
            dst_ref=c_buf.at[col * steps + at],
            send_sem=c_sem.at[col * steps + at],
            recv_sem=c_in.at[col * steps + at],
            device_id=at_unit(fc),
        )

    def side(at):
        return pltpu.make_async_remote_copy(
            src_ref=x_out.at[at],
            dst_ref=x_buf.at[at],
            send_sem=x_sem.at[at],
            recv_sem=x_in.at[at],
            device_id=at_unit(fx),
        )

    def hop(at, up):
        slot = at if up else at + steps
        return pltpu.make_async_remote_copy(
            src_ref=z_out.at[at],
            dst_ref=z_buf.at[slot],
            send_sem=z_sem.at[at],
            recv_sem=z_in.at[slot],
            device_id=at_unit(f + 4 if up else f - 4),
        )

    def far(k, below):
        return z - k if below else z + k

    def each(first, last, body):
        for k in range(first, last - 1, -1):
            if k == 0:
                body(0, True)
            else:
                pl.when(z - k >= 0)(functools.partial(body, k, True))
                pl.when(z + k < steps)(functools.partial(body, k, False))

    each(steps - 1, 0, lambda k, below: pair(1 - x, far(k, below)).start())
    each(steps - 1, 0, lambda k, below: pair(x, far(k, below)).start())

    def wide(value):
        return value.astype(jnp.float32)

    def send_side(k, below):
        at = far(k, below)
        pair(1 - x, at).wait_recv()
        total = wide(p_ref[4 * at + 2 * (1 - x) + c]) + wide(c_buf[(1 - x) * steps + at])
        x_out[at] = total.astype(x_out.dtype)
        side(at).start()

    each(steps - 1, 0, send_side)
    for begin, _ in extras:
        begin()

    def send_hop(k, below):
        at = far(k, below)
        pair(x, at).wait_recv()
        side(at).wait_recv()
        up = not below

        def total():
            return (
                wide(p_ref[4 * at + 2 * x + c])
                + wide(c_buf[x * steps + at])
                + wide(x_buf[at])
            )

        def add():
            hop(at, up).wait_recv()
            z_out[at] = (total() + wide(z_buf[at if up else at + steps])).astype(z_out.dtype)

        def plain():
            z_out[at] = total().astype(z_out.dtype)

        more = z > 0 if up else z < steps - 1
        pl.when(more)(add)
        pl.when(jnp.logical_not(more))(plain)
        hop(at, up).start()

    each(steps - 1, 1, send_hop)
    pair(x, z).wait_recv()
    side(z).wait_recv()
    out_ref[...] = wide(p_ref[f]) + wide(c_buf[x * steps + z]) + wide(x_buf[z])

    def from_below():
        hop(z, True).wait_recv()
        out_ref[...] += wide(z_buf[z])

    def from_above():
        hop(z, False).wait_recv()
        out_ref[...] += wide(z_buf[z + steps])

    pl.when(z > 0)(from_below)
    pl.when(z < steps - 1)(from_above)
    for at in range(steps):
        pair(0, at).wait_send()
        pair(1, at).wait_send()
        side(at).wait_send()
        pl.when(z != at)(lambda at=at: hop(at, True).wait_send())
    for _, finish in extras:
        finish()
    if across:
        swap_copy(y_ref[0], y_out[0], *y_sems).wait()


def scatter_rows(value, which, extras=(), wide_extras=(), other=None):
    units, rows, width = value.shape
    steps = units // 4
    dma = pltpu.SemaphoreType.DMA
    across = other is not None
    passed = () if other is None else (other,)

    def buffers(count):
        return pltpu.VMEM((count, rows, width), value.dtype)

    shapes = [jax.ShapeDtypeStruct(each.shape, each.dtype) for each in (*extras, *passed)]
    places = [vmem] * (1 + len(extras)) + [anywhere] * across
    sems = [dma((each.shape[0],)) for each in extras for _ in range(2)]
    return pl.pallas_call(
        functools.partial(scatter_kernel, steps, wide_extras, across),
        out_shape=(jax.ShapeDtypeStruct((rows, width), jnp.float32), *shapes),
        in_specs=places,
        out_specs=tuple(places),
        scratch_shapes=sems
        + [dma] * (2 * across)
        + [buffers(n * steps) for n in (2, 1, 1, 1, 2)]
        + [dma((n * steps,)) for n in (2, 1, 1, 2, 1, 2)],
        compiler_params=wire_params(which),
        cost_estimate=wire,
    )(value, *extras, *passed)


def swap(value):
    return lax.ppermute(value, EXPERT, ((0, 1), (1, 0)))


def spread(value):
    return lax.all_to_all(value, FSDP, split_axis=0, concat_axis=0, tiled=True)


def low(value):
    return value.astype(jnp.bfloat16)


def full(value):
    return value.astype(jnp.float32)


def mul(left, right):
    return jnp.dot(left, right, preferred_element_type=jnp.float32)


def plane_shards(
    states,
    w_query,
    w_key,
    w_value,
    w_out,
    b_query,
    b_key,
    b_value,
    attn_gain,
    ffn_gain,
    router,
    shared_gate,
    shared_up,
    shared_down,
    shared_scale,
    expert_gate,
    expert_up,
    expert_down,
    routes,
    prefix,
    cotangent,
):
    length, width = states.shape
    units = router.shape[1]
    head_size = width // units
    part = w_query.shape[0]
    top_count = routes.shape[1]
    capacity = 4 * length * top_count // (3 * units)
    plane = units * length
    slots = units * capacity
    score_scale = head_size ** (-0.5)
    side = lax.axis_index(EXPERT)
    unit = lax.axis_index(FSDP)
    own_half = side == 0
    devices = tuple(range(2 * units))
    from_unit_a = tuple(((d % 2) * units + d // 2, d) for d in devices)
    from_unit_b = tuple(((1 - d % 2) * units + d // 2, d) for d in devices)

    vectors = jnp.concatenate(
        [
            jnp.stack([b_query, b_key, b_value, attn_gain, ffn_gain, shared_scale]),
            router.T,
        ]
    ).reshape(-1)
    count = vectors.shape[0]
    meta = jnp.concatenate([vectors, low(routes.reshape(-1)), low(prefix)])
    lines = -(-meta.shape[0] // (48 * head_size)) * 16
    meta = jnp.pad(meta, (0, lines * 3 * head_size - meta.shape[0]))
    meta = jnp.broadcast_to(meta.reshape(1, lines, -1), (units, lines, 3 * head_size))
    parcels = jnp.stack([w_query, w_key, w_value]).reshape(3, part, units, head_size)
    parcels = parcels.transpose(2, 1, 0, 3).reshape(units, part, 3 * head_size)
    eg_own, eu_own, ed_own = expert_gate[0].T, expert_up[0].T, expert_down[0]
    state_rows, parcels, eg_other = start(
        states, jnp.concatenate([parcels, meta], axis=1), eg_own
    )
    eg = (eg_own, eg_other)
    w_qkv = parcels[:, :part].reshape(width, 3 * head_size)
    wo_here = lax.ppermute(w_out, (EXPERT, FSDP), tuple((d, u) for u, d in from_unit_a))
    wo_there = lax.ppermute(w_out, (EXPERT, FSDP), tuple((d, u) for u, d in from_unit_b))
    state_rows, shared_own, ed_own, wo_here, wo_there = lax.optimization_barrier(
        (state_rows, (shared_gate, shared_up, shared_down), ed_own, wo_here, wo_there)
    )
    w_o = jnp.concatenate(
        [jnp.where(own_half, wo_here, wo_there), jnp.where(own_half, wo_there, wo_here)]
    )
    ed_other = swap(ed_own)
    meta = parcels[:, part:].reshape(2 * units, -1)
    vectors = meta[:, :count].reshape(2 * units, 6 + units, part)
    vectors = vectors.transpose(1, 0, 2).reshape(6 + units, width)
    gain_a = full(vectors[3])
    gain_f = full(vectors[4])
    small_w = jnp.concatenate([vectors[6:], vectors[5:6]])
    meta = lax.dynamic_index_in_dim(meta.reshape(2, units, -1), side, 0, keepdims=False)
    route_end = count + length * top_count
    plane_routes = meta[:, count:route_end].astype(jnp.int32).reshape(plane, top_count)
    prefixes = meta[:, route_end].astype(jnp.int32)

    hidden = shared_gate.shape[1] // units
    band = -(-2 * hidden // 128) * 128

    shared_own = jnp.stack([shared_own[0].T, shared_own[1].T, shared_own[2]])
    shared_own = shared_own.reshape(3, units, hidden, part * 2).transpose(1, 0, 2, 3)
    shared_own = spread(shared_own.reshape(units, 3 * hidden, part * 2))

    state_rows = state_rows.reshape(plane, width)
    wide = full(state_rows)
    _, unit_rows = rms_parts(wide)
    normed_a = low(unit_rows * gain_a)
    bias = lax.dynamic_index_in_dim(
        full(vectors[:3]).reshape(3, units, head_size), unit, 1, keepdims=False
    )
    pre = mul(normed_a, w_qkv) + bias.reshape(1, -1)
    cos_table, sine_table = rope_tables(length, head_size)
    cos_table, sine_table = cos_table[:, 0], sine_table[:, 0]
    pre = pre.reshape(units, length, 3 * head_size)
    queries = low(rotate(pre[..., :head_size], cos_table, sine_table))
    keys_rot = low(rotate(pre[..., head_size : 2 * head_size], cos_table, sine_table))
    values_all = low(pre[..., 2 * head_size :])
    position = jnp.arange(length, dtype=jnp.int32)
    visible = (position[None, None, :] <= position[None, :, None]) | (
        position[None, None, :] < prefixes[:, None, None]
    )
    scores = (
        jnp.einsum("btd,bsd->bts", queries, keys_rot, preferred_element_type=jnp.float32)
        * score_scale
    )
    attn_probs = jax.nn.softmax(jnp.where(visible, scores, -1e30), axis=-1)
    probs_low = low(attn_probs)
    mixed = low(
        jnp.einsum("bts,bsd->btd", probs_low, values_all, preferred_element_type=jnp.float32)
    )
    mixed = mixed.reshape(plane, head_size)
    attn_part = low(mul(mixed, w_o)).reshape(units, length, width)
    attn_part, shared_own = lax.optimization_barrier((attn_part, shared_own))
    shared_own = shared_own.transpose(1, 0, 2).reshape(3, hidden, width)
    attn_out, shared_other = scatter_rows(attn_part, 1, other=shared_own)
    middle = full(states) + attn_out

    inverse_f, unit_f = rms_parts(middle)
    normed_f = low(unit_f * gain_f)
    shared_all = jnp.concatenate(
        [
            shared_own,
            shared_other,
            jnp.zeros((3, band - 2 * hidden, width), jnp.bfloat16),
        ],
        axis=1,
    )
    s_gate, s_up, s_down = shared_all[0], shared_all[1], shared_all[2]
    normed_f, ed_other = lax.optimization_barrier((normed_f, ed_other))
    ed = (ed_own, ed_other)
    rows, eu_other = gather_rows(normed_f, units, 2, eu_own)
    eu = (eu_own, eu_other)
    rows, cot_own = lax.optimization_barrier((rows, cotangent))
    cot_rows = lax.all_gather(cot_own, FSDP, axis=0, tiled=True)
    rows = rows.reshape(plane, width)
    small = multiply_by_transpose(rows, small_w)
    logits, mix_pre = small[:, :units], small[:, units]
    unit_ids = jnp.arange(units, dtype=jnp.int32)
    route_hit = jnp.any(plane_routes[:, :, None] == unit_ids[None, None, :], axis=1)
    gates = jax.nn.softmax(jnp.where(route_hit, logits, -1e30), axis=-1)
    here = unit_ids == unit
    gate_here = jnp.sum(jnp.where(route_hit & here, gates, 0.0), axis=-1)
    gate_here = gate_here.reshape(units, length)
    hit = jnp.any(plane_routes == unit, axis=-1).reshape(units, length)
    hits = hit.astype(jnp.int32)
    place_ids = jnp.cumsum(hits, axis=1) - hits
    pick = hit[:, None, :] & (
        place_ids[:, None, :] == jnp.arange(capacity, dtype=jnp.int32)[None, :, None]
    )
    slot_gate = jnp.sum(jnp.where(pick, gate_here[:, None, :], 0.0), axis=-1).reshape(-1, 1)
    slot_of = jnp.where(hit, place_ids + capacity * unit_ids[:, None], -1).reshape(plane, 1)
    pick_back = low(slot_of == jnp.arange(slots, dtype=jnp.int32)[None, :])
    pick_low = low(pick)

    def take(value):
        return low(
            jnp.einsum(
                "spt,std->spd",
                pick_low,
                value.reshape(units, length, width),
                preferred_element_type=jnp.float32,
            )
        ).reshape(slots, width)

    shared_mix = jax.nn.sigmoid(mix_pre)[:, None]
    sgate_pre = multiply_by_transpose(rows, s_gate)
    sup_pre = multiply_by_transpose(rows, s_up)
    act_wide = jax.nn.silu(sgate_pre) * sup_pre
    act_mixed = low(shared_mix * act_wide)
    expert_rows = take(rows)
    gate_pre = [multiply_by_transpose(expert_rows, w) for w in eg]
    up_pre = [multiply_by_transpose(expert_rows, w) for w in eu]
    expert_act = [low(jax.nn.silu(g) * u) for g, u in zip(gate_pre, up_pre)]
    expert_y = mul(expert_act[0], ed[0]) + mul(expert_act[1], ed[1])
    ffn_part = low(
        mul(
            jnp.concatenate([act_mixed, pick_back], axis=1),
            jnp.concatenate([s_down, low(slot_gate * expert_y)]),
        )
    )
    ffn_part, cot_rows = lax.optimization_barrier((ffn_part, cot_rows))
    ffn_out = lax.psum_scatter(ffn_part, FSDP, scatter_dimension=0, tiled=True)

    cot_slots = take(cot_rows)
    pulls = [multiply_by_transpose(cot_slots, w) for w in ed]
    gate_sum = sum(jnp.sum(full(a) * p, axis=-1) for a, p in zip(expert_act, pulls))
    gate_sum = gate_sum.reshape(units, capacity)
    gate_sum = jnp.sum(jnp.where(pick, gate_sum[:, :, None], 0.0), axis=1)
    pulls = [slot_gate * p for p in pulls]
    grad_eg = [low(p * u * silu_slope(g)) for p, u, g in zip(pulls, up_pre, gate_pre)]
    grad_eu = [low(p * jax.nn.silu(g)) for p, g in zip(pulls, gate_pre)]
    act_gated = [low(slot_gate * full(a)) for a in expert_act]
    swapped = (
        low(crossing_token_rows(act_gated[1], cot_slots)),
        low(crossing_token_rows(grad_eg[1], expert_rows)),
        low(crossing_token_rows(grad_eu[1], expert_rows)),
    )
    cot_rows, swapped = lax.optimization_barrier((cot_rows, swapped))
    ed_low, egw_low, euw_low = swapped
    ed_back = swap(ed_low)
    pull = multiply_by_transpose(cot_rows, s_down)
    mix_sum = jnp.sum(act_wide * pull, axis=-1)
    pull = shared_mix * pull
    grad_sgate = low(pull * sup_pre * silu_slope(sgate_pre))
    grad_sup = low(pull * jax.nn.silu(sgate_pre))
    rowin = sum(mul(g, w) for g, w in zip(grad_eg + grad_eu, eg + eu))
    rows_part = low(
        mul(
            jnp.concatenate([grad_sgate, grad_sup, pick_back], axis=1),
            jnp.concatenate([s_gate, s_up, low(rowin)]),
        )
    )
    grad_shared = jnp.stack(
        [
            crossing_token_rows(grad_sgate, rows),
            crossing_token_rows(grad_sup, rows),
            crossing_token_rows(act_mixed, cot_rows),
        ]
    )
    shared_mine = grad_shared[:, :hidden]
    shared_low = low(grad_shared[:, hidden : 2 * hidden])
    rows_part, ed_back, ffn_out = lax.optimization_barrier((rows_part, ed_back, ffn_out))
    scalars = jnp.stack([mix_sum.reshape(units, length), gate_sum], axis=1)
    lanes = -(-length // 128) * 128
    scalars = jnp.pad(scalars, ((0, 0), (0, 6), (0, lanes - length)))
    back, scalars, shared_back = scatter_rows(
        rows_part.reshape(units, length, width), 3, (scalars,), (False,), shared_low
    )
    shared_sum = low(shared_mine + full(shared_back))
    shared_sum = shared_sum.reshape(3 * hidden, units, part * 2).transpose(1, 0, 2)

    grad_out = full(cotangent)
    own_small = multiply_by_transpose(normed_f, small_w)
    own_mix = jax.nn.sigmoid(own_small[:, units])
    own_hit = jnp.any(routes[:, :, None] == unit_ids[None, None, :], axis=1)
    own_gates = jax.nn.softmax(jnp.where(own_hit, own_small[:, :units], -1e30), axis=-1)
    own_gates = jnp.where(own_hit, own_gates, 0.0)
    mix_total = jnp.sum(scalars[:, 0, :length], axis=0)
    grad_mix = low(own_mix * (1.0 - own_mix) * mix_total)
    grad_gate = scalars[:, 1, :length].T
    grad_logits = low(
        own_gates * (grad_gate - jnp.sum(own_gates * grad_gate, axis=-1, keepdims=True))
    )
    grad_small = jnp.concatenate([grad_logits, grad_mix[:, None]], axis=1)
    grad_small_w = crossing_token_rows(grad_small, normed_f)
    grad_norm_f = back + mul(grad_small, small_w)
    grad_from_f, grad_gain_f = norm_back(grad_norm_f, unit_f, inverse_f, gain_f)
    grad_mid = grad_out + grad_from_f

    output = low(middle + full(ffn_out))
    grad_attn, egw_back = gather_rows(low(grad_mid), units, 4, egw_low)
    grad_attn, shared_sum, euw_low = lax.optimization_barrier((grad_attn, shared_sum, euw_low))
    euw_back = swap(euw_low)
    shared_sum = spread(shared_sum)
    grad_attn = grad_attn.reshape(plane, width)
    grad_wo = crossing_token_rows(mixed, grad_attn)
    grad_mixed = low(multiply_by_transpose(grad_attn, w_o)).reshape(units, length, head_size)
    grad_probs = jnp.einsum(
        "btd,bsd->bts", grad_mixed, values_all, preferred_element_type=jnp.float32
    )
    row_inner = jnp.sum(attn_probs * grad_probs, axis=-1, keepdims=True)
    grad_scores = low(attn_probs * (grad_probs - row_inner))
    grad_q = (
        jnp.einsum("bts,bsd->btd", grad_scores, keys_rot, preferred_element_type=jnp.float32)
        * score_scale
    )
    grad_k = (
        jnp.einsum("bts,btd->bsd", grad_scores, queries, preferred_element_type=jnp.float32)
        * score_scale
    )
    grad_v = jnp.einsum(
        "bts,btd->bsd", probs_low, grad_mixed, preferred_element_type=jnp.float32
    )
    grad_pre = jnp.concatenate(
        [
            low(unrotate(grad_q, cos_table, sine_table)),
            low(unrotate(grad_k, cos_table, sine_table)),
            low(grad_v),
        ],
        axis=-1,
    ).reshape(plane, 3 * head_size)
    grad_qkv = crossing_token_rows(normed_a, grad_pre)
    grad_gain_a = jnp.sum(grad_qkv * full(w_qkv), axis=1) / gain_a
    grad_bias = jnp.sum(full(grad_pre), axis=0).reshape(3, head_size // part, part)
    norm_part = low(multiply_by_transpose(grad_pre, w_qkv)).reshape(units, length, width)

    grad_qkv = grad_qkv.reshape(2, units * part, 3 * head_size)
    qkv_mine = jnp.where(own_half, grad_qkv[0], grad_qkv[1])
    qkv_back = swap(low(jnp.where(own_half, grad_qkv[1], grad_qkv[0])))
    qkv_sum = low(qkv_mine + full(qkv_back)).reshape(units, part, 3 * head_size)
    norm_part, shared_sum, qkv_sum = lax.optimization_barrier(
        (norm_part, shared_sum, qkv_sum)
    )
    owners = jnp.arange(2 * units, dtype=jnp.int32)
    bias_rows = jnp.where(
        (owners // 2 == unit)[None, :, None], jnp.tile(grad_bias, (1, units, 1)), 0.0
    )
    tiny = jnp.concatenate([grad_small_w, grad_gain_a[None], grad_gain_f[None]])
    tiny = jnp.concatenate([tiny.reshape(units + 3, 2 * units, part), bias_rows])
    tiny_rows = tiny.shape[0]
    tiny_high = lax.reduce_precision(tiny, 8, 7)
    tiny = low(jnp.stack([tiny_high, tiny - tiny_high])).transpose(2, 0, 1, 3)
    tiny = tiny.reshape(2 * units, -1)
    tiny_count = tiny.shape[1]
    lines = -(-tiny_count // 4096) * 16
    tiny = jnp.pad(tiny, ((0, 0), (0, lines * 256 - tiny_count)))
    grad_norm_a, tiny, qkv_sum = scatter_rows(
        norm_part, 5, (tiny.reshape(2 * units, lines, 256), qkv_sum), (True, False)
    )
    tiny = full(tiny.reshape(2 * units, -1)[:, :tiny_count])
    tiny = jnp.sum(tiny.reshape(4 * units, tiny_rows, part), axis=0)
    grad_norm_a, act_gated, grad_eu, euw_back = lax.optimization_barrier(
        (grad_norm_a, act_gated, grad_eu, euw_back)
    )

    inverse_a, unit_a = rms_parts(full(states))
    grad_from_a, _ = norm_back(grad_norm_a, unit_a, inverse_a, gain_a)
    grad_states = grad_mid + grad_from_a

    grad_qkv = full(qkv_sum)
    grad_qkv = grad_qkv.reshape(units, part, 3, head_size).transpose(2, 1, 0, 3)
    grad_qkv = grad_qkv.reshape(3, part, width)

    blocks = grad_wo.reshape(2, part, width)
    grad_wo_own = lax.ppermute(
        jnp.where(own_half, blocks[0], blocks[1]), (EXPERT, FSDP), from_unit_a
    ) + lax.ppermute(
        jnp.where(own_half, blocks[1], blocks[0]), (EXPERT, FSDP), from_unit_b
    )

    grad_egw = crossing_token_rows(grad_eg[0], expert_rows) + full(egw_back)
    grad_euw = crossing_token_rows(grad_eu[0], expert_rows) + full(euw_back)
    grad_ed = crossing_token_rows(act_gated[0], cot_slots) + full(ed_back)

    shared_sum = full(shared_sum).reshape(units, 3, hidden, part * 2)
    shared_sum = shared_sum.transpose(1, 0, 2, 3).reshape(3, units * hidden, part * 2)

    return (
        output,
        grad_states,
        grad_qkv[0],
        grad_qkv[1],
        grad_qkv[2],
        grad_wo_own,
        tiny[units + 3],
        tiny[units + 4],
        tiny[units + 5],
        tiny[units + 1],
        tiny[units + 2],
        tiny[:units].T,
        shared_sum[0].T,
        shared_sum[1].T,
        shared_sum[2],
        tiny[units],
        grad_egw.T[None],
        grad_euw.T[None],
        grad_ed[None],
    )


def solution(mesh):
    placed = (
        P((EXPERT, FSDP), None),
        P((EXPERT, FSDP), None),
        P((EXPERT, FSDP), None),
        P((EXPERT, FSDP), None),
        P((EXPERT, FSDP), None),
        P((EXPERT, FSDP)),
        P((EXPERT, FSDP)),
        P((EXPERT, FSDP)),
        P((EXPERT, FSDP)),
        P((EXPERT, FSDP)),
        P((EXPERT, FSDP), None),
        P(FSDP, EXPERT),
        P(FSDP, EXPERT),
        P(EXPERT, FSDP),
        P((EXPERT, FSDP)),
        P(FSDP, None, EXPERT),
        P(FSDP, None, EXPERT),
        P(FSDP, EXPERT, None),
        P((EXPERT, FSDP), None),
        P((EXPERT, FSDP)),
        P((EXPERT, FSDP), None),
    )
    fits = mesh.shape[FSDP] == H == 16 and mesh.shape[EXPERT] == 2
    return jax.shard_map(
        plane_shards if fits else shards,
        mesh=mesh,
        in_specs=placed,
        out_specs=(
            P((EXPERT, FSDP), None),
            P((EXPERT, FSDP), None),
            P((EXPERT, FSDP), None),
            P((EXPERT, FSDP), None),
            P((EXPERT, FSDP), None),
            P((EXPERT, FSDP), None),
            P((EXPERT, FSDP)),
            P((EXPERT, FSDP)),
            P((EXPERT, FSDP)),
            P((EXPERT, FSDP)),
            P((EXPERT, FSDP)),
            P((EXPERT, FSDP), None),
            P(FSDP, EXPERT),
            P(FSDP, EXPERT),
            P(EXPERT, FSDP),
            P((EXPERT, FSDP)),
            P(FSDP, None, EXPERT),
            P(FSDP, None, EXPERT),
            P(FSDP, EXPERT, None),
        ),
        check_vma=False,
    )
```

```python
import functools

import jax
import jax.numpy as jnp
from jax import lax
from jax.experimental import pallas as pl
from jax.experimental.pallas import tpu as pltpu
from jax.sharding import PartitionSpec as P

H = 16
EXPERT, FSDP = "expert", "fsdp"


norm_eps = 1e-06
rope_base = 1000000.0


def rope_tables(length, head_size):
    position = jnp.arange(length, dtype=jnp.float32)
    freqs = rope_base ** (-jnp.arange(0, head_size, 2, dtype=jnp.float32) / head_size)
    angles = position[:, None] * freqs[None, :]
    angles = jnp.concatenate([angles, angles], axis=-1)
    return (jnp.cos(angles)[:, None, :], jnp.sin(angles)[:, None, :])


def rotate(values, cos_table, sine_table):
    half_size = values.shape[-1] // 2
    turned = jnp.concatenate([-values[..., half_size:], values[..., :half_size]], axis=-1)
    return values * cos_table + turned * sine_table


def unrotate(values, cos_table, sine_table):
    half_size = values.shape[-1] // 2
    moved = values * sine_table
    turned = jnp.concatenate([moved[..., half_size:], -moved[..., :half_size]], axis=-1)
    return values * cos_table + turned


def slot_tables(route_rows, expert_count, capacity):
    flat_ids = route_rows.reshape(-1)
    hit_table = (flat_ids[:, None] == jnp.arange(expert_count, dtype=jnp.int32)[None, :]).astype(
        jnp.int32
    )
    before = jnp.cumsum(hit_table, axis=0) - hit_table
    place_ids = jnp.sum(before * hit_table, axis=1)
    slot_ids = flat_ids * capacity + place_ids
    match_table = (
        slot_ids[None, :] == jnp.arange(expert_count * capacity, dtype=jnp.int32)[:, None]
    ).astype(jnp.int32)
    slot_owner = jnp.sum(
        match_table * jnp.arange(flat_ids.shape[0], dtype=jnp.int32)[None, :], axis=1
    )
    filled = jnp.sum(match_table, axis=1)
    return (slot_ids, slot_owner, filled)


def crossing_token_rows(left, right):
    return lax.dot_general(
        left, right, (((0,), (0,)), ((), ())), preferred_element_type=jnp.float32
    )


def multiply_by_transpose(left, right):
    return lax.dot_general(
        left, right, (((1,), (1,)), ((), ())), preferred_element_type=jnp.float32
    )


def rms_parts(values):
    inverse = lax.rsqrt(jnp.mean(values * values, axis=-1, keepdims=True) + norm_eps)
    return (inverse, values * inverse)


def norm_back(grad_in, unit_rows, inverse, gain_full):
    scaled = grad_in * gain_full
    grad_rows = inverse * (
        scaled - unit_rows * jnp.mean(scaled * unit_rows, axis=-1, keepdims=True)
    )
    return (grad_rows, jnp.sum(grad_in * unit_rows, axis=0))


def silu_slope(values):
    sigma = jax.nn.sigmoid(values)
    return sigma * (1.0 + values * (1.0 - sigma))


def shards(
    states,
    w_query,
    w_key,
    w_value,
    w_out,
    b_query,
    b_key,
    b_value,
    attn_gain,
    ffn_gain,
    router,
    shared_gate,
    shared_up,
    shared_down,
    shared_scale,
    expert_gate,
    expert_up,
    expert_down,
    routes,
    prefix,
    cotangent,
):
    length = states.shape[0]
    model_width = states.shape[1]
    head_count = H
    head_size = model_width // head_count
    expert_count = router.shape[1]
    top_count = routes.shape[1]
    capacity = 4 * length * top_count // (3 * expert_count)
    score_scale = head_size ** (-0.5)
    (
        query_full,
        key_full,
        value_full,
        out_full,
        query_bias,
        key_bias,
        value_bias,
        gain_attn,
        router_full,
        sscale_full,
        gain_ffn,
    ) = (
        lax.all_gather(w_query, (EXPERT, FSDP), axis=0, tiled=True),
        lax.all_gather(w_key, (EXPERT, FSDP), axis=0, tiled=True),
        lax.all_gather(w_value, (EXPERT, FSDP), axis=0, tiled=True),
        lax.all_gather(w_out, (EXPERT, FSDP), axis=0, tiled=True),
        lax.all_gather(b_query, (EXPERT, FSDP), axis=0, tiled=True),
        lax.all_gather(b_key, (EXPERT, FSDP), axis=0, tiled=True),
        lax.all_gather(b_value, (EXPERT, FSDP), axis=0, tiled=True),
        lax.all_gather(attn_gain, (EXPERT, FSDP), axis=0, tiled=True),
        lax.all_gather(router, (EXPERT, FSDP), axis=0, tiled=True),
        lax.all_gather(shared_scale, (EXPERT, FSDP), axis=0, tiled=True),
        lax.all_gather(ffn_gain, (EXPERT, FSDP), axis=0, tiled=True),
    )
    residual = states.astype(jnp.float32)
    inverse_a, unit_a = rms_parts(residual)
    gain_a = gain_attn.astype(jnp.float32)
    normed_a = (unit_a * gain_a).astype(jnp.bfloat16)
    query_pre = jnp.dot(
        normed_a, query_full, preferred_element_type=jnp.float32
    ) + query_bias.astype(jnp.float32)
    key_pre = jnp.dot(normed_a, key_full, preferred_element_type=jnp.float32) + key_bias.astype(
        jnp.float32
    )
    value_pre = jnp.dot(
        normed_a, value_full, preferred_element_type=jnp.float32
    ) + value_bias.astype(jnp.float32)
    cos_table, sine_table = rope_tables(length, head_size)
    queries = rotate(
        query_pre.reshape(length, head_count, head_size), cos_table, sine_table
    ).astype(jnp.bfloat16)
    keys_rot = rotate(key_pre.reshape(length, head_count, head_size), cos_table, sine_table).astype(
        jnp.bfloat16
    )
    values_all = value_pre.astype(jnp.bfloat16).reshape(length, head_count, head_size)
    position = jnp.arange(length, dtype=jnp.int32)
    visible = (position[None, :] <= position[:, None]) | (position[None, :] < prefix[0])

    def masked_scores():
        scores = (
            jnp.einsum("thd,shd->hts", queries, keys_rot, preferred_element_type=jnp.float32)
            * score_scale
        )
        return jnp.where(visible[None], scores, -1e30)

    scores = masked_scores()
    top_score = jnp.max(scores, axis=-1, keepdims=True)
    log_total = top_score + jnp.log(jnp.sum(jnp.exp(scores - top_score), axis=-1, keepdims=True))
    attn_probs = jnp.exp(scores - log_total)
    probs_low = attn_probs.astype(jnp.bfloat16)
    attn_mixed = (
        jnp.einsum("hts,shd->thd", probs_low, values_all, preferred_element_type=jnp.float32)
        .reshape(length, model_width)
        .astype(jnp.bfloat16)
    )
    middle = residual + jnp.dot(attn_mixed, out_full, preferred_element_type=jnp.float32)
    sgate_rows, sup_rows, sdown_rows = (
        lax.all_gather(shared_gate, FSDP, axis=0, tiled=True),
        lax.all_gather(shared_up, FSDP, axis=0, tiled=True),
        lax.all_gather(shared_down, FSDP, axis=1, tiled=True),
    )
    inverse_f, unit_f = rms_parts(middle)
    gain_f = gain_ffn.astype(jnp.float32)
    normed_f = (unit_f * gain_f).astype(jnp.bfloat16)
    logits = jnp.dot(normed_f, router_full, preferred_element_type=jnp.float32)
    route_hit = (
        routes[:, :, None] == jnp.arange(expert_count, dtype=jnp.int32)[None, None, :]
    ).astype(jnp.float32)
    chosen = jnp.sum(route_hit * logits[:, None, :], axis=-1)
    gate_probs = jax.nn.softmax(chosen, axis=-1)
    slot_ids, slot_owner, filled = slot_tables(routes, expert_count, capacity)
    token_of = slot_owner // top_count
    slot_live = filled > 0
    outgoing = jnp.where(slot_live[:, None], normed_f[token_of], jnp.zeros((), jnp.bfloat16))
    arrived = lax.all_to_all(
        outgoing.reshape(expert_count, capacity, model_width),
        FSDP,
        split_axis=0,
        concat_axis=0,
        tiled=True,
    )
    expert_token_rows = lax.all_gather(arrived, EXPERT, axis=0, tiled=True).reshape(
        -1, model_width
    )
    gate_weight_matrix = expert_gate[0]
    up_weight_matrix = expert_up[0]
    down_w = expert_down[0]
    gate_pre = jnp.dot(expert_token_rows, gate_weight_matrix, preferred_element_type=jnp.float32)
    up_pre = jnp.dot(expert_token_rows, up_weight_matrix, preferred_element_type=jnp.float32)
    expert_act = (jax.nn.silu(gate_pre) * up_pre).astype(jnp.bfloat16)
    expert_sum = lax.psum_scatter(
        jnp.dot(expert_act, down_w, preferred_element_type=jnp.float32).astype(jnp.bfloat16),
        EXPERT,
        scatter_dimension=0,
        tiled=True,
    )
    returned = lax.all_to_all(
        expert_sum.reshape(arrived.shape), FSDP, split_axis=0, concat_axis=0, tiled=True
    )
    returned = returned.reshape(expert_count * capacity, model_width)
    picked = returned[slot_ids].reshape(length, top_count, model_width).astype(jnp.float32)
    routed = jnp.sum(gate_probs[..., None] * picked, axis=1)
    sgate_use, sup_use, sdown_use = (sgate_rows, sup_rows, sdown_rows)
    pair_rows_in = lax.all_gather(normed_f, EXPERT, axis=0, tiled=True)
    sgate_pre = jnp.dot(pair_rows_in, sgate_use, preferred_element_type=jnp.float32)
    sup_pre = jnp.dot(pair_rows_in, sup_use, preferred_element_type=jnp.float32)
    shared_act = (jax.nn.silu(sgate_pre) * sup_pre).astype(jnp.bfloat16)
    shared_out = lax.psum_scatter(
        jnp.dot(shared_act, sdown_use, preferred_element_type=jnp.float32).astype(jnp.bfloat16),
        EXPERT,
        scatter_dimension=0,
        tiled=True,
    ).astype(jnp.float32)
    mix_pre = jnp.dot(normed_f, sscale_full, preferred_element_type=jnp.float32)
    shared_mix = jax.nn.sigmoid(mix_pre)
    output = (middle + routed + shared_mix[:, None] * shared_out).astype(jnp.bfloat16)
    grad_out = cotangent.astype(jnp.float32)
    scaled_cot = (shared_mix[:, None] * grad_out).astype(jnp.bfloat16)
    grad_mix = (shared_mix * (1.0 - shared_mix) * jnp.sum(grad_out * shared_out, axis=-1)).astype(
        jnp.bfloat16
    )
    cot_rows = lax.all_gather(scaled_cot, EXPERT, axis=0, tiled=True)
    grad_sdown = crossing_token_rows(shared_act, cot_rows)
    grad_sscale = crossing_token_rows(normed_f, grad_mix)
    grad_sact = multiply_by_transpose(cot_rows, sdown_use)
    grad_sgate = (grad_sact * sup_pre * silu_slope(sgate_pre)).astype(jnp.bfloat16)
    grad_sup = (grad_sact * jax.nn.silu(sgate_pre)).astype(jnp.bfloat16)
    grad_sgate_w = crossing_token_rows(pair_rows_in, grad_sgate)
    grad_sup_w = crossing_token_rows(pair_rows_in, grad_sup)
    gate_rows = grad_sgate
    up_rows = grad_sup
    shared_in = lax.psum_scatter(
        (
            multiply_by_transpose(gate_rows, sgate_use) + multiply_by_transpose(up_rows, sup_use)
        ).astype(jnp.bfloat16),
        EXPERT,
        scatter_dimension=0,
        tiled=True,
    ).astype(jnp.float32)
    grad_sgate_own, grad_sup_own, grad_sdown_own = (
        lax.psum_scatter(grad_sgate_w, FSDP, scatter_dimension=0, tiled=True),
        lax.psum_scatter(grad_sup_w, FSDP, scatter_dimension=0, tiled=True),
        lax.psum_scatter(grad_sdown, FSDP, scatter_dimension=1, tiled=True),
    )
    grad_gate = jnp.sum(grad_out[:, None, :] * picked, axis=-1)
    grad_chosen = gate_probs * (grad_gate - jnp.sum(gate_probs * grad_gate, axis=-1, keepdims=True))
    grad_logits = jnp.sum(route_hit * grad_chosen[..., None], axis=1).astype(jnp.bfloat16)
    grad_router_all = crossing_token_rows(normed_f, grad_logits)
    grad_norm_f = shared_in + multiply_by_transpose(grad_logits, router_full)
    grad_norm_f = (
        grad_norm_f
        + grad_mix.astype(jnp.float32)[:, None] * sscale_full.astype(jnp.float32)[None, :]
    )
    gate_slot = gate_probs.reshape(-1)[slot_owner] * filled.astype(jnp.float32)
    grad_slots = (gate_slot[:, None] * grad_out[token_of]).astype(jnp.bfloat16)
    grad_arrived = lax.all_to_all(
        grad_slots.reshape(expert_count, capacity, model_width),
        FSDP,
        split_axis=0,
        concat_axis=0,
        tiled=True,
    )
    grad_y = lax.all_gather(grad_arrived, EXPERT, axis=0, tiled=True).reshape(-1, model_width)
    gate_pullback_value, up_back = (gate_pre, up_pre)
    act_back = (jax.nn.silu(gate_pullback_value) * up_back).astype(jnp.bfloat16)
    grad_edown = crossing_token_rows(act_back, grad_y)
    activation_gradient = multiply_by_transpose(grad_y, down_w)
    expert_gate_gradient = (activation_gradient * up_back * silu_slope(gate_pullback_value)).astype(
        jnp.bfloat16
    )
    expert_up_gradient = (activation_gradient * jax.nn.silu(gate_pullback_value)).astype(
        jnp.bfloat16
    )
    grad_egate_w = crossing_token_rows(expert_token_rows, expert_gate_gradient)
    expert_up_weight_gradient = crossing_token_rows(expert_token_rows, expert_up_gradient)
    gate_rows = expert_gate_gradient
    up_rows = expert_up_gradient
    grad_rowin = lax.psum_scatter(
        multiply_by_transpose(gate_rows, gate_weight_matrix)
        + multiply_by_transpose(up_rows, up_weight_matrix),
        EXPERT,
        scatter_dimension=0,
        tiled=True,
    )
    grad_back = lax.all_to_all(
        grad_rowin.astype(jnp.bfloat16).reshape(arrived.shape),
        FSDP,
        split_axis=0,
        concat_axis=0,
        tiled=True,
    )
    grad_back = grad_back.reshape(expert_count * capacity, model_width)
    grad_norm_f = grad_norm_f + jnp.sum(
        grad_back[slot_ids].reshape(length, top_count, model_width).astype(jnp.float32), axis=1
    )
    grad_from_f, grad_gain_f = norm_back(grad_norm_f, unit_f, inverse_f, gain_f)
    grad_mid = grad_out + grad_from_f
    grad_attn = grad_mid.astype(jnp.bfloat16)
    grad_wout = crossing_token_rows(attn_mixed, grad_attn)
    grad_mixed = (
        multiply_by_transpose(grad_attn, out_full)
        .astype(jnp.bfloat16)
        .reshape(length, head_count, head_size)
    )
    probs_again = jnp.exp(masked_scores() - log_total)
    probs_low_again = probs_again.astype(jnp.bfloat16)
    grad_probs = jnp.einsum(
        "thd,shd->hts", grad_mixed, values_all, preferred_element_type=jnp.float32
    )
    row_inner = jnp.sum(probs_again * grad_probs, axis=-1, keepdims=True)
    grad_scores = (probs_again * (grad_probs - row_inner)).astype(jnp.bfloat16)
    grad_q = (
        jnp.einsum("hts,shd->thd", grad_scores, keys_rot, preferred_element_type=jnp.float32)
        * score_scale
    )
    grad_k = (
        jnp.einsum("hts,thd->shd", grad_scores, queries, preferred_element_type=jnp.float32)
        * score_scale
    )
    grad_v = jnp.einsum(
        "hts,thd->shd", probs_low_again, grad_mixed, preferred_element_type=jnp.float32
    )
    grad_qpre = (
        unrotate(grad_q, cos_table, sine_table).reshape(length, model_width).astype(jnp.bfloat16)
    )
    grad_kpre = (
        unrotate(grad_k, cos_table, sine_table).reshape(length, model_width).astype(jnp.bfloat16)
    )
    grad_vpre = grad_v.reshape(length, model_width).astype(jnp.bfloat16)
    grad_norm_a = (
        multiply_by_transpose(grad_qpre, query_full)
        + multiply_by_transpose(grad_kpre, key_full)
        + multiply_by_transpose(grad_vpre, value_full)
    )
    grad_from_a, grad_gain_a = norm_back(grad_norm_a, unit_a, inverse_a, gain_a)
    grad_states = grad_mid + grad_from_a
    (
        grad_wq_own,
        grad_wk_own,
        grad_wv_own,
        grad_wo_own,
        grad_bq_own,
        grad_bk_own,
        grad_bv_own,
        grad_ga_own,
        grad_gf_own,
        grad_router_own,
        grad_sscale_own,
    ) = (
        lax.psum_scatter(
            crossing_token_rows(normed_a, grad_qpre),
            (EXPERT, FSDP),
            scatter_dimension=0,
            tiled=True,
        ),
        lax.psum_scatter(
            crossing_token_rows(normed_a, grad_kpre),
            (EXPERT, FSDP),
            scatter_dimension=0,
            tiled=True,
        ),
        lax.psum_scatter(
            crossing_token_rows(normed_a, grad_vpre),
            (EXPERT, FSDP),
            scatter_dimension=0,
            tiled=True,
        ),
        lax.psum_scatter(grad_wout, (EXPERT, FSDP), scatter_dimension=0, tiled=True),
        lax.psum_scatter(
            jnp.sum(grad_qpre.astype(jnp.float32), axis=0),
            (EXPERT, FSDP),
            scatter_dimension=0,
            tiled=True,
        ),
        lax.psum_scatter(
            jnp.sum(grad_kpre.astype(jnp.float32), axis=0),
            (EXPERT, FSDP),
            scatter_dimension=0,
            tiled=True,
        ),
        lax.psum_scatter(
            jnp.sum(grad_vpre.astype(jnp.float32), axis=0),
            (EXPERT, FSDP),
            scatter_dimension=0,
            tiled=True,
        ),
        lax.psum_scatter(grad_gain_a, (EXPERT, FSDP), scatter_dimension=0, tiled=True),
        lax.psum_scatter(grad_gain_f, (EXPERT, FSDP), scatter_dimension=0, tiled=True),
        lax.psum_scatter(grad_router_all, (EXPERT, FSDP), scatter_dimension=0, tiled=True),
        lax.psum_scatter(grad_sscale, (EXPERT, FSDP), scatter_dimension=0, tiled=True),
    )
    return (
        output,
        grad_states,
        grad_wq_own,
        grad_wk_own,
        grad_wv_own,
        grad_wo_own,
        grad_bq_own,
        grad_bk_own,
        grad_bv_own,
        grad_ga_own,
        grad_gf_own,
        grad_router_own,
        grad_sgate_own,
        grad_sup_own,
        grad_sdown_own,
        grad_sscale_own,
        grad_egate_w[None],
        expert_up_weight_gradient[None],
        grad_edown[None],
    )


def place():
    f = lax.axis_index(FSDP)
    return (f, f // 4, (f // 2) % 2, f % 2, f + 2 - 4 * ((f // 2) % 2), f + 1 - 2 * (f % 2))


def at_unit(target):
    return {FSDP: target}


def greet(f, z, fx, fc, steps, across):
    barrier = pltpu.get_barrier_semaphore()

    def hello(target):
        pl.semaphore_signal(barrier, inc=1, device_id=at_unit(target))

    hello(fx)
    hello(fc)
    pl.when(z > 0)(lambda: hello(f - 4))
    pl.when(z < steps - 1)(lambda: hello(f + 4))
    count = 2 + jnp.where(z > 0, 1, 0) + jnp.where(z < steps - 1, 1, 0)
    if across:
        other = 1 - lax.axis_index(EXPERT)
        pl.semaphore_signal(barrier, inc=1, device_id={EXPERT: other})
        count += 1
    pl.semaphore_wait(barrier, count)


def swap_copy(src, dst, sent, arrived):
    return pltpu.make_async_remote_copy(
        src_ref=src,
        dst_ref=dst,
        send_sem=sent,
        recv_sem=arrived,
        device_id={EXPERT: 1 - lax.axis_index(EXPERT)},
    )


def greet_all(units):
    barrier = pltpu.get_barrier_semaphore()
    e, f = lax.axis_index(EXPERT), lax.axis_index(FSDP)
    me = e * units + f

    def hello(step, carry):
        to = lax.rem(me + step, 2 * units)
        pl.semaphore_signal(
            barrier, inc=1, device_id={EXPERT: to // units, FSDP: lax.rem(to, units)}
        )
        return carry

    lax.fori_loop(1, 2 * units, hello, 0)
    pl.semaphore_wait(barrier, 2 * units - 1)


def gather_body(steps, x_ref, out_ref, up_sem, down_sem, x_sem, c_sem, z_in, x_in, c_in):
    f, z, x, c, fx, fc = place()

    def copy(src, slot, target, done, arrived):
        return pltpu.make_async_remote_copy(
            src_ref=src,
            dst_ref=out_ref.at[slot],
            send_sem=done,
            recv_sem=arrived,
            device_id=at_unit(target),
        )

    def own_slot(at):
        return f + 4 * (at - z)

    def source(k, at):
        return x_ref if k == 0 else out_ref.at[own_slot(at)]

    def up(k, at):
        return copy(source(k, at), own_slot(at), f + 4, up_sem.at[at], z_in.at[at])

    def down(k, at):
        return copy(source(k, at), own_slot(at), f - 4, down_sem.at[at], z_in.at[at])

    def side(k, at):
        return copy(source(k, at), own_slot(at), fx, x_sem.at[at], x_in.at[at])

    def pair(k, at):
        index = x * steps + at
        return copy(source(k, at), own_slot(at), fc, c_sem.at[index], c_in.at[index])

    def step(k, below):
        at = z - k if below else z + k
        if k > 0:
            up(k, at).wait_recv()
        if k == 0 or below:
            pl.when(z < steps - 1)(lambda: up(k, at).start())
        if k == 0 or not below:
            pl.when(z > 0)(lambda: down(k, at).start())
        side(k, at).start()
        pair(k, at).start()

    def relay(k, below):
        at = z - k if below else z + k
        slot = fx + 4 * (at - z)
        index = (1 - x) * steps + at
        copy(out_ref.at[slot], slot, fx, x_sem.at[at], x_in.at[at]).wait_recv()
        copy(out_ref.at[slot], slot, fc, c_sem.at[index], c_in.at[index]).start()

    def begin():
        step(0, True)
        out_ref[f] = x_ref[...]

    def finish(between=None):
        for k in range(1, steps):
            pl.when(z - k >= 0)(functools.partial(step, k, True))
            pl.when(z + k < steps)(functools.partial(step, k, False))
            if k == 1:
                relay(0, True)
            else:
                pl.when(z - k + 1 >= 0)(functools.partial(relay, k - 1, True))
                pl.when(z + k - 1 < steps)(functools.partial(relay, k - 1, False))
            if between is not None:
                between(k - 1)
        pl.when(z - steps + 1 >= 0)(functools.partial(relay, steps - 1, True))
        pl.when(z + steps - 1 < steps)(functools.partial(relay, steps - 1, False))
        if between is not None:
            between(steps - 1)
        for at in range(steps):
            pl.when((at <= z) & (z < steps - 1))(lambda at=at: up(1, at).wait_send())
            pl.when((at >= z) & (z > 0))(lambda at=at: down(1, at).wait_send())
            side(1, at).wait_send()
            for col in range(2):
                slot = 4 * at + 2 * col + 1 - c
                index = col * steps + at
                copy(out_ref.at[slot], slot, fc, c_sem.at[index], c_in.at[index]).wait()

    return begin, finish


def gather_sems(steps):
    dma = pltpu.SemaphoreType.DMA
    return [dma((n * steps,)) for n in (1, 1, 1, 2, 1, 1, 2)]


def gather_kernel(steps, across, *refs):
    if across:
        x_ref, y_ref, out_ref, y_out, y_sent, y_in = refs[:6]
        sems = refs[6:]
    else:
        x_ref, out_ref = refs[:2]
        sems = refs[2:]
    f, z, x, c, fx, fc = place()
    greet(f, z, fx, fc, steps, across)
    if across:
        swap_copy(y_ref, y_out, y_sent, y_in).start()
    begin, finish = gather_body(steps, x_ref, out_ref, *sems)
    begin()
    finish()
    if across:
        swap_copy(y_ref, y_out, y_sent, y_in).wait()


vmem = pl.BlockSpec(memory_space=pltpu.VMEM)
anywhere = pl.BlockSpec(memory_space=pl.ANY)
wire = pl.CostEstimate(flops=50_000_000_000, bytes_accessed=20_000_000, transcendentals=0)


def wire_params(which):
    return pltpu.CompilerParams(
        collective_id=which, has_side_effects=True, vmem_limit_bytes=60 << 20
    )


def gather_rows(value, units, which, other=None):
    rows, width = value.shape
    steps = units // 4
    out = jax.ShapeDtypeStruct((units, rows, width), value.dtype)
    across = other is not None
    return pl.pallas_call(
        functools.partial(gather_kernel, steps, across),
        out_shape=(out, jax.ShapeDtypeStruct(other.shape, other.dtype)) if across else out,
        in_specs=[vmem, anywhere] if across else [vmem],
        out_specs=(vmem, anywhere) if across else vmem,
        scratch_shapes=[pltpu.SemaphoreType.DMA] * (2 * across) + gather_sems(steps),
        compiler_params=wire_params(which),
        cost_estimate=wire,
    )(*((value, other) if across else (value,)))


swap_parts = 4


def start_kernel(
    units,
    x_ref,
    parcel_ref,
    y_ref,
    out_ref,
    got_ref,
    y_out,
    y_sent,
    y_in,
    sent,
    arrived,
    other_sent,
    other_in,
    *sems,
):
    steps = units // 4
    e, f = lax.axis_index(EXPERT), lax.axis_index(FSDP)
    me = e * units + f
    greet_all(units)
    begin, finish = gather_body(steps, x_ref, out_ref, *sems)

    swap_rows = y_ref.shape[0] // swap_parts

    def swap_part(index):
        at = pl.ds(index * swap_rows, swap_rows)
        return swap_copy(y_ref.at[at], y_out.at[at], y_sent.at[index], y_in.at[index])

    def parcel(owner, unit):
        return pltpu.make_async_remote_copy(
            src_ref=parcel_ref.at[unit],
            dst_ref=got_ref.at[owner],
            send_sem=sent.at[unit],
            recv_sem=arrived.at[lax.rem(owner, units)],
            device_id={FSDP: unit},
        )

    def across(unit, half):
        owner = half * units + unit
        return swap_copy(
            got_ref.at[owner], got_ref.at[owner], other_sent.at[unit], other_in.at[unit]
        )

    def across_own(half):
        return swap_copy(
            parcel_ref.at[f], got_ref.at[half * units + f], other_sent.at[f], other_in.at[f]
        )

    def send(step, carry):
        parcel(me, lax.rem(f + step, units)).start()
        return carry

    z = f // 4

    def hand_level(at):
        def hand(unit):
            parcel(e * units + unit, unit).wait_recv()
            across(unit, e).start()

        for j in range(4):
            unit = 4 * at + j
            pl.when(unit != f)(functools.partial(hand, unit))

    def wait_sent(step, carry):
        unit = lax.rem(f + step, units)
        parcel(me, unit).wait_send()
        across(unit, e).wait_send()
        across(unit, 1 - e).wait_recv()
        return carry

    begin()
    lax.fori_loop(1, units, send, 0)
    across_own(e).start()
    for index in range(swap_parts // 2):
        swap_part(index).start()
    got_ref[me] = parcel_ref[f]

    def hand_over(k):
        if k == 0:
            hand_level(z)
            for index in range(swap_parts // 2, swap_parts):
                swap_part(index).start()
        else:
            pl.when(z - k >= 0)(lambda: hand_level(z - k))
            pl.when(z + k < steps)(lambda: hand_level(z + k))

    finish(hand_over)
    lax.fori_loop(1, units, wait_sent, 0)
    across_own(e).wait_send()
    across_own(1 - e).wait_recv()
    for index in range(swap_parts):
        swap_part(index).wait()


def start(states, parcels, other):
    rows, width = states.shape
    units = parcels.shape[0]
    dma = pltpu.SemaphoreType.DMA
    return pl.pallas_call(
        functools.partial(start_kernel, units),
        out_shape=(
            jax.ShapeDtypeStruct((units, rows, width), states.dtype),
            jax.ShapeDtypeStruct((2 * units,) + parcels.shape[1:], states.dtype),
            jax.ShapeDtypeStruct(other.shape, other.dtype),
        ),
        in_specs=[vmem, vmem, anywhere],
        out_specs=(vmem, vmem, anywhere),
        scratch_shapes=[dma((swap_parts,))] * 2 + [dma((units,))] * 4 + gather_sems(units // 4),
        compiler_params=wire_params(0),
        cost_estimate=wire,
    )(states, parcels, other)


def scatter_kernel(steps, wide_extras, across, *refs):
    refs = list(refs)
    extra = len(wide_extras)

    def take(count):
        taken = refs[:count]
        del refs[:count]
        return taken

    (p_ref,) = take(1)
    ex_refs, y_ref = take(extra), take(across)
    (out_ref,) = take(1)
    ex_outs, y_out = take(extra), take(across)
    ex_sems = [take(2) for _ in range(extra)]
    y_sems = take(2 * across)
    c_buf, x_out, x_buf, z_out, z_buf, c_sem, x_sem, z_sem, c_in, x_in, z_in = refs
    f, z, x, c, fx, fc = place()
    units = 4 * steps
    e = lax.axis_index(EXPERT)
    extras = []

    def add_extra(wide, ex_ref, ex_out, sems):
        me = e * units + f if wide else f
        count = 2 * units if wide else units

        def copy(to):
            target = {EXPERT: to // units, FSDP: lax.rem(to, units)} if wide else at_unit(to)
            return pltpu.make_async_remote_copy(
                src_ref=ex_ref.at[to],
                dst_ref=ex_out.at[me],
                send_sem=sems[0].at[to],
                recv_sem=sems[1].at[me],
                device_id=target,
            )

        def got(owner):
            return pltpu.make_async_remote_copy(
                src_ref=ex_ref.at[owner],
                dst_ref=ex_out.at[owner],
                send_sem=sems[0].at[owner],
                recv_sem=sems[1].at[owner],
                device_id=at_unit(f),
            )

        def send(step, carry):
            copy(lax.rem(me + step, count)).start()
            return carry

        def wait(step, carry):
            owner = lax.rem(me + step, count)
            copy(owner).wait_send()
            got(owner).wait_recv()
            return carry

        def begin():
            lax.fori_loop(1, count, send, 0)
            ex_out[me] = ex_ref[me]

        extras.append((begin, lambda: lax.fori_loop(1, count, wait, 0)))

    for extra in zip(wide_extras, ex_refs, ex_outs, ex_sems):
        add_extra(*extra)
    if extras:
        greet_all(units)
    else:
        greet(f, z, fx, fc, steps, across)
    if across:
        swap_copy(y_ref[0], y_out[0], *y_sems).start()

    def pair(col, at):
        return pltpu.make_async_remote_copy(
            src_ref=p_ref.at[4 * at + 2 * col + 1 - c],
            dst_ref=c_buf.at[col * steps + at],
            send_sem=c_sem.at[col * steps + at],
            recv_sem=c_in.at[col * steps + at],
            device_id=at_unit(fc),
        )

    def side(at):
        return pltpu.make_async_remote_copy(
            src_ref=x_out.at[at],
            dst_ref=x_buf.at[at],
            send_sem=x_sem.at[at],
            recv_sem=x_in.at[at],
            device_id=at_unit(fx),
        )

    def hop(at, up):
        slot = at if up else at + steps
        return pltpu.make_async_remote_copy(
            src_ref=z_out.at[at],
            dst_ref=z_buf.at[slot],
            send_sem=z_sem.at[at],
            recv_sem=z_in.at[slot],
            device_id=at_unit(f + 4 if up else f - 4),
        )

    def far(k, below):
        return z - k if below else z + k

    def each(first, last, body):
        for k in range(first, last - 1, -1):
            if k == 0:
                body(0, True)
            else:
                pl.when(z - k >= 0)(functools.partial(body, k, True))
                pl.when(z + k < steps)(functools.partial(body, k, False))

    each(steps - 1, 0, lambda k, below: pair(1 - x, far(k, below)).start())
    each(steps - 1, 0, lambda k, below: pair(x, far(k, below)).start())

    def wide(value):
        return value.astype(jnp.float32)

    def send_side(k, below):
        at = far(k, below)
        pair(1 - x, at).wait_recv()
        total = wide(p_ref[4 * at + 2 * (1 - x) + c]) + wide(c_buf[(1 - x) * steps + at])
        x_out[at] = total.astype(x_out.dtype)
        side(at).start()

    each(steps - 1, 0, send_side)
    for begin, _ in extras:
        begin()

    def send_hop(k, below):
        at = far(k, below)
        pair(x, at).wait_recv()
        side(at).wait_recv()
        up = not below

        def total():
            return (
                wide(p_ref[4 * at + 2 * x + c])
                + wide(c_buf[x * steps + at])
                + wide(x_buf[at])
            )

        def add():
            hop(at, up).wait_recv()
            z_out[at] = (total() + wide(z_buf[at if up else at + steps])).astype(z_out.dtype)

        def plain():
            z_out[at] = total().astype(z_out.dtype)

        more = z > 0 if up else z < steps - 1
        pl.when(more)(add)
        pl.when(jnp.logical_not(more))(plain)
        hop(at, up).start()

    each(steps - 1, 1, send_hop)
    pair(x, z).wait_recv()
    side(z).wait_recv()
    out_ref[...] = wide(p_ref[f]) + wide(c_buf[x * steps + z]) + wide(x_buf[z])

    def from_below():
        hop(z, True).wait_recv()
        out_ref[...] += wide(z_buf[z])

    def from_above():
        hop(z, False).wait_recv()
        out_ref[...] += wide(z_buf[z + steps])

    pl.when(z > 0)(from_below)
    pl.when(z < steps - 1)(from_above)
    for at in range(steps):
        pair(0, at).wait_send()
        pair(1, at).wait_send()
        side(at).wait_send()
        pl.when(z != at)(lambda at=at: hop(at, True).wait_send())
    for _, finish in extras:
        finish()
    if across:
        swap_copy(y_ref[0], y_out[0], *y_sems).wait()


def scatter_rows(value, which, extras=(), wide_extras=(), other=None):
    units, rows, width = value.shape
    steps = units // 4
    dma = pltpu.SemaphoreType.DMA
    across = other is not None
    passed = () if other is None else (other,)

    def buffers(count):
        return pltpu.VMEM((count, rows, width), value.dtype)

    shapes = [jax.ShapeDtypeStruct(each.shape, each.dtype) for each in (*extras, *passed)]
    places = [vmem] * (1 + len(extras)) + [anywhere] * across
    sems = [dma((each.shape[0],)) for each in extras for _ in range(2)]
    return pl.pallas_call(
        functools.partial(scatter_kernel, steps, wide_extras, across),
        out_shape=(jax.ShapeDtypeStruct((rows, width), jnp.float32), *shapes),
        in_specs=places,
        out_specs=tuple(places),
        scratch_shapes=sems
        + [dma] * (2 * across)
        + [buffers(n * steps) for n in (2, 1, 1, 1, 2)]
        + [dma((n * steps,)) for n in (2, 1, 1, 2, 1, 2)],
        compiler_params=wire_params(which),
        cost_estimate=wire,
    )(value, *extras, *passed)


def swap(value):
    return lax.ppermute(value, EXPERT, ((0, 1), (1, 0)))


def spread(value):
    return lax.all_to_all(value, FSDP, split_axis=0, concat_axis=0, tiled=True)


def low(value):
    return value.astype(jnp.bfloat16)


def full(value):
    return value.astype(jnp.float32)


def mul(left, right):
    return jnp.dot(left, right, preferred_element_type=jnp.float32)


def plane_shards(
    states,
    w_query,
    w_key,
    w_value,
    w_out,
    b_query,
    b_key,
    b_value,
    attn_gain,
    ffn_gain,
    router,
    shared_gate,
    shared_up,
    shared_down,
    shared_scale,
    expert_gate,
    expert_up,
    expert_down,
    routes,
    prefix,
    cotangent,
):
    length, width = states.shape
    units = router.shape[1]
    head_size = width // units
    part = w_query.shape[0]
    top_count = routes.shape[1]
    capacity = 4 * length * top_count // (3 * units)
    plane = units * length
    slots = units * capacity
    score_scale = head_size ** (-0.5)
    side = lax.axis_index(EXPERT)
    unit = lax.axis_index(FSDP)
    own_half = side == 0
    devices = tuple(range(2 * units))
    from_unit_a = tuple(((d % 2) * units + d // 2, d) for d in devices)
    from_unit_b = tuple(((1 - d % 2) * units + d // 2, d) for d in devices)

    vectors = jnp.concatenate(
        [
            jnp.stack([b_query, b_key, b_value, attn_gain, ffn_gain, shared_scale]),
            router.T,
        ]
    ).reshape(-1)
    count = vectors.shape[0]
    meta = jnp.concatenate([vectors, low(routes.reshape(-1)), low(prefix)])
    lines = -(-meta.shape[0] // (48 * head_size)) * 16
    meta = jnp.pad(meta, (0, lines * 3 * head_size - meta.shape[0]))
    meta = jnp.broadcast_to(meta.reshape(1, lines, -1), (units, lines, 3 * head_size))
    parcels = jnp.stack([w_query, w_key, w_value]).reshape(3, part, units, head_size)
    parcels = parcels.transpose(2, 1, 0, 3).reshape(units, part, 3 * head_size)
    eg_own, eu_own, ed_own = expert_gate[0].T, expert_up[0].T, expert_down[0]
    state_rows, parcels, eg_other = start(
        states, jnp.concatenate([parcels, meta], axis=1), eg_own
    )
    eg = (eg_own, eg_other)
    w_qkv = parcels[:, :part].reshape(width, 3 * head_size)
    state_rows, shared_own, ed_own, wo_own = lax.optimization_barrier(
        (state_rows, (shared_gate, shared_up, shared_down), ed_own, w_out)
    )
    wo_here = lax.ppermute(wo_own, (EXPERT, FSDP), tuple((d, u) for u, d in from_unit_a))
    wo_there = lax.ppermute(wo_own, (EXPERT, FSDP), tuple((d, u) for u, d in from_unit_b))
    w_o = jnp.concatenate(
        [jnp.where(own_half, wo_here, wo_there), jnp.where(own_half, wo_there, wo_here)]
    )
    ed_other = swap(ed_own)
    meta = parcels[:, part:].reshape(2 * units, -1)
    vectors = meta[:, :count].reshape(2 * units, 6 + units, part)
    vectors = vectors.transpose(1, 0, 2).reshape(6 + units, width)
    gain_a = full(vectors[3])
    gain_f = full(vectors[4])
    small_w = jnp.concatenate([vectors[6:], vectors[5:6]])
    meta = lax.dynamic_index_in_dim(meta.reshape(2, units, -1), side, 0, keepdims=False)
    route_end = count + length * top_count
    plane_routes = meta[:, count:route_end].astype(jnp.int32).reshape(plane, top_count)
    prefixes = meta[:, route_end].astype(jnp.int32)

    hidden = shared_gate.shape[1] // units
    band = -(-2 * hidden // 128) * 128

    shared_own = jnp.stack([shared_own[0].T, shared_own[1].T, shared_own[2]])
    shared_own = shared_own.reshape(3, units, hidden, part * 2).transpose(1, 0, 2, 3)
    shared_own = spread(shared_own.reshape(units, 3 * hidden, part * 2))

    state_rows = state_rows.reshape(plane, width)
    wide = full(state_rows)
    _, unit_rows = rms_parts(wide)
    normed_a = low(unit_rows * gain_a)
    bias = lax.dynamic_index_in_dim(
        full(vectors[:3]).reshape(3, units, head_size), unit, 1, keepdims=False
    )
    pre = mul(normed_a, w_qkv) + bias.reshape(1, -1)
    cos_table, sine_table = rope_tables(length, head_size)
    cos_table, sine_table = cos_table[:, 0], sine_table[:, 0]
    pre = pre.reshape(units, length, 3 * head_size)
    queries = low(rotate(pre[..., :head_size], cos_table, sine_table))
    keys_rot = low(rotate(pre[..., head_size : 2 * head_size], cos_table, sine_table))
    values_all = low(pre[..., 2 * head_size :])
    position = jnp.arange(length, dtype=jnp.int32)
    visible = (position[None, None, :] <= position[None, :, None]) | (
        position[None, None, :] < prefixes[:, None, None]
    )
    scores = (
        jnp.einsum("btd,bsd->bts", queries, keys_rot, preferred_element_type=jnp.float32)
        * score_scale
    )
    attn_probs = jax.nn.softmax(jnp.where(visible, scores, -1e30), axis=-1)
    probs_low = low(attn_probs)
    mixed = low(
        jnp.einsum("bts,bsd->btd", probs_low, values_all, preferred_element_type=jnp.float32)
    )
    mixed = mixed.reshape(plane, head_size)
    attn_part = low(mul(mixed, w_o)).reshape(units, length, width)
    attn_part, shared_own = lax.optimization_barrier((attn_part, shared_own))
    shared_own = shared_own.transpose(1, 0, 2).reshape(3, hidden, width)
    attn_out, shared_other = scatter_rows(attn_part, 1, other=shared_own)
    middle = full(states) + attn_out

    inverse_f, unit_f = rms_parts(middle)
    normed_f = low(unit_f * gain_f)
    shared_all = jnp.concatenate(
        [
            shared_own,
            shared_other,
            jnp.zeros((3, band - 2 * hidden, width), jnp.bfloat16),
        ],
        axis=1,
    )
    s_gate, s_up, s_down = shared_all[0], shared_all[1], shared_all[2]
    normed_f, ed_other = lax.optimization_barrier((normed_f, ed_other))
    ed = (ed_own, ed_other)
    rows, eu_other = gather_rows(normed_f, units, 2, eu_own)
    eu = (eu_own, eu_other)
    rows, cot_own = lax.optimization_barrier((rows, cotangent))
    cot_rows = lax.all_gather(cot_own, FSDP, axis=0, tiled=True)
    rows = rows.reshape(plane, width)
    small = multiply_by_transpose(rows, small_w)
    logits, mix_pre = small[:, :units], small[:, units]
    unit_ids = jnp.arange(units, dtype=jnp.int32)
    route_hit = jnp.any(plane_routes[:, :, None] == unit_ids[None, None, :], axis=1)
    gates = jax.nn.softmax(jnp.where(route_hit, logits, -1e30), axis=-1)
    here = unit_ids == unit
    gate_here = jnp.sum(jnp.where(route_hit & here, gates, 0.0), axis=-1)
    gate_here = gate_here.reshape(units, length)
    hit = jnp.any(plane_routes == unit, axis=-1).reshape(units, length)
    hits = hit.astype(jnp.int32)
    place_ids = jnp.cumsum(hits, axis=1) - hits
    pick = hit[:, None, :] & (
        place_ids[:, None, :] == jnp.arange(capacity, dtype=jnp.int32)[None, :, None]
    )
    slot_gate = jnp.sum(jnp.where(pick, gate_here[:, None, :], 0.0), axis=-1).reshape(-1, 1)
    slot_of = jnp.where(hit, place_ids + capacity * unit_ids[:, None], -1).reshape(plane, 1)
    pick_back = low(slot_of == jnp.arange(slots, dtype=jnp.int32)[None, :])
    pick_low = low(pick)

    def take(value):
        return low(
            jnp.einsum(
                "spt,std->spd",
                pick_low,
                value.reshape(units, length, width),
                preferred_element_type=jnp.float32,
            )
        ).reshape(slots, width)

    shared_mix = jax.nn.sigmoid(mix_pre)[:, None]
    sgate_pre = multiply_by_transpose(rows, s_gate)
    sup_pre = multiply_by_transpose(rows, s_up)
    act_wide = jax.nn.silu(sgate_pre) * sup_pre
    act_mixed = low(shared_mix * act_wide)
    expert_rows = take(rows)
    gate_pre = [multiply_by_transpose(expert_rows, w) for w in eg]
    up_pre = [multiply_by_transpose(expert_rows, w) for w in eu]
    expert_act = [low(jax.nn.silu(g) * u) for g, u in zip(gate_pre, up_pre)]
    expert_y = mul(expert_act[0], ed[0]) + mul(expert_act[1], ed[1])
    ffn_part = low(
        mul(
            jnp.concatenate([act_mixed, pick_back], axis=1),
            jnp.concatenate([s_down, low(slot_gate * expert_y)]),
        )
    )
    ffn_part, cot_rows = lax.optimization_barrier((ffn_part, cot_rows))
    ffn_out = lax.psum_scatter(ffn_part, FSDP, scatter_dimension=0, tiled=True)

    cot_slots = take(cot_rows)
    pulls = [multiply_by_transpose(cot_slots, w) for w in ed]
    gate_sum = sum(jnp.sum(full(a) * p, axis=-1) for a, p in zip(expert_act, pulls))
    gate_sum = gate_sum.reshape(units, capacity)
    gate_sum = jnp.sum(jnp.where(pick, gate_sum[:, :, None], 0.0), axis=1)
    pulls = [slot_gate * p for p in pulls]
    grad_eg = [low(p * u * silu_slope(g)) for p, u, g in zip(pulls, up_pre, gate_pre)]
    grad_eu = [low(p * jax.nn.silu(g)) for p, g in zip(pulls, gate_pre)]
    act_gated = [low(slot_gate * full(a)) for a in expert_act]
    swapped = (
        low(crossing_token_rows(act_gated[1], cot_slots)),
        low(crossing_token_rows(grad_eg[1], expert_rows)),
        low(crossing_token_rows(grad_eu[1], expert_rows)),
    )
    cot_rows, swapped = lax.optimization_barrier((cot_rows, swapped))
    ed_low, egw_low, euw_low = swapped
    ed_back = swap(ed_low)
    pull = multiply_by_transpose(cot_rows, s_down)
    mix_sum = jnp.sum(act_wide * pull, axis=-1)
    pull = shared_mix * pull
    grad_sgate = low(pull * sup_pre * silu_slope(sgate_pre))
    grad_sup = low(pull * jax.nn.silu(sgate_pre))
    rowin = sum(mul(g, w) for g, w in zip(grad_eg + grad_eu, eg + eu))
    rows_part = low(
        mul(
            jnp.concatenate([grad_sgate, grad_sup, pick_back], axis=1),
            jnp.concatenate([s_gate, s_up, low(rowin)]),
        )
    )
    grad_shared = jnp.stack(
        [
            crossing_token_rows(grad_sgate, rows),
            crossing_token_rows(grad_sup, rows),
            crossing_token_rows(act_mixed, cot_rows),
        ]
    )
    shared_mine = grad_shared[:, :hidden]
    shared_low = low(grad_shared[:, hidden : 2 * hidden])
    rows_part, ed_back, ffn_out = lax.optimization_barrier((rows_part, ed_back, ffn_out))
    scalars = jnp.stack([mix_sum.reshape(units, length), gate_sum], axis=1)
    lanes = -(-length // 128) * 128
    scalars = jnp.pad(scalars, ((0, 0), (0, 6), (0, lanes - length)))
    back, scalars, shared_back = scatter_rows(
        rows_part.reshape(units, length, width), 3, (scalars,), (False,), shared_low
    )
    shared_sum = low(shared_mine + full(shared_back))
    shared_sum = shared_sum.reshape(3 * hidden, units, part * 2).transpose(1, 0, 2)

    grad_out = full(cotangent)
    own_small = multiply_by_transpose(normed_f, small_w)
    own_mix = jax.nn.sigmoid(own_small[:, units])
    own_hit = jnp.any(routes[:, :, None] == unit_ids[None, None, :], axis=1)
    own_gates = jax.nn.softmax(jnp.where(own_hit, own_small[:, :units], -1e30), axis=-1)
    own_gates = jnp.where(own_hit, own_gates, 0.0)
    mix_total = jnp.sum(scalars[:, 0, :length], axis=0)
    grad_mix = low(own_mix * (1.0 - own_mix) * mix_total)
    grad_gate = scalars[:, 1, :length].T
    grad_logits = low(
        own_gates * (grad_gate - jnp.sum(own_gates * grad_gate, axis=-1, keepdims=True))
    )
    grad_small = jnp.concatenate([grad_logits, grad_mix[:, None]], axis=1)
    grad_small_w = crossing_token_rows(grad_small, normed_f)
    grad_norm_f = back + mul(grad_small, small_w)
    grad_from_f, grad_gain_f = norm_back(grad_norm_f, unit_f, inverse_f, gain_f)
    grad_mid = grad_out + grad_from_f

    output = low(middle + full(ffn_out))
    grad_attn, egw_back = gather_rows(low(grad_mid), units, 4, egw_low)
    grad_attn, shared_sum, euw_low = lax.optimization_barrier((grad_attn, shared_sum, euw_low))
    euw_back = swap(euw_low)
    shared_sum = spread(shared_sum)
    grad_attn = grad_attn.reshape(plane, width)
    grad_wo = crossing_token_rows(mixed, grad_attn)
    blocks = low(grad_wo).reshape(2, part, width)
    wo_pieces = (
        lax.ppermute(jnp.where(own_half, blocks[0], blocks[1]), (EXPERT, FSDP), from_unit_a),
        lax.ppermute(jnp.where(own_half, blocks[1], blocks[0]), (EXPERT, FSDP), from_unit_b),
    )
    grad_mixed = low(multiply_by_transpose(grad_attn, w_o)).reshape(units, length, head_size)
    grad_probs = jnp.einsum(
        "btd,bsd->bts", grad_mixed, values_all, preferred_element_type=jnp.float32
    )
    row_inner = jnp.sum(attn_probs * grad_probs, axis=-1, keepdims=True)
    grad_scores = low(attn_probs * (grad_probs - row_inner))
    grad_q = (
        jnp.einsum("bts,bsd->btd", grad_scores, keys_rot, preferred_element_type=jnp.float32)
        * score_scale
    )
    grad_k = (
        jnp.einsum("bts,btd->bsd", grad_scores, queries, preferred_element_type=jnp.float32)
        * score_scale
    )
    grad_v = jnp.einsum(
        "bts,btd->bsd", probs_low, grad_mixed, preferred_element_type=jnp.float32
    )
    grad_pre = jnp.concatenate(
        [
            low(unrotate(grad_q, cos_table, sine_table)),
            low(unrotate(grad_k, cos_table, sine_table)),
            low(grad_v),
        ],
        axis=-1,
    ).reshape(plane, 3 * head_size)
    grad_qkv = crossing_token_rows(normed_a, grad_pre)
    grad_gain_a = jnp.sum(grad_qkv * full(w_qkv), axis=1) / gain_a
    grad_bias = jnp.sum(full(grad_pre), axis=0).reshape(3, head_size // part, part)
    norm_part = low(multiply_by_transpose(grad_pre, w_qkv)).reshape(units, length, width)

    grad_qkv = grad_qkv.reshape(2, units * part, 3 * head_size)
    qkv_mine = jnp.where(own_half, grad_qkv[0], grad_qkv[1])
    qkv_back = swap(low(jnp.where(own_half, grad_qkv[1], grad_qkv[0])))
    qkv_sum = low(qkv_mine + full(qkv_back)).reshape(units, part, 3 * head_size)
    norm_part, shared_sum, qkv_sum = lax.optimization_barrier(
        (norm_part, shared_sum, qkv_sum)
    )
    owners = jnp.arange(2 * units, dtype=jnp.int32)
    bias_rows = jnp.where(
        (owners // 2 == unit)[None, :, None], jnp.tile(grad_bias, (1, units, 1)), 0.0
    )
    tiny = jnp.concatenate([grad_small_w, grad_gain_a[None], grad_gain_f[None]])
    tiny = jnp.concatenate([tiny.reshape(units + 3, 2 * units, part), bias_rows])
    tiny_rows = tiny.shape[0]
    tiny_high = lax.reduce_precision(tiny, 8, 7)
    tiny = low(jnp.stack([tiny_high, tiny - tiny_high])).transpose(2, 0, 1, 3)
    tiny = tiny.reshape(2 * units, -1)
    tiny_count = tiny.shape[1]
    lines = -(-tiny_count // 4096) * 16
    tiny = jnp.pad(tiny, ((0, 0), (0, lines * 256 - tiny_count)))
    grad_norm_a, tiny, qkv_sum = scatter_rows(
        norm_part, 5, (tiny.reshape(2 * units, lines, 256), qkv_sum), (True, False)
    )
    tiny = full(tiny.reshape(2 * units, -1)[:, :tiny_count])
    tiny = jnp.sum(tiny.reshape(4 * units, tiny_rows, part), axis=0)
    grad_norm_a, act_gated, grad_eu, euw_back, wo_pieces = lax.optimization_barrier(
        (grad_norm_a, act_gated, grad_eu, euw_back, wo_pieces)
    )

    inverse_a, unit_a = rms_parts(full(states))
    grad_from_a, _ = norm_back(grad_norm_a, unit_a, inverse_a, gain_a)
    grad_states = grad_mid + grad_from_a

    grad_qkv = full(qkv_sum)
    grad_qkv = grad_qkv.reshape(units, part, 3, head_size).transpose(2, 1, 0, 3)
    grad_qkv = grad_qkv.reshape(3, part, width)

    grad_wo_own = full(wo_pieces[0]) + full(wo_pieces[1])

    grad_egw = crossing_token_rows(grad_eg[0], expert_rows) + full(egw_back)
    grad_euw = crossing_token_rows(grad_eu[0], expert_rows) + full(euw_back)
    grad_ed = crossing_token_rows(act_gated[0], cot_slots) + full(ed_back)

    shared_sum = full(shared_sum).reshape(units, 3, hidden, part * 2)
    shared_sum = shared_sum.transpose(1, 0, 2, 3).reshape(3, units * hidden, part * 2)

    return (
        output,
        grad_states,
        grad_qkv[0],
        grad_qkv[1],
        grad_qkv[2],
        grad_wo_own,
        tiny[units + 3],
        tiny[units + 4],
        tiny[units + 5],
        tiny[units + 1],
        tiny[units + 2],
        tiny[:units].T,
        shared_sum[0].T,
        shared_sum[1].T,
        shared_sum[2],
        tiny[units],
        grad_egw.T[None],
        grad_euw.T[None],
        grad_ed[None],
    )


def solution(mesh):
    placed = (
        P((EXPERT, FSDP), None),
        P((EXPERT, FSDP), None),
        P((EXPERT, FSDP), None),
        P((EXPERT, FSDP), None),
        P((EXPERT, FSDP), None),
        P((EXPERT, FSDP)),
        P((EXPERT, FSDP)),
        P((EXPERT, FSDP)),
        P((EXPERT, FSDP)),
        P((EXPERT, FSDP)),
        P((EXPERT, FSDP), None),
        P(FSDP, EXPERT),
        P(FSDP, EXPERT),
        P(EXPERT, FSDP),
        P((EXPERT, FSDP)),
        P(FSDP, None, EXPERT),
        P(FSDP, None, EXPERT),
        P(FSDP, EXPERT, None),
        P((EXPERT, FSDP), None),
        P((EXPERT, FSDP)),
        P((EXPERT, FSDP), None),
    )
    fits = mesh.shape[FSDP] == H == 16 and mesh.shape[EXPERT] == 2
    return jax.shard_map(
        plane_shards if fits else shards,
        mesh=mesh,
        in_specs=placed,
        out_specs=(
            P((EXPERT, FSDP), None),
            P((EXPERT, FSDP), None),
            P((EXPERT, FSDP), None),
            P((EXPERT, FSDP), None),
            P((EXPERT, FSDP), None),
            P((EXPERT, FSDP), None),
            P((EXPERT, FSDP)),
            P((EXPERT, FSDP)),
            P((EXPERT, FSDP)),
            P((EXPERT, FSDP)),
            P((EXPERT, FSDP)),
            P((EXPERT, FSDP), None),
            P(FSDP, EXPERT),
            P(FSDP, EXPERT),
            P(EXPERT, FSDP),
            P((EXPERT, FSDP)),
            P(FSDP, None, EXPERT),
            P(FSDP, None, EXPERT),
            P(FSDP, EXPERT, None),
        ),
        check_vma=False,
    )
```

```python
import functools

import jax
import jax.numpy as jnp
from jax import lax
from jax.experimental import pallas as pl
from jax.experimental.pallas import tpu as pltpu
from jax.sharding import PartitionSpec as P

H = 16
EXPERT, FSDP = "expert", "fsdp"


norm_eps = 1e-06
rope_base = 1000000.0


def rope_tables(length, head_size):
    position = jnp.arange(length, dtype=jnp.float32)
    freqs = rope_base ** (-jnp.arange(0, head_size, 2, dtype=jnp.float32) / head_size)
    angles = position[:, None] * freqs[None, :]
    angles = jnp.concatenate([angles, angles], axis=-1)
    return (jnp.cos(angles)[:, None, :], jnp.sin(angles)[:, None, :])


def rotate(values, cos_table, sine_table):
    half_size = values.shape[-1] // 2
    turned = jnp.concatenate([-values[..., half_size:], values[..., :half_size]], axis=-1)
    return values * cos_table + turned * sine_table


def unrotate(values, cos_table, sine_table):
    half_size = values.shape[-1] // 2
    moved = values * sine_table
    turned = jnp.concatenate([moved[..., half_size:], -moved[..., :half_size]], axis=-1)
    return values * cos_table + turned


def slot_tables(route_rows, expert_count, capacity):
    flat_ids = route_rows.reshape(-1)
    hit_table = (flat_ids[:, None] == jnp.arange(expert_count, dtype=jnp.int32)[None, :]).astype(
        jnp.int32
    )
    before = jnp.cumsum(hit_table, axis=0) - hit_table
    place_ids = jnp.sum(before * hit_table, axis=1)
    slot_ids = flat_ids * capacity + place_ids
    match_table = (
        slot_ids[None, :] == jnp.arange(expert_count * capacity, dtype=jnp.int32)[:, None]
    ).astype(jnp.int32)
    slot_owner = jnp.sum(
        match_table * jnp.arange(flat_ids.shape[0], dtype=jnp.int32)[None, :], axis=1
    )
    filled = jnp.sum(match_table, axis=1)
    return (slot_ids, slot_owner, filled)


def crossing_token_rows(left, right):
    return lax.dot_general(
        left, right, (((0,), (0,)), ((), ())), preferred_element_type=jnp.float32
    )


def multiply_by_transpose(left, right):
    return lax.dot_general(
        left, right, (((1,), (1,)), ((), ())), preferred_element_type=jnp.float32
    )


def rms_parts(values):
    inverse = lax.rsqrt(jnp.mean(values * values, axis=-1, keepdims=True) + norm_eps)
    return (inverse, values * inverse)


def norm_back(grad_in, unit_rows, inverse, gain_full):
    scaled = grad_in * gain_full
    grad_rows = inverse * (
        scaled - unit_rows * jnp.mean(scaled * unit_rows, axis=-1, keepdims=True)
    )
    return (grad_rows, jnp.sum(grad_in * unit_rows, axis=0))


def silu_slope(values):
    sigma = jax.nn.sigmoid(values)
    return sigma * (1.0 + values * (1.0 - sigma))


def shards(
    states,
    w_query,
    w_key,
    w_value,
    w_out,
    b_query,
    b_key,
    b_value,
    attn_gain,
    ffn_gain,
    router,
    shared_gate,
    shared_up,
    shared_down,
    shared_scale,
    expert_gate,
    expert_up,
    expert_down,
    routes,
    prefix,
    cotangent,
):
    length = states.shape[0]
    model_width = states.shape[1]
    head_count = H
    head_size = model_width // head_count
    expert_count = router.shape[1]
    top_count = routes.shape[1]
    capacity = 4 * length * top_count // (3 * expert_count)
    score_scale = head_size ** (-0.5)
    (
        query_full,
        key_full,
        value_full,
        out_full,
        query_bias,
        key_bias,
        value_bias,
        gain_attn,
        router_full,
        sscale_full,
        gain_ffn,
    ) = (
        lax.all_gather(w_query, (EXPERT, FSDP), axis=0, tiled=True),
        lax.all_gather(w_key, (EXPERT, FSDP), axis=0, tiled=True),
        lax.all_gather(w_value, (EXPERT, FSDP), axis=0, tiled=True),
        lax.all_gather(w_out, (EXPERT, FSDP), axis=0, tiled=True),
        lax.all_gather(b_query, (EXPERT, FSDP), axis=0, tiled=True),
        lax.all_gather(b_key, (EXPERT, FSDP), axis=0, tiled=True),
        lax.all_gather(b_value, (EXPERT, FSDP), axis=0, tiled=True),
        lax.all_gather(attn_gain, (EXPERT, FSDP), axis=0, tiled=True),
        lax.all_gather(router, (EXPERT, FSDP), axis=0, tiled=True),
        lax.all_gather(shared_scale, (EXPERT, FSDP), axis=0, tiled=True),
        lax.all_gather(ffn_gain, (EXPERT, FSDP), axis=0, tiled=True),
    )
    residual = states.astype(jnp.float32)
    inverse_a, unit_a = rms_parts(residual)
    gain_a = gain_attn.astype(jnp.float32)
    normed_a = (unit_a * gain_a).astype(jnp.bfloat16)
    query_pre = jnp.dot(
        normed_a, query_full, preferred_element_type=jnp.float32
    ) + query_bias.astype(jnp.float32)
    key_pre = jnp.dot(normed_a, key_full, preferred_element_type=jnp.float32) + key_bias.astype(
        jnp.float32
    )
    value_pre = jnp.dot(
        normed_a, value_full, preferred_element_type=jnp.float32
    ) + value_bias.astype(jnp.float32)
    cos_table, sine_table = rope_tables(length, head_size)
    queries = rotate(
        query_pre.reshape(length, head_count, head_size), cos_table, sine_table
    ).astype(jnp.bfloat16)
    keys_rot = rotate(key_pre.reshape(length, head_count, head_size), cos_table, sine_table).astype(
        jnp.bfloat16
    )
    values_all = value_pre.astype(jnp.bfloat16).reshape(length, head_count, head_size)
    position = jnp.arange(length, dtype=jnp.int32)
    visible = (position[None, :] <= position[:, None]) | (position[None, :] < prefix[0])

    def masked_scores():
        scores = (
            jnp.einsum("thd,shd->hts", queries, keys_rot, preferred_element_type=jnp.float32)
            * score_scale
        )
        return jnp.where(visible[None], scores, -1e30)

    scores = masked_scores()
    top_score = jnp.max(scores, axis=-1, keepdims=True)
    log_total = top_score + jnp.log(jnp.sum(jnp.exp(scores - top_score), axis=-1, keepdims=True))
    attn_probs = jnp.exp(scores - log_total)
    probs_low = attn_probs.astype(jnp.bfloat16)
    attn_mixed = (
        jnp.einsum("hts,shd->thd", probs_low, values_all, preferred_element_type=jnp.float32)
        .reshape(length, model_width)
        .astype(jnp.bfloat16)
    )
    middle = residual + jnp.dot(attn_mixed, out_full, preferred_element_type=jnp.float32)
    sgate_rows, sup_rows, sdown_rows = (
        lax.all_gather(shared_gate, FSDP, axis=0, tiled=True),
        lax.all_gather(shared_up, FSDP, axis=0, tiled=True),
        lax.all_gather(shared_down, FSDP, axis=1, tiled=True),
    )
    inverse_f, unit_f = rms_parts(middle)
    gain_f = gain_ffn.astype(jnp.float32)
    normed_f = (unit_f * gain_f).astype(jnp.bfloat16)
    logits = jnp.dot(normed_f, router_full, preferred_element_type=jnp.float32)
    route_hit = (
        routes[:, :, None] == jnp.arange(expert_count, dtype=jnp.int32)[None, None, :]
    ).astype(jnp.float32)
    chosen = jnp.sum(route_hit * logits[:, None, :], axis=-1)
    gate_probs = jax.nn.softmax(chosen, axis=-1)
    slot_ids, slot_owner, filled = slot_tables(routes, expert_count, capacity)
    token_of = slot_owner // top_count
    slot_live = filled > 0
    outgoing = jnp.where(slot_live[:, None], normed_f[token_of], jnp.zeros((), jnp.bfloat16))
    arrived = lax.all_to_all(
        outgoing.reshape(expert_count, capacity, model_width),
        FSDP,
        split_axis=0,
        concat_axis=0,
        tiled=True,
    )
    expert_token_rows = lax.all_gather(arrived, EXPERT, axis=0, tiled=True).reshape(
        -1, model_width
    )
    gate_weight_matrix = expert_gate[0]
    up_weight_matrix = expert_up[0]
    down_w = expert_down[0]
    gate_pre = jnp.dot(expert_token_rows, gate_weight_matrix, preferred_element_type=jnp.float32)
    up_pre = jnp.dot(expert_token_rows, up_weight_matrix, preferred_element_type=jnp.float32)
    expert_act = (jax.nn.silu(gate_pre) * up_pre).astype(jnp.bfloat16)
    expert_sum = lax.psum_scatter(
        jnp.dot(expert_act, down_w, preferred_element_type=jnp.float32).astype(jnp.bfloat16),
        EXPERT,
        scatter_dimension=0,
        tiled=True,
    )
    returned = lax.all_to_all(
        expert_sum.reshape(arrived.shape), FSDP, split_axis=0, concat_axis=0, tiled=True
    )
    returned = returned.reshape(expert_count * capacity, model_width)
    picked = returned[slot_ids].reshape(length, top_count, model_width).astype(jnp.float32)
    routed = jnp.sum(gate_probs[..., None] * picked, axis=1)
    sgate_use, sup_use, sdown_use = (sgate_rows, sup_rows, sdown_rows)
    pair_rows_in = lax.all_gather(normed_f, EXPERT, axis=0, tiled=True)
    sgate_pre = jnp.dot(pair_rows_in, sgate_use, preferred_element_type=jnp.float32)
    sup_pre = jnp.dot(pair_rows_in, sup_use, preferred_element_type=jnp.float32)
    shared_act = (jax.nn.silu(sgate_pre) * sup_pre).astype(jnp.bfloat16)
    shared_out = lax.psum_scatter(
        jnp.dot(shared_act, sdown_use, preferred_element_type=jnp.float32).astype(jnp.bfloat16),
        EXPERT,
        scatter_dimension=0,
        tiled=True,
    ).astype(jnp.float32)
    mix_pre = jnp.dot(normed_f, sscale_full, preferred_element_type=jnp.float32)
    shared_mix = jax.nn.sigmoid(mix_pre)
    output = (middle + routed + shared_mix[:, None] * shared_out).astype(jnp.bfloat16)
    grad_out = cotangent.astype(jnp.float32)
    scaled_cot = (shared_mix[:, None] * grad_out).astype(jnp.bfloat16)
    grad_mix = (shared_mix * (1.0 - shared_mix) * jnp.sum(grad_out * shared_out, axis=-1)).astype(
        jnp.bfloat16
    )
    cot_rows = lax.all_gather(scaled_cot, EXPERT, axis=0, tiled=True)
    grad_sdown = crossing_token_rows(shared_act, cot_rows)
    grad_sscale = crossing_token_rows(normed_f, grad_mix)
    grad_sact = multiply_by_transpose(cot_rows, sdown_use)
    grad_sgate = (grad_sact * sup_pre * silu_slope(sgate_pre)).astype(jnp.bfloat16)
    grad_sup = (grad_sact * jax.nn.silu(sgate_pre)).astype(jnp.bfloat16)
    grad_sgate_w = crossing_token_rows(pair_rows_in, grad_sgate)
    grad_sup_w = crossing_token_rows(pair_rows_in, grad_sup)
    gate_rows = grad_sgate
    up_rows = grad_sup
    shared_in = lax.psum_scatter(
        (
            multiply_by_transpose(gate_rows, sgate_use) + multiply_by_transpose(up_rows, sup_use)
        ).astype(jnp.bfloat16),
        EXPERT,
        scatter_dimension=0,
        tiled=True,
    ).astype(jnp.float32)
    grad_sgate_own, grad_sup_own, grad_sdown_own = (
        lax.psum_scatter(grad_sgate_w, FSDP, scatter_dimension=0, tiled=True),
        lax.psum_scatter(grad_sup_w, FSDP, scatter_dimension=0, tiled=True),
        lax.psum_scatter(grad_sdown, FSDP, scatter_dimension=1, tiled=True),
    )
    grad_gate = jnp.sum(grad_out[:, None, :] * picked, axis=-1)
    grad_chosen = gate_probs * (grad_gate - jnp.sum(gate_probs * grad_gate, axis=-1, keepdims=True))
    grad_logits = jnp.sum(route_hit * grad_chosen[..., None], axis=1).astype(jnp.bfloat16)
    grad_router_all = crossing_token_rows(normed_f, grad_logits)
    grad_norm_f = shared_in + multiply_by_transpose(grad_logits, router_full)
    grad_norm_f = (
        grad_norm_f
        + grad_mix.astype(jnp.float32)[:, None] * sscale_full.astype(jnp.float32)[None, :]
    )
    gate_slot = gate_probs.reshape(-1)[slot_owner] * filled.astype(jnp.float32)
    grad_slots = (gate_slot[:, None] * grad_out[token_of]).astype(jnp.bfloat16)
    grad_arrived = lax.all_to_all(
        grad_slots.reshape(expert_count, capacity, model_width),
        FSDP,
        split_axis=0,
        concat_axis=0,
        tiled=True,
    )
    grad_y = lax.all_gather(grad_arrived, EXPERT, axis=0, tiled=True).reshape(-1, model_width)
    gate_pullback_value, up_back = (gate_pre, up_pre)
    act_back = (jax.nn.silu(gate_pullback_value) * up_back).astype(jnp.bfloat16)
    grad_edown = crossing_token_rows(act_back, grad_y)
    activation_gradient = multiply_by_transpose(grad_y, down_w)
    expert_gate_gradient = (activation_gradient * up_back * silu_slope(gate_pullback_value)).astype(
        jnp.bfloat16
    )
    expert_up_gradient = (activation_gradient * jax.nn.silu(gate_pullback_value)).astype(
        jnp.bfloat16
    )
    grad_egate_w = crossing_token_rows(expert_token_rows, expert_gate_gradient)
    expert_up_weight_gradient = crossing_token_rows(expert_token_rows, expert_up_gradient)
    gate_rows = expert_gate_gradient
    up_rows = expert_up_gradient
    grad_rowin = lax.psum_scatter(
        multiply_by_transpose(gate_rows, gate_weight_matrix)
        + multiply_by_transpose(up_rows, up_weight_matrix),
        EXPERT,
        scatter_dimension=0,
        tiled=True,
    )
    grad_back = lax.all_to_all(
        grad_rowin.astype(jnp.bfloat16).reshape(arrived.shape),
        FSDP,
        split_axis=0,
        concat_axis=0,
        tiled=True,
    )
    grad_back = grad_back.reshape(expert_count * capacity, model_width)
    grad_norm_f = grad_norm_f + jnp.sum(
        grad_back[slot_ids].reshape(length, top_count, model_width).astype(jnp.float32), axis=1
    )
    grad_from_f, grad_gain_f = norm_back(grad_norm_f, unit_f, inverse_f, gain_f)
    grad_mid = grad_out + grad_from_f
    grad_attn = grad_mid.astype(jnp.bfloat16)
    grad_wout = crossing_token_rows(attn_mixed, grad_attn)
    grad_mixed = (
        multiply_by_transpose(grad_attn, out_full)
        .astype(jnp.bfloat16)
        .reshape(length, head_count, head_size)
    )
    probs_again = jnp.exp(masked_scores() - log_total)
    probs_low_again = probs_again.astype(jnp.bfloat16)
    grad_probs = jnp.einsum(
        "thd,shd->hts", grad_mixed, values_all, preferred_element_type=jnp.float32
    )
    row_inner = jnp.sum(probs_again * grad_probs, axis=-1, keepdims=True)
    grad_scores = (probs_again * (grad_probs - row_inner)).astype(jnp.bfloat16)
    grad_q = (
        jnp.einsum("hts,shd->thd", grad_scores, keys_rot, preferred_element_type=jnp.float32)
        * score_scale
    )
    grad_k = (
        jnp.einsum("hts,thd->shd", grad_scores, queries, preferred_element_type=jnp.float32)
        * score_scale
    )
    grad_v = jnp.einsum(
        "hts,thd->shd", probs_low_again, grad_mixed, preferred_element_type=jnp.float32
    )
    grad_qpre = (
        unrotate(grad_q, cos_table, sine_table).reshape(length, model_width).astype(jnp.bfloat16)
    )
    grad_kpre = (
        unrotate(grad_k, cos_table, sine_table).reshape(length, model_width).astype(jnp.bfloat16)
    )
    grad_vpre = grad_v.reshape(length, model_width).astype(jnp.bfloat16)
    grad_norm_a = (
        multiply_by_transpose(grad_qpre, query_full)
        + multiply_by_transpose(grad_kpre, key_full)
        + multiply_by_transpose(grad_vpre, value_full)
    )
    grad_from_a, grad_gain_a = norm_back(grad_norm_a, unit_a, inverse_a, gain_a)
    grad_states = grad_mid + grad_from_a
    (
        grad_wq_own,
        grad_wk_own,
        grad_wv_own,
        grad_wo_own,
        grad_bq_own,
        grad_bk_own,
        grad_bv_own,
        grad_ga_own,
        grad_gf_own,
        grad_router_own,
        grad_sscale_own,
    ) = (
        lax.psum_scatter(
            crossing_token_rows(normed_a, grad_qpre),
            (EXPERT, FSDP),
            scatter_dimension=0,
            tiled=True,
        ),
        lax.psum_scatter(
            crossing_token_rows(normed_a, grad_kpre),
            (EXPERT, FSDP),
            scatter_dimension=0,
            tiled=True,
        ),
        lax.psum_scatter(
            crossing_token_rows(normed_a, grad_vpre),
            (EXPERT, FSDP),
            scatter_dimension=0,
            tiled=True,
        ),
        lax.psum_scatter(grad_wout, (EXPERT, FSDP), scatter_dimension=0, tiled=True),
        lax.psum_scatter(
            jnp.sum(grad_qpre.astype(jnp.float32), axis=0),
            (EXPERT, FSDP),
            scatter_dimension=0,
            tiled=True,
        ),
        lax.psum_scatter(
            jnp.sum(grad_kpre.astype(jnp.float32), axis=0),
            (EXPERT, FSDP),
            scatter_dimension=0,
            tiled=True,
        ),
        lax.psum_scatter(
            jnp.sum(grad_vpre.astype(jnp.float32), axis=0),
            (EXPERT, FSDP),
            scatter_dimension=0,
            tiled=True,
        ),
        lax.psum_scatter(grad_gain_a, (EXPERT, FSDP), scatter_dimension=0, tiled=True),
        lax.psum_scatter(grad_gain_f, (EXPERT, FSDP), scatter_dimension=0, tiled=True),
        lax.psum_scatter(grad_router_all, (EXPERT, FSDP), scatter_dimension=0, tiled=True),
        lax.psum_scatter(grad_sscale, (EXPERT, FSDP), scatter_dimension=0, tiled=True),
    )
    return (
        output,
        grad_states,
        grad_wq_own,
        grad_wk_own,
        grad_wv_own,
        grad_wo_own,
        grad_bq_own,
        grad_bk_own,
        grad_bv_own,
        grad_ga_own,
        grad_gf_own,
        grad_router_own,
        grad_sgate_own,
        grad_sup_own,
        grad_sdown_own,
        grad_sscale_own,
        grad_egate_w[None],
        expert_up_weight_gradient[None],
        grad_edown[None],
    )


def place():
    f = lax.axis_index(FSDP)
    return (f, f // 4, (f // 2) % 2, f % 2, f + 2 - 4 * ((f // 2) % 2), f + 1 - 2 * (f % 2))


def at_unit(target):
    return {FSDP: target}


def greet(f, z, fx, fc, steps, across):
    barrier = pltpu.get_barrier_semaphore()

    def hello(target):
        pl.semaphore_signal(barrier, inc=1, device_id=at_unit(target))

    hello(fx)
    hello(fc)
    pl.when(z > 0)(lambda: hello(f - 4))
    pl.when(z < steps - 1)(lambda: hello(f + 4))
    count = 2 + jnp.where(z > 0, 1, 0) + jnp.where(z < steps - 1, 1, 0)
    if across:
        other = 1 - lax.axis_index(EXPERT)
        pl.semaphore_signal(barrier, inc=1, device_id={EXPERT: other})
        count += 1
    pl.semaphore_wait(barrier, count)


def swap_copy(src, dst, sent, arrived):
    return pltpu.make_async_remote_copy(
        src_ref=src,
        dst_ref=dst,
        send_sem=sent,
        recv_sem=arrived,
        device_id={EXPERT: 1 - lax.axis_index(EXPERT)},
    )


def greet_all(units):
    barrier = pltpu.get_barrier_semaphore()
    e, f = lax.axis_index(EXPERT), lax.axis_index(FSDP)
    me = e * units + f

    def hello(step, carry):
        to = lax.rem(me + step, 2 * units)
        pl.semaphore_signal(
            barrier, inc=1, device_id={EXPERT: to // units, FSDP: lax.rem(to, units)}
        )
        return carry

    lax.fori_loop(1, 2 * units, hello, 0)
    pl.semaphore_wait(barrier, 2 * units - 1)


def gather_body(steps, x_ref, out_ref, up_sem, down_sem, x_sem, c_sem, z_in, x_in, c_in):
    f, z, x, c, fx, fc = place()

    def copy(src, slot, target, done, arrived):
        return pltpu.make_async_remote_copy(
            src_ref=src,
            dst_ref=out_ref.at[slot],
            send_sem=done,
            recv_sem=arrived,
            device_id=at_unit(target),
        )

    def own_slot(at):
        return f + 4 * (at - z)

    def source(k, at):
        return x_ref if k == 0 else out_ref.at[own_slot(at)]

    def up(k, at):
        return copy(source(k, at), own_slot(at), f + 4, up_sem.at[at], z_in.at[at])

    def down(k, at):
        return copy(source(k, at), own_slot(at), f - 4, down_sem.at[at], z_in.at[at])

    def side(k, at):
        return copy(source(k, at), own_slot(at), fx, x_sem.at[at], x_in.at[at])

    def pair(k, at):
        index = x * steps + at
        return copy(source(k, at), own_slot(at), fc, c_sem.at[index], c_in.at[index])

    def step(k, below):
        at = z - k if below else z + k
        if k > 0:
            up(k, at).wait_recv()
        if k == 0 or below:
            pl.when(z < steps - 1)(lambda: up(k, at).start())
        if k == 0 or not below:
            pl.when(z > 0)(lambda: down(k, at).start())
        side(k, at).start()
        pair(k, at).start()

    def relay(k, below):
        at = z - k if below else z + k
        slot = fx + 4 * (at - z)
        index = (1 - x) * steps + at
        copy(out_ref.at[slot], slot, fx, x_sem.at[at], x_in.at[at]).wait_recv()
        copy(out_ref.at[slot], slot, fc, c_sem.at[index], c_in.at[index]).start()

    def begin():
        step(0, True)
        out_ref[f] = x_ref[...]

    def finish(between=None):
        for k in range(1, steps):
            pl.when(z - k >= 0)(functools.partial(step, k, True))
            pl.when(z + k < steps)(functools.partial(step, k, False))
            if k == 1:
                relay(0, True)
            else:
                pl.when(z - k + 1 >= 0)(functools.partial(relay, k - 1, True))
                pl.when(z + k - 1 < steps)(functools.partial(relay, k - 1, False))
            if between is not None:
                between(k - 1)
        pl.when(z - steps + 1 >= 0)(functools.partial(relay, steps - 1, True))
        pl.when(z + steps - 1 < steps)(functools.partial(relay, steps - 1, False))
        if between is not None:
            between(steps - 1)
        for at in range(steps):
            pl.when((at <= z) & (z < steps - 1))(lambda at=at: up(1, at).wait_send())
            pl.when((at >= z) & (z > 0))(lambda at=at: down(1, at).wait_send())
            side(1, at).wait_send()
            for col in range(2):
                slot = 4 * at + 2 * col + 1 - c
                index = col * steps + at
                copy(out_ref.at[slot], slot, fc, c_sem.at[index], c_in.at[index]).wait()

    return begin, finish


def gather_sems(steps):
    dma = pltpu.SemaphoreType.DMA
    return [dma((n * steps,)) for n in (1, 1, 1, 2, 1, 1, 2)]


def gather_kernel(steps, across, *refs):
    if across:
        x_ref, y_ref, out_ref, y_out, y_sent, y_in = refs[:6]
        sems = refs[6:]
    else:
        x_ref, out_ref = refs[:2]
        sems = refs[2:]
    f, z, x, c, fx, fc = place()
    greet(f, z, fx, fc, steps, across)
    if across:
        swap_copy(y_ref, y_out, y_sent, y_in).start()
    begin, finish = gather_body(steps, x_ref, out_ref, *sems)
    begin()
    finish()
    if across:
        swap_copy(y_ref, y_out, y_sent, y_in).wait()


vmem = pl.BlockSpec(memory_space=pltpu.VMEM)
anywhere = pl.BlockSpec(memory_space=pl.ANY)
wire = pl.CostEstimate(flops=50_000_000_000, bytes_accessed=20_000_000, transcendentals=0)


def wire_params(which):
    return pltpu.CompilerParams(
        collective_id=which, has_side_effects=True, vmem_limit_bytes=60 << 20
    )


def gather_rows(value, units, which, other=None):
    rows, width = value.shape
    steps = units // 4
    out = jax.ShapeDtypeStruct((units, rows, width), value.dtype)
    across = other is not None
    return pl.pallas_call(
        functools.partial(gather_kernel, steps, across),
        out_shape=(out, jax.ShapeDtypeStruct(other.shape, other.dtype)) if across else out,
        in_specs=[vmem, anywhere] if across else [vmem],
        out_specs=(vmem, anywhere) if across else vmem,
        scratch_shapes=[pltpu.SemaphoreType.DMA] * (2 * across) + gather_sems(steps),
        compiler_params=wire_params(which),
        cost_estimate=wire,
    )(*((value, other) if across else (value,)))


swap_parts = 4


def start_kernel(
    units,
    x_ref,
    parcel_ref,
    y_ref,
    out_ref,
    got_ref,
    y_out,
    y_sent,
    y_in,
    sent,
    arrived,
    other_sent,
    other_in,
    *sems,
):
    steps = units // 4
    e, f = lax.axis_index(EXPERT), lax.axis_index(FSDP)
    me = e * units + f
    greet_all(units)
    begin, finish = gather_body(steps, x_ref, out_ref, *sems)

    swap_rows = y_ref.shape[0] // swap_parts

    def swap_part(index):
        at = pl.ds(index * swap_rows, swap_rows)
        return swap_copy(y_ref.at[at], y_out.at[at], y_sent.at[index], y_in.at[index])

    def parcel(owner, unit):
        return pltpu.make_async_remote_copy(
            src_ref=parcel_ref.at[unit],
            dst_ref=got_ref.at[owner],
            send_sem=sent.at[unit],
            recv_sem=arrived.at[lax.rem(owner, units)],
            device_id={FSDP: unit},
        )

    def across(unit, half):
        owner = half * units + unit
        return swap_copy(
            got_ref.at[owner], got_ref.at[owner], other_sent.at[unit], other_in.at[unit]
        )

    def across_own(half):
        return swap_copy(
            parcel_ref.at[f], got_ref.at[half * units + f], other_sent.at[f], other_in.at[f]
        )

    def send(step, carry):
        parcel(me, lax.rem(f + step, units)).start()
        return carry

    z = f // 4

    def hand_level(at):
        def hand(unit):
            parcel(e * units + unit, unit).wait_recv()
            across(unit, e).start()

        for j in range(4):
            unit = 4 * at + j
            pl.when(unit != f)(functools.partial(hand, unit))

    def wait_sent(step, carry):
        unit = lax.rem(f + step, units)
        parcel(me, unit).wait_send()
        across(unit, e).wait_send()
        across(unit, 1 - e).wait_recv()
        return carry

    begin()
    lax.fori_loop(1, units, send, 0)
    across_own(e).start()
    for index in range(swap_parts // 2):
        swap_part(index).start()
    got_ref[me] = parcel_ref[f]

    def hand_over(k):
        if k == 0:
            hand_level(z)
            for index in range(swap_parts // 2, swap_parts):
                swap_part(index).start()
        else:
            pl.when(z - k >= 0)(lambda: hand_level(z - k))
            pl.when(z + k < steps)(lambda: hand_level(z + k))

    finish(hand_over)
    lax.fori_loop(1, units, wait_sent, 0)
    across_own(e).wait_send()
    across_own(1 - e).wait_recv()
    for index in range(swap_parts):
        swap_part(index).wait()


def start(states, parcels, other):
    rows, width = states.shape
    units = parcels.shape[0]
    dma = pltpu.SemaphoreType.DMA
    return pl.pallas_call(
        functools.partial(start_kernel, units),
        out_shape=(
            jax.ShapeDtypeStruct((units, rows, width), states.dtype),
            jax.ShapeDtypeStruct((2 * units,) + parcels.shape[1:], states.dtype),
            jax.ShapeDtypeStruct(other.shape, other.dtype),
        ),
        in_specs=[vmem, vmem, anywhere],
        out_specs=(vmem, vmem, anywhere),
        scratch_shapes=[dma((swap_parts,))] * 2 + [dma((units,))] * 4 + gather_sems(units // 4),
        compiler_params=wire_params(0),
        cost_estimate=wire,
    )(states, parcels, other)


def scatter_kernel(steps, wide_extras, across, *refs):
    refs = list(refs)
    extra = len(wide_extras)

    def take(count):
        taken = refs[:count]
        del refs[:count]
        return taken

    (p_ref,) = take(1)
    ex_refs, y_ref = take(extra), take(across)
    (out_ref,) = take(1)
    ex_outs, y_out = take(extra), take(across)
    ex_sems = [take(2) for _ in range(extra)]
    y_sems = take(2 * across)
    c_buf, x_out, x_buf, z_out, z_buf, c_sem, x_sem, z_sem, c_in, x_in, z_in = refs
    f, z, x, c, fx, fc = place()
    units = 4 * steps
    e = lax.axis_index(EXPERT)
    extras = []

    def add_extra(wide, ex_ref, ex_out, sems):
        me = e * units + f if wide else f
        count = 2 * units if wide else units

        def copy(to):
            target = {EXPERT: to // units, FSDP: lax.rem(to, units)} if wide else at_unit(to)
            return pltpu.make_async_remote_copy(
                src_ref=ex_ref.at[to],
                dst_ref=ex_out.at[me],
                send_sem=sems[0].at[to],
                recv_sem=sems[1].at[me],
                device_id=target,
            )

        def got(owner):
            return pltpu.make_async_remote_copy(
                src_ref=ex_ref.at[owner],
                dst_ref=ex_out.at[owner],
                send_sem=sems[0].at[owner],
                recv_sem=sems[1].at[owner],
                device_id=at_unit(f),
            )

        def send(step, carry):
            copy(lax.rem(me + step, count)).start()
            return carry

        def wait(step, carry):
            owner = lax.rem(me + step, count)
            copy(owner).wait_send()
            got(owner).wait_recv()
            return carry

        def begin():
            lax.fori_loop(1, count, send, 0)
            ex_out[me] = ex_ref[me]

        extras.append((begin, lambda: lax.fori_loop(1, count, wait, 0)))

    for extra in zip(wide_extras, ex_refs, ex_outs, ex_sems):
        add_extra(*extra)
    if extras:
        greet_all(units)
    else:
        greet(f, z, fx, fc, steps, across)
    if across:
        swap_copy(y_ref[0], y_out[0], *y_sems).start()

    def pair(col, at):
        return pltpu.make_async_remote_copy(
            src_ref=p_ref.at[4 * at + 2 * col + 1 - c],
            dst_ref=c_buf.at[col * steps + at],
            send_sem=c_sem.at[col * steps + at],
            recv_sem=c_in.at[col * steps + at],
            device_id=at_unit(fc),
        )

    def side(at):
        return pltpu.make_async_remote_copy(
            src_ref=x_out.at[at],
            dst_ref=x_buf.at[at],
            send_sem=x_sem.at[at],
            recv_sem=x_in.at[at],
            device_id=at_unit(fx),
        )

    def hop(at, up):
        slot = at if up else at + steps
        return pltpu.make_async_remote_copy(
            src_ref=z_out.at[at],
            dst_ref=z_buf.at[slot],
            send_sem=z_sem.at[at],
            recv_sem=z_in.at[slot],
            device_id=at_unit(f + 4 if up else f - 4),
        )

    def far(k, below):
        return z - k if below else z + k

    def each(first, last, body):
        for k in range(first, last - 1, -1):
            if k == 0:
                body(0, True)
            else:
                pl.when(z - k >= 0)(functools.partial(body, k, True))
                pl.when(z + k < steps)(functools.partial(body, k, False))

    each(steps - 1, 0, lambda k, below: pair(1 - x, far(k, below)).start())
    each(steps - 1, 0, lambda k, below: pair(x, far(k, below)).start())

    def wide(value):
        return value.astype(jnp.float32)

    def send_side(k, below):
        at = far(k, below)
        pair(1 - x, at).wait_recv()
        total = wide(p_ref[4 * at + 2 * (1 - x) + c]) + wide(c_buf[(1 - x) * steps + at])
        x_out[at] = total.astype(x_out.dtype)
        side(at).start()

    each(steps - 1, 0, send_side)
    for begin, _ in extras:
        begin()

    def send_hop(k, below):
        at = far(k, below)
        pair(x, at).wait_recv()
        side(at).wait_recv()
        up = not below

        def total():
            return (
                wide(p_ref[4 * at + 2 * x + c])
                + wide(c_buf[x * steps + at])
                + wide(x_buf[at])
            )

        def add():
            hop(at, up).wait_recv()
            z_out[at] = (total() + wide(z_buf[at if up else at + steps])).astype(z_out.dtype)

        def plain():
            z_out[at] = total().astype(z_out.dtype)

        more = z > 0 if up else z < steps - 1
        pl.when(more)(add)
        pl.when(jnp.logical_not(more))(plain)
        hop(at, up).start()

    each(steps - 1, 1, send_hop)
    pair(x, z).wait_recv()
    side(z).wait_recv()
    out_ref[...] = wide(p_ref[f]) + wide(c_buf[x * steps + z]) + wide(x_buf[z])

    def from_below():
        hop(z, True).wait_recv()
        out_ref[...] += wide(z_buf[z])

    def from_above():
        hop(z, False).wait_recv()
        out_ref[...] += wide(z_buf[z + steps])

    pl.when(z > 0)(from_below)
    pl.when(z < steps - 1)(from_above)
    for at in range(steps):
        pair(0, at).wait_send()
        pair(1, at).wait_send()
        side(at).wait_send()
        pl.when(z != at)(lambda at=at: hop(at, True).wait_send())
    for _, finish in extras:
        finish()
    if across:
        swap_copy(y_ref[0], y_out[0], *y_sems).wait()


def scatter_rows(value, which, extras=(), wide_extras=(), other=None):
    units, rows, width = value.shape
    steps = units // 4
    dma = pltpu.SemaphoreType.DMA
    across = other is not None
    passed = () if other is None else (other,)

    def buffers(count):
        return pltpu.VMEM((count, rows, width), value.dtype)

    shapes = [jax.ShapeDtypeStruct(each.shape, each.dtype) for each in (*extras, *passed)]
    places = [vmem] * (1 + len(extras)) + [anywhere] * across
    sems = [dma((each.shape[0],)) for each in extras for _ in range(2)]
    return pl.pallas_call(
        functools.partial(scatter_kernel, steps, wide_extras, across),
        out_shape=(jax.ShapeDtypeStruct((rows, width), jnp.float32), *shapes),
        in_specs=places,
        out_specs=tuple(places),
        scratch_shapes=sems
        + [dma] * (2 * across)
        + [buffers(n * steps) for n in (2, 1, 1, 1, 2)]
        + [dma((n * steps,)) for n in (2, 1, 1, 2, 1, 2)],
        compiler_params=wire_params(which),
        cost_estimate=wire,
    )(value, *extras, *passed)


def swap(value):
    return lax.ppermute(value, EXPERT, ((0, 1), (1, 0)))


def spread(value):
    return lax.all_to_all(value, FSDP, split_axis=0, concat_axis=0, tiled=True)


def low(value):
    return value.astype(jnp.bfloat16)


def full(value):
    return value.astype(jnp.float32)


def mul(left, right):
    return jnp.dot(left, right, preferred_element_type=jnp.float32)


def plane_shards(
    states,
    w_query,
    w_key,
    w_value,
    w_out,
    b_query,
    b_key,
    b_value,
    attn_gain,
    ffn_gain,
    router,
    shared_gate,
    shared_up,
    shared_down,
    shared_scale,
    expert_gate,
    expert_up,
    expert_down,
    routes,
    prefix,
    cotangent,
):
    length, width = states.shape
    units = router.shape[1]
    head_size = width // units
    part = w_query.shape[0]
    top_count = routes.shape[1]
    capacity = 4 * length * top_count // (3 * units)
    plane = units * length
    slots = units * capacity
    score_scale = head_size ** (-0.5)
    side = lax.axis_index(EXPERT)
    unit = lax.axis_index(FSDP)
    own_half = side == 0
    devices = tuple(range(2 * units))
    from_unit_a = tuple(((d % 2) * units + d // 2, d) for d in devices)
    from_unit_b = tuple(((1 - d % 2) * units + d // 2, d) for d in devices)

    vectors = jnp.concatenate(
        [
            jnp.stack([b_query, b_key, b_value, attn_gain, ffn_gain, shared_scale]),
            router.T,
        ]
    ).reshape(-1)
    count = vectors.shape[0]
    meta = jnp.concatenate([vectors, low(routes.reshape(-1)), low(prefix)])
    lines = -(-meta.shape[0] // (48 * head_size)) * 16
    meta = jnp.pad(meta, (0, lines * 3 * head_size - meta.shape[0]))
    meta = jnp.broadcast_to(meta.reshape(1, lines, -1), (units, lines, 3 * head_size))
    parcels = jnp.stack([w_query, w_key, w_value]).reshape(3, part, units, head_size)
    parcels = parcels.transpose(2, 1, 0, 3).reshape(units, part, 3 * head_size)
    eg_own, eu_own, ed_own = expert_gate[0].T, expert_up[0].T, expert_down[0]
    state_rows, parcels, eg_other = start(
        states, jnp.concatenate([parcels, meta], axis=1), eg_own
    )
    eg = (eg_own, eg_other)
    w_qkv = parcels[:, :part].reshape(width, 3 * head_size)
    state_rows, shared_own, ed_own, wo_own = lax.optimization_barrier(
        (state_rows, (shared_gate, shared_up, shared_down), ed_own, w_out)
    )
    wo_here = lax.ppermute(wo_own, (EXPERT, FSDP), tuple((d, u) for u, d in from_unit_a))
    wo_there = lax.ppermute(wo_own, (EXPERT, FSDP), tuple((d, u) for u, d in from_unit_b))
    w_o = jnp.concatenate(
        [jnp.where(own_half, wo_here, wo_there), jnp.where(own_half, wo_there, wo_here)]
    )
    ed_other = swap(ed_own)
    meta = parcels[:, part:].reshape(2 * units, -1)
    vectors = meta[:, :count].reshape(2 * units, 6 + units, part)
    vectors = vectors.transpose(1, 0, 2).reshape(6 + units, width)
    gain_a = full(vectors[3])
    gain_f = full(vectors[4])
    small_w = jnp.concatenate([vectors[6:], vectors[5:6]])
    meta = lax.dynamic_index_in_dim(meta.reshape(2, units, -1), side, 0, keepdims=False)
    route_end = count + length * top_count
    plane_routes = meta[:, count:route_end].astype(jnp.int32).reshape(plane, top_count)
    prefixes = meta[:, route_end].astype(jnp.int32)

    hidden = shared_gate.shape[1] // units
    band = -(-2 * hidden // 128) * 128

    shared_own = jnp.stack([shared_own[0].T, shared_own[1].T, shared_own[2]])
    shared_own = shared_own.reshape(3, units, hidden, part * 2).transpose(1, 0, 2, 3)
    shared_own = spread(shared_own.reshape(units, 3 * hidden, part * 2))

    state_rows = state_rows.reshape(plane, width)
    wide = full(state_rows)
    _, unit_rows = rms_parts(wide)
    normed_a = low(unit_rows * gain_a)
    bias = lax.dynamic_index_in_dim(
        full(vectors[:3]).reshape(3, units, head_size), unit, 1, keepdims=False
    )
    pre = mul(normed_a, w_qkv) + bias.reshape(1, -1)
    cos_table, sine_table = rope_tables(length, head_size)
    cos_table, sine_table = cos_table[:, 0], sine_table[:, 0]
    pre = pre.reshape(units, length, 3 * head_size)
    queries = low(rotate(pre[..., :head_size], cos_table, sine_table))
    keys_rot = low(rotate(pre[..., head_size : 2 * head_size], cos_table, sine_table))
    values_all = low(pre[..., 2 * head_size :])
    position = jnp.arange(length, dtype=jnp.int32)
    visible = (position[None, None, :] <= position[None, :, None]) | (
        position[None, None, :] < prefixes[:, None, None]
    )
    scores = (
        jnp.einsum("btd,bsd->bts", queries, keys_rot, preferred_element_type=jnp.float32)
        * score_scale
    )
    attn_probs = jax.nn.softmax(jnp.where(visible, scores, -1e30), axis=-1)
    probs_low = low(attn_probs)
    mixed = low(
        jnp.einsum("bts,bsd->btd", probs_low, values_all, preferred_element_type=jnp.float32)
    )
    mixed = mixed.reshape(plane, head_size)
    attn_part = low(mul(mixed, w_o)).reshape(units, length, width)
    attn_part, shared_own = lax.optimization_barrier((attn_part, shared_own))
    shared_own = shared_own.transpose(1, 0, 2).reshape(3, hidden, width)
    attn_out, shared_other = scatter_rows(attn_part, 1, other=shared_own)
    middle = full(states) + attn_out

    inverse_f, unit_f = rms_parts(middle)
    normed_f = low(unit_f * gain_f)
    shared_all = jnp.concatenate(
        [
            shared_own,
            shared_other,
            jnp.zeros((3, band - 2 * hidden, width), jnp.bfloat16),
        ],
        axis=1,
    )
    s_gate, s_up, s_down = shared_all[0], shared_all[1], shared_all[2]
    normed_f, ed_other = lax.optimization_barrier((normed_f, ed_other))
    ed = (ed_own, ed_other)
    rows, eu_other = gather_rows(normed_f, units, 2, eu_own)
    eu = (eu_own, eu_other)
    rows, cot_own = lax.optimization_barrier((rows, cotangent))
    cot_rows = lax.all_gather(cot_own, FSDP, axis=0, tiled=True)
    rows = rows.reshape(plane, width)
    small = multiply_by_transpose(rows, small_w)
    logits, mix_pre = small[:, :units], small[:, units]
    unit_ids = jnp.arange(units, dtype=jnp.int32)
    route_hit = jnp.any(plane_routes[:, :, None] == unit_ids[None, None, :], axis=1)
    gates = jax.nn.softmax(jnp.where(route_hit, logits, -1e30), axis=-1)
    here = unit_ids == unit
    gate_here = jnp.sum(jnp.where(route_hit & here, gates, 0.0), axis=-1)
    gate_here = gate_here.reshape(units, length)
    hit = jnp.any(plane_routes == unit, axis=-1).reshape(units, length)
    hits = hit.astype(jnp.int32)
    place_ids = jnp.cumsum(hits, axis=1) - hits
    pick = hit[:, None, :] & (
        place_ids[:, None, :] == jnp.arange(capacity, dtype=jnp.int32)[None, :, None]
    )
    slot_gate = jnp.sum(jnp.where(pick, gate_here[:, None, :], 0.0), axis=-1).reshape(-1, 1)
    slot_of = jnp.where(hit, place_ids + capacity * unit_ids[:, None], -1).reshape(plane, 1)
    pick_back = low(slot_of == jnp.arange(slots, dtype=jnp.int32)[None, :])
    pick_low = low(pick)

    def take(value):
        return low(
            jnp.einsum(
                "spt,std->spd",
                pick_low,
                value.reshape(units, length, width),
                preferred_element_type=jnp.float32,
            )
        ).reshape(slots, width)

    shared_mix = jax.nn.sigmoid(mix_pre)[:, None]
    sgate_pre = multiply_by_transpose(rows, s_gate)
    sup_pre = multiply_by_transpose(rows, s_up)
    act_wide = jax.nn.silu(sgate_pre) * sup_pre
    act_mixed = low(shared_mix * act_wide)
    expert_rows = take(rows)
    gate_pre = [multiply_by_transpose(expert_rows, w) for w in eg]
    up_pre = [multiply_by_transpose(expert_rows, w) for w in eu]
    expert_act = [low(jax.nn.silu(g) * u) for g, u in zip(gate_pre, up_pre)]
    expert_y = mul(expert_act[0], ed[0]) + mul(expert_act[1], ed[1])
    ffn_part = low(
        mul(
            jnp.concatenate([act_mixed, pick_back], axis=1),
            jnp.concatenate([s_down, low(slot_gate * expert_y)]),
        )
    )
    ffn_part, cot_rows = lax.optimization_barrier((ffn_part, cot_rows))
    ffn_out = lax.psum_scatter(ffn_part, FSDP, scatter_dimension=0, tiled=True)

    cot_slots = take(cot_rows)
    pulls = [multiply_by_transpose(cot_slots, w) for w in ed]
    gate_sum = sum(jnp.sum(full(a) * p, axis=-1) for a, p in zip(expert_act, pulls))
    gate_sum = gate_sum.reshape(units, capacity)
    gate_sum = jnp.sum(jnp.where(pick, gate_sum[:, :, None], 0.0), axis=1)
    pulls = [slot_gate * p for p in pulls]
    grad_eg = [low(p * u * silu_slope(g)) for p, u, g in zip(pulls, up_pre, gate_pre)]
    grad_eu = [low(p * jax.nn.silu(g)) for p, g in zip(pulls, gate_pre)]
    act_gated = [low(slot_gate * full(a)) for a in expert_act]
    swapped = (
        low(crossing_token_rows(act_gated[1], cot_slots)),
        low(crossing_token_rows(grad_eg[1], expert_rows)),
        low(crossing_token_rows(grad_eu[1], expert_rows)),
    )
    cot_rows, swapped = lax.optimization_barrier((cot_rows, swapped))
    ed_low, egw_low, euw_low = swapped
    ed_back = swap(ed_low)
    pull = multiply_by_transpose(cot_rows, s_down)
    mix_sum = jnp.sum(act_wide * pull, axis=-1)
    pull = shared_mix * pull
    grad_sgate = low(pull * sup_pre * silu_slope(sgate_pre))
    grad_sup = low(pull * jax.nn.silu(sgate_pre))
    rowin = sum(mul(g, w) for g, w in zip(grad_eg + grad_eu, eg + eu))
    rows_part = low(
        mul(
            jnp.concatenate([grad_sgate, grad_sup, pick_back], axis=1),
            jnp.concatenate([s_gate, s_up, low(rowin)]),
        )
    )
    grad_shared = jnp.stack(
        [
            crossing_token_rows(grad_sgate, rows),
            crossing_token_rows(grad_sup, rows),
            crossing_token_rows(act_mixed, cot_rows),
        ]
    )
    shared_mine = grad_shared[:, :hidden]
    shared_low = low(grad_shared[:, hidden : 2 * hidden])
    rows_part, ed_back, ffn_out = lax.optimization_barrier((rows_part, ed_back, ffn_out))
    scalars = jnp.stack([mix_sum.reshape(units, length), gate_sum], axis=1)
    lanes = -(-length // 128) * 128
    scalars = jnp.pad(scalars, ((0, 0), (0, 6), (0, lanes - length)))
    back, scalars, shared_back = scatter_rows(
        rows_part.reshape(units, length, width), 3, (scalars,), (False,), shared_low
    )
    shared_sum = low(shared_mine + full(shared_back))
    shared_sum = shared_sum.reshape(3 * hidden, units, part * 2).transpose(1, 0, 2)

    grad_out = full(cotangent)
    own_small = multiply_by_transpose(normed_f, small_w)
    own_mix = jax.nn.sigmoid(own_small[:, units])
    own_hit = jnp.any(routes[:, :, None] == unit_ids[None, None, :], axis=1)
    own_gates = jax.nn.softmax(jnp.where(own_hit, own_small[:, :units], -1e30), axis=-1)
    own_gates = jnp.where(own_hit, own_gates, 0.0)
    mix_total = jnp.sum(scalars[:, 0, :length], axis=0)
    grad_mix = low(own_mix * (1.0 - own_mix) * mix_total)
    grad_gate = scalars[:, 1, :length].T
    grad_logits = low(
        own_gates * (grad_gate - jnp.sum(own_gates * grad_gate, axis=-1, keepdims=True))
    )
    grad_small = jnp.concatenate([grad_logits, grad_mix[:, None]], axis=1)
    grad_small_w = crossing_token_rows(grad_small, normed_f)
    grad_norm_f = back + mul(grad_small, small_w)
    grad_from_f, grad_gain_f = norm_back(grad_norm_f, unit_f, inverse_f, gain_f)
    grad_mid = grad_out + grad_from_f

    output = low(middle + full(ffn_out))
    grad_attn, egw_back = gather_rows(low(grad_mid), units, 4, egw_low)
    grad_attn, shared_sum, euw_low = lax.optimization_barrier((grad_attn, shared_sum, euw_low))
    euw_back = swap(euw_low)
    shared_sum = spread(shared_sum)
    grad_attn = grad_attn.reshape(plane, width)
    grad_wo = crossing_token_rows(mixed, grad_attn)
    blocks = low(grad_wo).reshape(2, part, width)
    wo_pieces = (
        lax.ppermute(jnp.where(own_half, blocks[0], blocks[1]), (EXPERT, FSDP), from_unit_a),
        lax.ppermute(jnp.where(own_half, blocks[1], blocks[0]), (EXPERT, FSDP), from_unit_b),
    )
    grad_mixed = low(multiply_by_transpose(grad_attn, w_o)).reshape(units, length, head_size)
    grad_probs = jnp.einsum(
        "btd,bsd->bts", grad_mixed, values_all, preferred_element_type=jnp.float32
    )
    row_inner = jnp.sum(attn_probs * grad_probs, axis=-1, keepdims=True)
    grad_scores = low(attn_probs * (grad_probs - row_inner))
    grad_q = (
        jnp.einsum("bts,bsd->btd", grad_scores, keys_rot, preferred_element_type=jnp.float32)
        * score_scale
    )
    grad_k = (
        jnp.einsum("bts,btd->bsd", grad_scores, queries, preferred_element_type=jnp.float32)
        * score_scale
    )
    grad_v = jnp.einsum(
        "bts,btd->bsd", probs_low, grad_mixed, preferred_element_type=jnp.float32
    )
    grad_pre = jnp.concatenate(
        [
            low(unrotate(grad_q, cos_table, sine_table)),
            low(unrotate(grad_k, cos_table, sine_table)),
            low(grad_v),
        ],
        axis=-1,
    ).reshape(plane, 3 * head_size)
    grad_qkv = crossing_token_rows(normed_a, grad_pre)
    grad_gain_a = jnp.sum(grad_qkv * full(w_qkv), axis=1) / gain_a
    grad_bias = jnp.sum(full(grad_pre), axis=0).reshape(3, head_size // part, part)
    norm_part = low(multiply_by_transpose(grad_pre, w_qkv)).reshape(units, length, width)

    grad_qkv = grad_qkv.reshape(2, units * part, 3 * head_size)
    qkv_mine = jnp.where(own_half, grad_qkv[0], grad_qkv[1])
    qkv_back = swap(low(jnp.where(own_half, grad_qkv[1], grad_qkv[0])))
    qkv_sum = low(qkv_mine + full(qkv_back)).reshape(units, part, 3 * head_size)
    norm_part, shared_sum, qkv_sum = lax.optimization_barrier(
        (norm_part, shared_sum, qkv_sum)
    )
    bias_rows = jnp.where(here[None, :, None, None], grad_bias[:, None], 0.0)
    bias_rows = bias_rows.reshape(3, 2 * units, part)
    tiny = jnp.concatenate([grad_small_w, grad_gain_a[None], grad_gain_f[None]])
    tiny = jnp.concatenate([tiny.reshape(units + 3, 2 * units, part), bias_rows])
    tiny_rows = tiny.shape[0]
    tiny_high = lax.reduce_precision(tiny, 8, 7)
    tiny = low(jnp.stack([tiny_high, tiny - tiny_high])).transpose(2, 0, 1, 3)
    tiny = tiny.reshape(2 * units, -1)
    tiny_count = tiny.shape[1]
    lines = -(-tiny_count // 4096) * 16
    tiny = jnp.pad(tiny, ((0, 0), (0, lines * 256 - tiny_count)))
    grad_norm_a, tiny, qkv_sum = scatter_rows(
        norm_part, 5, (tiny.reshape(2 * units, lines, 256), qkv_sum), (True, False)
    )
    tiny = full(tiny.reshape(2 * units, -1)[:, :tiny_count])
    tiny = jnp.sum(tiny.reshape(4 * units, tiny_rows, part), axis=0)
    grad_norm_a, act_gated, grad_eu, euw_back, wo_pieces = lax.optimization_barrier(
        (grad_norm_a, act_gated, grad_eu, euw_back, wo_pieces)
    )

    inverse_a, unit_a = rms_parts(full(states))
    grad_from_a, _ = norm_back(grad_norm_a, unit_a, inverse_a, gain_a)
    grad_states = grad_mid + grad_from_a

    grad_qkv = full(qkv_sum).reshape(units, part, 3, head_size).transpose(2, 1, 0, 3)
    grad_qkv = grad_qkv.reshape(3, part, width)

    grad_wo_own = full(wo_pieces[0]) + full(wo_pieces[1])

    grad_egw = crossing_token_rows(grad_eg[0], expert_rows) + full(egw_back)
    grad_euw = crossing_token_rows(grad_eu[0], expert_rows) + full(euw_back)
    grad_ed = crossing_token_rows(act_gated[0], cot_slots) + full(ed_back)

    grad_sg, grad_su, grad_sd = (
        shared_sum[:, i * hidden : (i + 1) * hidden].reshape(units * hidden, part * 2)
        for i in range(3)
    )
    same = jnp.eye(part * 2, dtype=jnp.bfloat16)

    return (
        output,
        grad_states,
        grad_qkv[0],
        grad_qkv[1],
        grad_qkv[2],
        grad_wo_own,
        tiny[units + 3],
        tiny[units + 4],
        tiny[units + 5],
        tiny[units + 1],
        tiny[units + 2],
        tiny[:units].T,
        multiply_by_transpose(same, grad_sg),
        multiply_by_transpose(same, grad_su),
        full(grad_sd),
        tiny[units],
        grad_egw.T[None],
        grad_euw.T[None],
        grad_ed[None],
    )


def solution(mesh):
    placed = (
        P((EXPERT, FSDP), None),
        P((EXPERT, FSDP), None),
        P((EXPERT, FSDP), None),
        P((EXPERT, FSDP), None),
        P((EXPERT, FSDP), None),
        P((EXPERT, FSDP)),
        P((EXPERT, FSDP)),
        P((EXPERT, FSDP)),
        P((EXPERT, FSDP)),
        P((EXPERT, FSDP)),
        P((EXPERT, FSDP), None),
        P(FSDP, EXPERT),
        P(FSDP, EXPERT),
        P(EXPERT, FSDP),
        P((EXPERT, FSDP)),
        P(FSDP, None, EXPERT),
        P(FSDP, None, EXPERT),
        P(FSDP, EXPERT, None),
        P((EXPERT, FSDP), None),
        P((EXPERT, FSDP)),
        P((EXPERT, FSDP), None),
    )
    fits = mesh.shape[FSDP] == H == 16 and mesh.shape[EXPERT] == 2
    return jax.shard_map(
        plane_shards if fits else shards,
        mesh=mesh,
        in_specs=placed,
        out_specs=(
            P((EXPERT, FSDP), None),
            P((EXPERT, FSDP), None),
            P((EXPERT, FSDP), None),
            P((EXPERT, FSDP), None),
            P((EXPERT, FSDP), None),
            P((EXPERT, FSDP), None),
            P((EXPERT, FSDP)),
            P((EXPERT, FSDP)),
            P((EXPERT, FSDP)),
            P((EXPERT, FSDP)),
            P((EXPERT, FSDP)),
            P((EXPERT, FSDP), None),
            P(FSDP, EXPERT),
            P(FSDP, EXPERT),
            P(EXPERT, FSDP),
            P((EXPERT, FSDP)),
            P(FSDP, None, EXPERT),
            P(FSDP, None, EXPERT),
            P(FSDP, EXPERT, None),
        ),
        check_vma=False,
    )
```
